128 devices in a mesh: dp: 16 (over z, y), cent: 8 (over x, core).
Axes of the slice: x: 4, y: 4, z: 4, core: 2. Of those that a mesh axis runs over, the one named last changes fastest.
Arguments:
- clip_data: bfloat16 [16384, 4, 16, 192], P(('dp', 'cent')), may hold values from -6 to 6
- frame_counts: int32 [128, 128], P(('dp', 'cent')), may hold values from 1 to 4, 320 in all within a row
- send_list: int32 [128, 128], P(('dp', 'cent')), may hold values from 0 to 127, each once within a row
- cluster_ids: int32 [128, 128], P(('dp', 'cent')), may hold values from 0 to 43813, as said below
- expand_weight: bfloat16 [2, 192, 432], replicated, may hold values from -0.4375 to 0.4375
- depth_kernel: bfloat16 [2, 27, 432], replicated, may hold values from -1.25 to 1.25
- reduce_weight: bfloat16 [2, 432, 192], replicated, may hold values from -0.3125 to 0.3125
- head_weight: bfloat16 [192, 1024], replicated, may hold values from -0.4375 to 0.4375
- centroids: bfloat16 [50000, 1024], P('cent'), may hold values from -6 to 6
Outputs:
- embeddings: bfloat16 [16384, 1024], P(('dp', 'cent'))
- nearest: float32 [16384], P(('dp', 'cent'))
- own_sim: float32 [16384], P(('dp', 'cent'))
- peer_sim: float32 [16384], P(('dp', 'cent'))
The draws below stay inside these ranges and needn't reach their ends.
Inputs may be any that keep to these rules, and one draw needn't show every extreme that they name: `cluster_ids`: cluster id q is owned by the device with dp index (q % 6250) % 16 and cent index q // 6250. The clips of one device name at most 4 clusters of one owner, and in every draw one owner gets exactly 4 from every device. Only ids with q % 6250 < 64 occur.
All inputs are finite; a program needn't handle non-finite values.
Results may differ from the reference program's by a relative error of at most 0.014.
Values may be sent and summed in bfloat16 or wider, within the bound.
No kernel may reach another device: no remote copies, remote signals or barrier semaphores. Data moves between devices by JAX's collectives and lax.ppermute only.
A program may use at most 128 MiB of HBM per device.

```python
import math
import jax
import jax.numpy as jnp
import numpy as np
from jax import lax

C = 192
E = 432
D = 1024
K = 50000
LAYERS = 2
FR = 4
SIDE = 4
CL = 128
OWNERS = 128
CLIPS = 16384
KP = 6250
DP_SHARDS = 16
CAP = 4
GROUPS = 4
N_DP = 16
N_CENT = 8


def draw_cluster_ids(key, part):
    busiest = jax.random.randint(jax.random.fold_in(key, 1), (), 0, OWNERS)
    cent_count = K // KP

    def one_device(device):
        device_key = jax.random.fold_in(key, device + 100)
        tokens = jax.random.permutation(jax.random.fold_in(device_key, 2), CAP * (OWNERS - 1))
        ranked = tokens[:CL - CAP] // CAP
        others = (ranked + (ranked >= busiest).astype(jnp.int32)).astype(jnp.int32)
        listed = jnp.concatenate([jnp.full((CAP,), busiest, jnp.int32), others])
        shuffled_order = jax.random.permutation(jax.random.fold_in(device_key, 3), CL)
        targets = listed[shuffled_order]
        groups = jax.random.randint(jax.random.fold_in(device_key, 4), (CL,), 0, GROUPS)
        dp_part = targets // cent_count
        cent_part = targets % cent_count
        return (cent_part * KP + groups * DP_SHARDS + dp_part).astype(jnp.int32)
    return jax.vmap(one_device)(jnp.arange(OWNERS, dtype=jnp.int32))


def block_levels(own_key, extent, pieces, least, top_value):
    gain = 1.0
    for axis_at, shards_of in pieces:
        heights = jax.random.uniform(jax.random.fold_in(jax.random.fold_in(own_key, 6), axis_at), (shards_of,), jnp.float32, least / len(pieces), top_value / len(pieces))
        gain = gain * jnp.repeat(jnp.exp(heights), extent[axis_at] // shards_of).reshape((-1,) + (1,) * (len(extent) - 1 - axis_at))
    return gain


def split_up(count, total, limit, skew):
    loads = [(1 << 20) // math.isqrt(grade ** skew) + 1 for grade in range(2, count + 1)]
    surplus, counts = total - limit - (count - 1), [1] * (count - 1)
    while surplus > 0:
        movable = [i for i in range(count - 1) if counts[i] < limit]
        mass, left = sum([loads[i] for i in movable]), surplus
        for i in movable:
            extra = min(limit - counts[i], max(1, left * loads[i] // mass), surplus)
            counts[i] = counts[i] + extra
            surplus = surplus - extra
    return np.array([limit] + counts)


def ragged_sizes(key, number_of, total, limit, slope):
    if number_of == 2:
        one = jax.random.randint(key, (), max(1, total - limit), min(limit, total - 1) + 1)
        return jnp.stack([one, total - one])
    lengths = jnp.asarray(split_up(number_of, total, limit, slope), jnp.int32)
    twos = (number_of - 1) // 2
    source_of, receiver = lengths[1:1 + 2 * twos:2], lengths[2:2 + 2 * twos:2]
    room = jnp.minimum(source_of - 1, limit - receiver)
    moved = jax.random.randint(jax.random.fold_in(key, 1), (twos,), 0, 1 << 20) % (room + 1)
    lengths = lengths.at[1:1 + 2 * twos:2].set(source_of - moved).at[2:2 + 2 * twos:2].set(receiver + moved)
    return lengths[jax.random.permutation(jax.random.fold_in(key, 2), number_of)]


def centred(key, dims, deviation, bound, pieces=(), held_as=jnp.bfloat16):
    values = deviation * jax.random.normal(key, dims, jnp.float32)
    if pieces:
        values = values * block_levels(key, dims, pieces, -0.22, 0.18)
    return jnp.clip(values, -bound, bound).astype(held_as)


def setup_inputs(seed: int = 0) -> dict:
    splits = jax.random.split(jax.random.key(seed), 10)
    return {
        "clip_data": centred(splits[0], (CLIPS, FR, SIDE * SIDE, C), 1.0, 6.0, ((0, 128),)),
        "frame_counts": jax.vmap(lambda own: ragged_sizes(own, CL, CL * FR * 5 // 8, FR, 2))(jax.random.split(splits[1], OWNERS)).reshape((OWNERS, CL)).astype(jnp.int32),
        "send_list": jax.vmap(lambda own: jax.random.permutation(own, CL))(jax.random.split(splits[2], OWNERS)).reshape((OWNERS, CL)).astype(jnp.int32),
        "cluster_ids": draw_cluster_ids(jax.random.fold_in(splits[9], 71), 0),
        "expand_weight": centred(splits[4], (LAYERS, C, E), C ** -0.5, 0.4375),
        "depth_kernel": centred(splits[5], (LAYERS, 27, E), 27 ** -0.5, 1.25),
        "reduce_weight": centred(splits[6], (LAYERS, E, C), E ** -0.5, 0.3125),
        "head_weight": centred(splits[7], (C, D), C ** -0.5, 0.4375),
        "centroids": centred(splits[8], (K, D), 1.0, 6.0, ((0, 8),)),
    }


def depthwise(hidden, kernel):
    frame_count = hidden.shape[1]
    padded = jnp.pad(hidden, ((0, 0), (1, 1), (1, 1), (1, 1), (0, 0)))
    accumulated = jnp.zeros_like(hidden)
    for shift_t in range(3):
        for shift_y in range(3):
            for shift_x in range(3):
                accumulated = accumulated + kernel[9 * shift_t + 3 * shift_y + shift_x] * padded[:, shift_t:shift_t + frame_count, shift_y:shift_y + SIDE, shift_x:shift_x + SIDE, :]
    return accumulated

def embed_clips(clip_block, length_values, expand_weight, depth_kernel, reduce_weight, head_weight):
    clip_count, frame_count, positions, channels = clip_block.shape
    frame_mask = (jnp.arange(frame_count, dtype=jnp.float32)[None, :] < length_values[:, None]).astype(jnp.float32)
    mask_four = frame_mask[:, :, None, None]
    features = clip_block * mask_four.astype(jnp.bfloat16)
    for layer_index in range(expand_weight.shape[0]):
        hidden = jax.nn.relu(jnp.dot(features.reshape(-1, channels), expand_weight[layer_index], preferred_element_type=jnp.float32))
        expanded = hidden.shape[-1]
        hidden = hidden.reshape(clip_count, frame_count, SIDE, SIDE, expanded) * frame_mask[:, :, None, None, None]
        mixed = depthwise(hidden, depth_kernel[layer_index].astype(jnp.float32))
        activated = (mixed * jax.nn.sigmoid(mixed)).astype(jnp.bfloat16)
        branch = jnp.dot(activated.reshape(-1, expanded), reduce_weight[layer_index], preferred_element_type=jnp.float32)
        branch = branch.reshape(clip_count, frame_count, positions, channels)
        features = (features.astype(jnp.float32) + branch * mask_four).astype(jnp.bfloat16)
    pooled = (lax.optimization_barrier(jnp.sum(features.astype(jnp.float32), axis=(1, 2))) / (length_values * positions)[:, None]).astype(jnp.bfloat16)
    projected = jnp.dot(pooled, head_weight, preferred_element_type=jnp.float32)
    return (projected * lax.rsqrt(lax.optimization_barrier(jnp.sum(projected * projected, axis=1, keepdims=True)) + 1e-06)).astype(jnp.bfloat16)

def reference(clip_data, frame_counts, send_list, cluster_ids, expand_weight, depth_kernel, reduce_weight, head_weight, centroids):
    owner_total = N_DP * N_CENT
    total_rows = owner_total * CL
    source = jnp.arange(total_rows, dtype=jnp.int32)
    device = source // CL
    dp_index = device // N_CENT
    cent_index = device % N_CENT
    destination = send_list.reshape(-1).astype(jnp.int32)
    peer_index = destination % N_DP
    target_row = (peer_index * N_CENT + cent_index) * CL + destination - peer_index + dp_index
    shuffled = jnp.zeros_like(clip_data).at[target_row].set(clip_data)
    shuffled_counts = jnp.zeros((total_rows,), jnp.int32).at[target_row].set(frame_counts.reshape(-1).astype(jnp.int32))
    blocks = total_rows // 64

    def embed_block(pair):
        return embed_clips(pair[0], pair[1].astype(jnp.float32), expand_weight, depth_kernel, reduce_weight, head_weight)
    embeddings = lax.map(embed_block, (shuffled.reshape((blocks, 64) + clip_data.shape[1:]), shuffled_counts.reshape(blocks, 64)))
    embeddings = embeddings.reshape(total_rows, -1)

    def block_nearest(block_rows):
        scores = lax.dot_general(block_rows, centroids, (((1,), (1,)), ((), ())), preferred_element_type=jnp.float32)
        return lax.optimization_barrier(jnp.max(scores, axis=1))
    nearest = lax.map(block_nearest, embeddings.reshape(total_rows // 512, 512, -1)).reshape(-1)
    flat_ids = cluster_ids.reshape(-1).astype(jnp.int32)
    own_sim = lax.optimization_barrier(jnp.sum(embeddings.astype(jnp.float32) * centroids[flat_ids].astype(jnp.float32), axis=1))
    panel_index = flat_ids % KP
    target = panel_index % N_DP * N_CENT + flat_ids // KP
    capacity_all = owner_total * CAP

    def owner_peers(owner_id):
        ranking = jnp.where(target == owner_id, total_rows - source, 0)
        top_values, members = lax.top_k(ranking, capacity_all)
        filled = top_values > 0
        member_vectors = embeddings[members]
        member_ids = flat_ids[members]
        similarity = lax.dot_general(member_vectors, member_vectors, (((1,), (1,)), ((), ())), preferred_element_type=jnp.float32)
        slots = jnp.arange(capacity_all, dtype=jnp.int32)
        same_cluster = (member_ids[:, None] == member_ids[None, :]) & filled[:, None] & filled[None, :] & (slots[:, None] != slots[None, :])
        best_peer = lax.optimization_barrier(jnp.max(jnp.where(same_cluster, similarity, -1.0), axis=1))
        return (best_peer, jnp.where(filled, members, total_rows))
    peer_values, places = lax.map(owner_peers, jnp.arange(owner_total, dtype=jnp.int32))
    peer_sim = jnp.zeros((total_rows,), jnp.float32).at[places.reshape(-1)].set(peer_values.reshape(-1), mode='drop')
    return (embeddings, nearest, own_sim, peer_sim)
```

```python
import functools

import jax
import jax.numpy as jnp
from jax import lax
from jax.experimental import pallas as pl
from jax.experimental.pallas import tpu as pltpu
from jax.sharding import PartitionSpec as P

SIDE = 4
FRAMES = 4
SPOTS = SIDE * SIDE
BF = jnp.bfloat16
F32 = jnp.float32


def neighbours(at, extent):
    return [(at + shift - 1, shift) for shift in range(3) if 0 <= at + shift - 1 < extent]


def embed_kernel(
    clip_ref, count_ref, send_ref, expand_ref, depth_ref, reduce_ref, out_ref, x_ref, hidden_ref, act_ref, pool_ref
):
    channels, clips = clip_ref.shape[2], clip_ref.shape[3]
    expanded = expand_ref.shape[1]
    counts = count_ref[...]
    zero = jnp.zeros((channels, clips), BF)

    @pl.loop(0, FRAMES)
    def _(frame):
        kept = jnp.broadcast_to((counts > frame).astype(F32), (channels, clips)) > 0.5

        @pl.loop(0, SPOTS)
        def _(spot):
            x_ref[frame * SPOTS + spot] = jnp.where(
                kept, clip_ref[frame, spot].astype(F32), 0.0
            ).astype(BF)

    pool_ref[...] = jnp.zeros_like(pool_ref)
    for layer in range(2):

        @pl.loop(0, FRAMES * SPOTS // 2)
        def _(pair):
            both = jnp.concatenate([x_ref[2 * pair], x_ref[2 * pair + 1]], axis=1)
            hidden = jnp.dot(expand_ref[layer], both, preferred_element_type=F32)
            hidden = jnp.maximum(hidden, 0.0).astype(BF)
            hidden_ref[2 * pair] = hidden[:, :clips]
            hidden_ref[2 * pair + 1] = hidden[:, clips:]

        @pl.loop(0, expanded // 16)
        def _(tile):
            rows = pl.ds(pl.multiple_of(tile * 16, 16), 16)
            taps = depth_ref[layer, rows, :]
            weight = [
                jnp.broadcast_to(taps[:, tap : tap + 1], (16, clips)).astype(BF) for tap in range(27)
            ]
            for frame in range(FRAMES):
                for y in range(SIDE):
                    mixed = [None] * SIDE
                    for from_t, shift_t in neighbours(frame, FRAMES):
                        for from_y, shift_y in neighbours(y, SIDE):
                            base = from_t * SPOTS + from_y * SIDE
                            line = [hidden_ref[base + z, rows, :] for z in range(SIDE)]
                            for z in range(SIDE):
                                for from_z, shift_z in neighbours(z, SIDE):
                                    term = line[from_z] * weight[9 * shift_t + 3 * shift_y + shift_z]
                                    mixed[z] = term if mixed[z] is None else mixed[z] + term
                    for z in range(SIDE):
                        half = mixed[z] * BF(0.5)
                        act_ref[frame * SPOTS + y * SIDE + z, rows, :] = half + half * jnp.tanh(half)

        @pl.loop(0, FRAMES * SPOTS // 2)
        def _(pair):
            both = jnp.concatenate([act_ref[2 * pair], act_ref[2 * pair + 1]], axis=1)
            branch = jnp.dot(reduce_ref[layer], both, preferred_element_type=F32)
            kept = jnp.broadcast_to((counts > pair // (SPOTS // 2)).astype(F32), (channels, clips))
            for side in range(2):
                spot = 2 * pair + side
                x = x_ref[spot].astype(F32) + branch[:, side * clips : (side + 1) * clips] * kept
                x = x.astype(BF)
                if layer == 0:
                    x_ref[spot] = x
                else:
                    pool_ref[...] += x.astype(F32)

    pooled = (pool_ref[...] / (counts * SPOTS).astype(F32)).astype(BF)
    per_peer = out_ref.shape[1]
    n_dp = out_ref.shape[0]
    row = lax.broadcasted_iota(jnp.int32, (clips, clips), 0)
    slot = (row % per_peer) * n_dp + row // per_peer
    pick = (jnp.broadcast_to(send_ref[...], (clips, clips)) == slot).astype(F32).astype(BF)
    rows = lax.dot_general(pick, pooled, (((1,), (1,)), ((), ())), preferred_element_type=F32)
    rows = rows.astype(BF).reshape(n_dp, per_peer, channels)
    out_ref[:, :, :channels] = rows
    out_ref[:, :, channels:] = jnp.zeros((n_dp, per_peer, out_ref.shape[2] - channels), BF)


def embed(clip_data, frame_counts, send_list, expand_weight, depth_kernel, reduce_weight, n_dp):
    clips, frames, spots, channels = clip_data.shape
    expanded = expand_weight.shape[2]
    return pl.pallas_call(
        embed_kernel,
        out_shape=jax.ShapeDtypeStruct((n_dp, clips // n_dp, 256), BF),
        in_specs=[pl.BlockSpec(memory_space=pltpu.VMEM)] * 6,
        out_specs=pl.BlockSpec(memory_space=pltpu.VMEM),
        scratch_shapes=[
            pltpu.VMEM((frames * spots, channels, clips), BF),
            pltpu.VMEM((frames * spots, expanded, clips), BF),
            pltpu.VMEM((frames * spots, expanded, clips), BF),
            pltpu.VMEM((channels, clips), F32),
        ],
        compiler_params=pltpu.CompilerParams(vmem_limit_bytes=60 << 20),
        name="embed",
    )(
        jnp.transpose(clip_data, (1, 2, 3, 0)),
        frame_counts,
        send_list,
        jnp.swapaxes(expand_weight, 1, 2),
        jnp.swapaxes(depth_kernel, 1, 2).astype(F32),
        jnp.swapaxes(reduce_weight, 1, 2),
    )


def unit(projected, axis):
    square = jnp.sum(projected * projected, axis=axis, keepdims=True)
    return (projected * lax.rsqrt(square + 1e-06)).astype(BF)


LABEL_ROWS = 16


def own_kernel(arrived_ref, ids_ref, head_ref, payload_ref, vectors_ref):
    n_dp, per_peer, width = arrived_ref.shape
    clips = n_dp * per_peer
    channels = head_ref.shape[0]
    arrived = arrived_ref[...].reshape(clips, width)[:, :channels]
    row = lax.broadcasted_iota(jnp.int32, (clips, clips), 0)
    lane = lax.broadcasted_iota(jnp.int32, (clips, clips), 1)
    pick = (lane == (row % n_dp) * per_peer + row // n_dp).astype(F32).astype(BF)
    rows = jnp.dot(pick, arrived, preferred_element_type=F32).astype(BF)
    projected = jnp.dot(rows, head_ref[...], preferred_element_type=F32)
    vectors_ref[...] = unit(projected, 1)
    payload_ref[0:channels, :] = jnp.transpose(rows.astype(F32)).astype(BF)
    ids = ids_ref[...]
    which = lax.broadcasted_iota(jnp.int32, (LABEL_ROWS, clips), 0)
    high, low = ids // 256, ids % 256
    label = jnp.where(which == 0, high, jnp.where(which == 1, low, 0))
    payload_ref[channels:, :] = label.astype(F32).astype(BF)


def own(arrived, cluster_ids, head_weight):
    n_dp, per_peer, width = arrived.shape
    channels, dims = head_weight.shape
    clips = n_dp * per_peer
    return pl.pallas_call(
        own_kernel,
        out_shape=(
            jax.ShapeDtypeStruct((channels + LABEL_ROWS, clips), BF),
            jax.ShapeDtypeStruct((clips, dims), BF),
        ),
        in_specs=[pl.BlockSpec(memory_space=pltpu.VMEM)] * 3,
        out_specs=(pl.BlockSpec(memory_space=pltpu.VMEM),) * 2,
        name="own",
    )(arrived, cluster_ids, head_weight)


PANEL_ROWS = 784
OCCUR = 64


def nearest_kernel(panel_rows, base_ref, rows_ref, head_ref, panel_ref, turned_ref, near_ref, own_ref, best_ref):
    n_cent, height, clips = rows_ref.shape
    dims, channels = head_ref.shape
    total = n_cent * clips
    step = pl.program_id(0)
    last = pl.num_programs(0) - 1

    @pl.when(step == 0)
    def _():
        @pl.loop(0, n_cent // 2)
        def _(pair):
            both = jnp.concatenate([rows_ref[2 * pair], rows_ref[2 * pair + 1]], axis=1)
            projected = jnp.dot(head_ref[...], both[:channels], preferred_element_type=F32)
            cols = pl.ds(pl.multiple_of(pair * 2 * clips, 2 * clips), 2 * clips)
            turned_ref[:, cols] = unit(projected, 0)

        best_ref[...] = jnp.full_like(best_ref, -jnp.inf)

    def score(cols):
        return jnp.dot(panel_ref[...], turned_ref[:, cols], preferred_element_type=F32)

    def keep(scores, cols):
        rows = scores.shape[0]
        best_ref[:, cols] = jnp.maximum(
            best_ref[:, cols], jnp.max(scores.reshape(rows // 8, 8, scores.shape[1]), axis=0)
        )

    for block in range(total // 256):
        cols = pl.ds(block * 256, 256)

        @pl.when(step < last)
        def _():
            scores = score(cols)
            keep(scores, cols)

            @pl.when(step == 0)
            def _():
                label = jnp.concatenate(
                    [rows_ref[2 * block, channels:, :], rows_ref[2 * block + 1, channels:, :]], axis=1
                ).astype(F32)
                local_id = (label[0:1] * 256.0 + label[1:2]).astype(jnp.int32) - base_ref[0]
                index = lax.broadcasted_iota(jnp.int32, (OCCUR, 256), 0)
                own_ref[:, cols] = jnp.max(
                    jnp.where(index == local_id, scores[:OCCUR], -jnp.inf), axis=0, keepdims=True
                )

        @pl.when(step == last)
        def _():
            scores = score(cols)
            index = lax.broadcasted_iota(jnp.int32, scores.shape, 0) + last * panel_ref.shape[0]
            keep(jnp.where(index < panel_rows, scores, -jnp.inf), cols)
            near_ref[:, cols] = jnp.max(best_ref[:, cols], axis=0, keepdims=True)


def nearest_of(rows, head_turned, centroids, base):
    n_cent, height, clips = rows.shape
    dims, channels = head_turned.shape
    total = n_cent * clips
    panel_rows = centroids.shape[0]
    whole = lambda shape: pl.BlockSpec(shape, lambda step: (0,) * len(shape))
    return pl.pallas_call(
        functools.partial(nearest_kernel, panel_rows),
        grid=(pl.cdiv(panel_rows, PANEL_ROWS),),
        out_shape=(
            jax.ShapeDtypeStruct((dims, total), BF),
            jax.ShapeDtypeStruct((1, total), F32),
            jax.ShapeDtypeStruct((1, total), F32),
        ),
        in_specs=[
            pl.BlockSpec(memory_space=pltpu.SMEM),
            whole(rows.shape),
            whole(head_turned.shape),
            pl.BlockSpec((PANEL_ROWS, dims), lambda step: (step, 0)),
        ],
        out_specs=(whole((dims, total)), whole((1, total)), whole((1, total))),
        scratch_shapes=[pltpu.VMEM((8, total), F32)],
        compiler_params=pltpu.CompilerParams(vmem_limit_bytes=60 << 20),
        name="nearest",
    )(base, rows, head_turned, centroids)


GROUP = 4


def peer_kernel(place_ref, cols_ref, rows_ref, turned_ref, head_ref, near_ref, own_ref, out_ref, best_ref):
    n_dp, height, clips = cols_ref.shape
    n_cent = rows_ref.shape[0]
    channels = head_ref.shape[0]
    total = n_cent * clips
    eye = (
        lax.broadcasted_iota(jnp.int32, (clips, clips), 0)
        == lax.broadcasted_iota(jnp.int32, (clips, clips), 1)
    ).astype(F32).astype(BF)
    best_ref[...] = jnp.full_like(best_ref, -1.0)
    mine_dp, mine_cent = place_ref[0], place_ref[1]

    @pl.loop(0, n_dp // GROUP)
    def _(group):
        flipped = jnp.concatenate(
            [
                lax.dot_general(
                    eye, cols_ref[group * GROUP + at], (((1,), (1,)), ((), ())), preferred_element_type=F32
                )
                for at in range(GROUP)
            ],
            axis=0,
        )
        projected = jnp.dot(flipped[:, :channels].astype(BF), head_ref[...], preferred_element_type=F32)
        vectors = unit(projected, 1)
        ids = flipped[:, channels : channels + 1] * 256.0 + flipped[:, channels + 1 : channels + 2]
        wide = jnp.broadcast_to(ids, (GROUP * clips, 256))
        line = lax.broadcasted_iota(jnp.int32, (GROUP * clips, 256), 0)
        lane = lax.broadcasted_iota(jnp.int32, (GROUP * clips, 256), 1)
        for block in range(total // 256):
            cols = pl.ds(block * 256, 256)
            scores = jnp.dot(vectors, turned_ref[:, cols], preferred_element_type=F32)
            label = jnp.concatenate(
                [rows_ref[2 * block, channels:, :], rows_ref[2 * block + 1, channels:, :]], axis=1
            ).astype(F32)
            row_ids = label[0:1] * 256.0 + label[1:2]
            self_line = lane + (mine_dp - group * GROUP) * clips - (mine_cent - 2 * block) * clips
            inside = (lane // clips) == (mine_cent - 2 * block)
            same = (wide == row_ids) & jnp.logical_not(inside & (line == self_line))
            found = jnp.where(same, scores, -1.0)
            best_ref[:, cols] = jnp.maximum(
                best_ref[:, cols], jnp.max(found.reshape(GROUP * clips // 8, 8, 256), axis=0)
            )

    best = jnp.max(best_ref[...], axis=0, keepdims=True)
    for cent in range(n_cent):
        cols = slice(cent * clips, (cent + 1) * clips)
        out_ref[cent, 0:1, :] = near_ref[:, cols]
        out_ref[cent, 1:2, :] = own_ref[:, cols]
        out_ref[cent, 2:3, :] = best[:, cols]
        out_ref[cent, 3:4, :] = best[:, cols]


def peers_of(cols, rows, turned, head_weight, near, own_best, place):
    n_cent, height, clips = rows.shape
    total = n_cent * clips
    return pl.pallas_call(
        peer_kernel,
        out_shape=jax.ShapeDtypeStruct((n_cent, 4, clips), F32),
        in_specs=[pl.BlockSpec(memory_space=pltpu.SMEM)] + [pl.BlockSpec(memory_space=pltpu.VMEM)] * 6,
        out_specs=pl.BlockSpec(memory_space=pltpu.VMEM),
        scratch_shapes=[pltpu.VMEM((8, total), F32)],
        compiler_params=pltpu.CompilerParams(vmem_limit_bytes=60 << 20),
        name="peers",
    )(place, cols, rows, turned, head_weight, near, own_best)


def local(
    clip_data,
    frame_counts,
    send_list,
    cluster_ids,
    expand_weight,
    depth_kernel,
    reduce_weight,
    head_weight,
    centroids,
):
    n_dp = lax.axis_size("dp")
    n_cent = lax.axis_size("cent")
    panel_rows = centroids.shape[0]
    mine_dp, mine_cent = lax.axis_index("dp"), lax.axis_index("cent")
    base = (mine_cent * panel_rows).astype(jnp.int32)[None]
    place = jnp.stack([mine_dp, mine_cent]).astype(jnp.int32)
    pooled = embed(
        clip_data, frame_counts, send_list, expand_weight, depth_kernel, reduce_weight, n_dp
    )
    arrived = lax.all_to_all(pooled, "dp", split_axis=0, concat_axis=0, tiled=True)
    payload, vectors = own(arrived, cluster_ids, head_weight)
    rows = lax.all_gather(payload, "cent", axis=0)
    spread = jnp.broadcast_to(payload, (n_dp,) + payload.shape)
    cols = lax.all_to_all(spread, "dp", split_axis=0, concat_axis=0, tiled=True)
    turned, near, own_best = nearest_of(rows, jnp.swapaxes(head_weight, 0, 1), centroids, base)
    partial = peers_of(cols, rows, turned, head_weight, near, own_best, place)
    parts = lax.all_to_all(partial, "cent", split_axis=0, concat_axis=0, tiled=True)
    final = jnp.max(parts, axis=0)
    return (vectors, final[0], final[1], final[2])


def solution(mesh):
    placed = (
        P(("dp", "cent"), None, None, None),
        P(("dp", "cent"), None),
        P(("dp", "cent"), None),
        P(("dp", "cent"), None),
        P(),
        P(),
        P(),
        P(),
        P("cent", None),
    )
    return jax.shard_map(
        local,
        mesh=mesh,
        in_specs=placed,
        out_specs=(
            P(("dp", "cent"), None),
            P(("dp", "cent")),
            P(("dp", "cent")),
            P(("dp", "cent")),
        ),
        check_vma=False,
    )
```

```python
import functools

import jax
import jax.numpy as jnp
from jax import lax
from jax.experimental import pallas as pl
from jax.experimental.pallas import tpu as pltpu
from jax.sharding import PartitionSpec as P

SIDE = 4
FRAMES = 4
SPOTS = SIDE * SIDE
BF = jnp.bfloat16
F32 = jnp.float32


def neighbours(at, extent):
    return [(at + shift - 1, shift) for shift in range(3) if 0 <= at + shift - 1 < extent]


def embed_kernel(
    clip_ref, count_ref, send_ref, expand_ref, depth_ref, reduce_ref, out_ref, x_ref, hidden_ref, act_ref, pool_ref
):
    channels, clips = clip_ref.shape[2], clip_ref.shape[3]
    expanded = expand_ref.shape[1]
    counts = count_ref[...]
    zero = jnp.zeros((channels, clips), BF)

    @pl.loop(0, FRAMES)
    def _(frame):
        kept = jnp.broadcast_to((counts > frame).astype(F32), (channels, clips)) > 0.5

        @pl.loop(0, SPOTS)
        def _(spot):
            x_ref[frame * SPOTS + spot] = jnp.where(
                kept, clip_ref[frame, spot].astype(F32), 0.0
            ).astype(BF)

    pool_ref[...] = jnp.zeros_like(pool_ref)
    for layer in range(2):

        @pl.loop(0, FRAMES * SPOTS // 2)
        def _(pair):
            both = jnp.concatenate([x_ref[2 * pair], x_ref[2 * pair + 1]], axis=1)
            hidden = jnp.dot(expand_ref[layer], both, preferred_element_type=F32)
            hidden_ref[2 * pair] = hidden[:, :clips]
            hidden_ref[2 * pair + 1] = hidden[:, clips:]

        @pl.loop(0, expanded // 16)
        def _(tile):
            rows = pl.ds(pl.multiple_of(tile * 16, 16), 16)
            taps = depth_ref[layer, rows, :]
            weight = [
                jnp.broadcast_to(taps[:, tap : tap + 1], (16, clips)).astype(BF) for tap in range(27)
            ]
            hidden = [
                jnp.maximum(hidden_ref[spot, rows, :], 0.0).astype(BF) for spot in range(FRAMES * SPOTS)
            ]
            for frame in range(FRAMES):
                for y in range(SIDE):
                    mixed = [None] * SIDE
                    for from_t, shift_t in neighbours(frame, FRAMES):
                        for from_y, shift_y in neighbours(y, SIDE):
                            base = from_t * SPOTS + from_y * SIDE
                            line = hidden[base : base + SIDE]
                            for z in range(SIDE):
                                for from_z, shift_z in neighbours(z, SIDE):
                                    term = line[from_z] * weight[9 * shift_t + 3 * shift_y + shift_z]
                                    mixed[z] = term if mixed[z] is None else mixed[z] + term
                    for z in range(SIDE):
                        half = mixed[z] * BF(0.5)
                        act_ref[frame * SPOTS + y * SIDE + z, rows, :] = half + half * jnp.tanh(half)

        @pl.loop(0, FRAMES * SPOTS // 2)
        def _(pair):
            both = jnp.concatenate([act_ref[2 * pair], act_ref[2 * pair + 1]], axis=1)
            branch = jnp.dot(reduce_ref[layer], both, preferred_element_type=F32)
            kept = jnp.broadcast_to((counts > pair // (SPOTS // 2)).astype(F32), (channels, clips))
            for side in range(2):
                spot = 2 * pair + side
                x = x_ref[spot].astype(F32) + branch[:, side * clips : (side + 1) * clips] * kept
                x = x.astype(BF)
                if layer == 0:
                    x_ref[spot] = x
                else:
                    pool_ref[...] += x.astype(F32)

    pooled = (pool_ref[...] / (counts * SPOTS).astype(F32)).astype(BF)
    per_peer = out_ref.shape[1]
    n_dp = out_ref.shape[0]
    row = lax.broadcasted_iota(jnp.int32, (clips, clips), 0)
    slot = (row % per_peer) * n_dp + row // per_peer
    pick = (jnp.broadcast_to(send_ref[...], (clips, clips)) == slot).astype(F32).astype(BF)
    rows = lax.dot_general(pick, pooled, (((1,), (1,)), ((), ())), preferred_element_type=F32)
    rows = rows.astype(BF).reshape(n_dp, per_peer, channels)
    out_ref[:, :, :channels] = rows
    out_ref[:, :, channels:] = jnp.zeros((n_dp, per_peer, out_ref.shape[2] - channels), BF)


def embed(clip_data, frame_counts, send_list, expand_weight, depth_kernel, reduce_weight, n_dp):
    clips, frames, spots, channels = clip_data.shape
    expanded = expand_weight.shape[2]
    return pl.pallas_call(
        embed_kernel,
        out_shape=jax.ShapeDtypeStruct((n_dp, clips // n_dp, 256), BF),
        in_specs=[pl.BlockSpec(memory_space=pltpu.VMEM)] * 6,
        out_specs=pl.BlockSpec(memory_space=pltpu.VMEM),
        scratch_shapes=[
            pltpu.VMEM((frames * spots, channels, clips), BF),
            pltpu.VMEM((frames * spots, expanded, clips), F32),
            pltpu.VMEM((frames * spots, expanded, clips), BF),
            pltpu.VMEM((channels, clips), F32),
        ],
        compiler_params=pltpu.CompilerParams(vmem_limit_bytes=60 << 20),
        name="embed",
    )(
        jnp.transpose(clip_data, (1, 2, 3, 0)),
        frame_counts,
        send_list,
        jnp.swapaxes(expand_weight, 1, 2),
        jnp.swapaxes(depth_kernel, 1, 2).astype(F32),
        jnp.swapaxes(reduce_weight, 1, 2),
    )


def unit(projected, axis):
    square = jnp.sum(projected * projected, axis=axis, keepdims=True)
    return (projected * lax.rsqrt(square + 1e-06)).astype(BF)


LABEL_ROWS = 16


def own_kernel(arrived_ref, ids_ref, head_ref, payload_ref, vectors_ref):
    n_dp, per_peer, width = arrived_ref.shape
    clips = n_dp * per_peer
    channels = head_ref.shape[0]
    arrived = arrived_ref[...].reshape(clips, width)[:, :channels]
    row = lax.broadcasted_iota(jnp.int32, (clips, clips), 0)
    lane = lax.broadcasted_iota(jnp.int32, (clips, clips), 1)
    pick = (lane == (row % n_dp) * per_peer + row // n_dp).astype(F32).astype(BF)
    rows = jnp.dot(pick, arrived, preferred_element_type=F32).astype(BF)
    projected = jnp.dot(rows, head_ref[...], preferred_element_type=F32)
    vectors_ref[...] = unit(projected, 1)
    payload_ref[0:channels, :] = jnp.transpose(rows.astype(F32)).astype(BF)
    ids = ids_ref[...]
    which = lax.broadcasted_iota(jnp.int32, (LABEL_ROWS, clips), 0)
    high, low = ids // 256, ids % 256
    label = jnp.where(which == 0, high, jnp.where(which == 1, low, 0))
    payload_ref[channels:, :] = label.astype(F32).astype(BF)


def own(arrived, cluster_ids, head_weight):
    n_dp, per_peer, width = arrived.shape
    channels, dims = head_weight.shape
    clips = n_dp * per_peer
    return pl.pallas_call(
        own_kernel,
        out_shape=(
            jax.ShapeDtypeStruct((channels + LABEL_ROWS, clips), BF),
            jax.ShapeDtypeStruct((clips, dims), BF),
        ),
        in_specs=[pl.BlockSpec(memory_space=pltpu.VMEM)] * 3,
        out_specs=(pl.BlockSpec(memory_space=pltpu.VMEM),) * 2,
        name="own",
    )(arrived, cluster_ids, head_weight)


PANEL_ROWS = 784
OCCUR = 64


def nearest_kernel(panel_rows, base_ref, rows_ref, head_ref, panel_ref, turned_ref, near_ref, own_ref, best_ref):
    n_cent, height, clips = rows_ref.shape
    dims, channels = head_ref.shape
    total = n_cent * clips
    step = pl.program_id(0)
    last = pl.num_programs(0) - 1

    @pl.when(step == 0)
    def _():
        @pl.loop(0, n_cent // 2)
        def _(pair):
            both = jnp.concatenate([rows_ref[2 * pair], rows_ref[2 * pair + 1]], axis=1)
            projected = jnp.dot(head_ref[...], both[:channels], preferred_element_type=F32)
            cols = pl.ds(pl.multiple_of(pair * 2 * clips, 2 * clips), 2 * clips)
            turned_ref[:, cols] = unit(projected, 0)

        best_ref[...] = jnp.full_like(best_ref, -jnp.inf)

    def score(cols):
        return jnp.dot(panel_ref[...], turned_ref[:, cols], preferred_element_type=F32)

    def keep(scores, cols):
        rows = scores.shape[0]
        best_ref[:, cols] = jnp.maximum(
            best_ref[:, cols], jnp.max(scores.reshape(rows // 8, 8, scores.shape[1]), axis=0)
        )

    for block in range(total // 256):
        cols = pl.ds(block * 256, 256)

        @pl.when(step < last)
        def _():
            scores = score(cols)
            keep(scores, cols)

            @pl.when(step == 0)
            def _():
                label = jnp.concatenate(
                    [rows_ref[2 * block, channels:, :], rows_ref[2 * block + 1, channels:, :]], axis=1
                ).astype(F32)
                local_id = (label[0:1] * 256.0 + label[1:2]).astype(jnp.int32) - base_ref[0]
                index = lax.broadcasted_iota(jnp.int32, (OCCUR, 256), 0)
                own_ref[:, cols] = jnp.max(
                    jnp.where(index == local_id, scores[:OCCUR], -jnp.inf), axis=0, keepdims=True
                )

        @pl.when(step == last)
        def _():
            scores = score(cols)
            index = lax.broadcasted_iota(jnp.int32, scores.shape, 0) + last * panel_ref.shape[0]
            keep(jnp.where(index < panel_rows, scores, -jnp.inf), cols)
            near_ref[:, cols] = jnp.max(best_ref[:, cols], axis=0, keepdims=True)


def nearest_of(rows, head_turned, centroids, base):
    n_cent, height, clips = rows.shape
    dims, channels = head_turned.shape
    total = n_cent * clips
    panel_rows = centroids.shape[0]
    whole = lambda shape: pl.BlockSpec(shape, lambda step: (0,) * len(shape))
    return pl.pallas_call(
        functools.partial(nearest_kernel, panel_rows),
        grid=(pl.cdiv(panel_rows, PANEL_ROWS),),
        out_shape=(
            jax.ShapeDtypeStruct((dims, total), BF),
            jax.ShapeDtypeStruct((1, total), F32),
            jax.ShapeDtypeStruct((1, total), F32),
        ),
        in_specs=[
            pl.BlockSpec(memory_space=pltpu.SMEM),
            whole(rows.shape),
            whole(head_turned.shape),
            pl.BlockSpec((PANEL_ROWS, dims), lambda step: (step, 0)),
        ],
        out_specs=(whole((dims, total)), whole((1, total)), whole((1, total))),
        scratch_shapes=[pltpu.VMEM((8, total), F32)],
        compiler_params=pltpu.CompilerParams(vmem_limit_bytes=60 << 20),
        name="nearest",
    )(base, rows, head_turned, centroids)


GROUP = 4


def peer_kernel(place_ref, cols_ref, rows_ref, turned_ref, head_ref, near_ref, own_ref, out_ref, best_ref):
    n_dp, height, clips = cols_ref.shape
    n_cent = rows_ref.shape[0]
    channels = head_ref.shape[0]
    total = n_cent * clips
    eye = (
        lax.broadcasted_iota(jnp.int32, (clips, clips), 0)
        == lax.broadcasted_iota(jnp.int32, (clips, clips), 1)
    ).astype(F32).astype(BF)
    best_ref[...] = jnp.full_like(best_ref, -1.0)
    mine_dp, mine_cent = place_ref[0], place_ref[1]

    @pl.loop(0, n_dp // GROUP)
    def _(group):
        flipped = jnp.concatenate(
            [
                lax.dot_general(
                    eye, cols_ref[group * GROUP + at], (((1,), (1,)), ((), ())), preferred_element_type=F32
                )
                for at in range(GROUP)
            ],
            axis=0,
        )
        projected = jnp.dot(flipped[:, :channels].astype(BF), head_ref[...], preferred_element_type=F32)
        vectors = unit(projected, 1)
        ids = flipped[:, channels : channels + 1] * 256.0 + flipped[:, channels + 1 : channels + 2]
        wide = jnp.broadcast_to(ids, (GROUP * clips, 256))
        line = lax.broadcasted_iota(jnp.int32, (GROUP * clips, 256), 0)
        lane = lax.broadcasted_iota(jnp.int32, (GROUP * clips, 256), 1)
        for block in range(total // 256):
            cols = pl.ds(block * 256, 256)
            scores = jnp.dot(vectors, turned_ref[:, cols], preferred_element_type=F32)
            label = jnp.concatenate(
                [rows_ref[2 * block, channels:, :], rows_ref[2 * block + 1, channels:, :]], axis=1
            ).astype(F32)
            row_ids = label[0:1] * 256.0 + label[1:2]
            self_line = lane + (mine_dp - group * GROUP) * clips - (mine_cent - 2 * block) * clips
            inside = (lane // clips) == (mine_cent - 2 * block)
            same = (wide == row_ids) & jnp.logical_not(inside & (line == self_line))
            found = jnp.where(same, scores, -1.0)
            best_ref[:, cols] = jnp.maximum(
                best_ref[:, cols], jnp.max(found.reshape(GROUP * clips // 8, 8, 256), axis=0)
            )

    best = jnp.max(best_ref[...], axis=0, keepdims=True)
    for cent in range(n_cent):
        cols = slice(cent * clips, (cent + 1) * clips)
        out_ref[cent, 0:1, :] = near_ref[:, cols]
        out_ref[cent, 1:2, :] = own_ref[:, cols]
        out_ref[cent, 2:3, :] = best[:, cols]
        out_ref[cent, 3:4, :] = best[:, cols]


def peers_of(cols, rows, turned, head_weight, near, own_best, place):
    n_cent, height, clips = rows.shape
    total = n_cent * clips
    return pl.pallas_call(
        peer_kernel,
        out_shape=jax.ShapeDtypeStruct((n_cent, 4, clips), F32),
        in_specs=[pl.BlockSpec(memory_space=pltpu.SMEM)] + [pl.BlockSpec(memory_space=pltpu.VMEM)] * 6,
        out_specs=pl.BlockSpec(memory_space=pltpu.VMEM),
        scratch_shapes=[pltpu.VMEM((8, total), F32)],
        compiler_params=pltpu.CompilerParams(vmem_limit_bytes=60 << 20),
        name="peers",
    )(place, cols, rows, turned, head_weight, near, own_best)


def local(
    clip_data,
    frame_counts,
    send_list,
    cluster_ids,
    expand_weight,
    depth_kernel,
    reduce_weight,
    head_weight,
    centroids,
):
    n_dp = lax.axis_size("dp")
    n_cent = lax.axis_size("cent")
    panel_rows = centroids.shape[0]
    mine_dp, mine_cent = lax.axis_index("dp"), lax.axis_index("cent")
    base = (mine_cent * panel_rows).astype(jnp.int32)[None]
    place = jnp.stack([mine_dp, mine_cent]).astype(jnp.int32)
    pooled = embed(
        clip_data, frame_counts, send_list, expand_weight, depth_kernel, reduce_weight, n_dp
    )
    arrived = lax.all_to_all(pooled, "dp", split_axis=0, concat_axis=0, tiled=True)
    payload, vectors = own(arrived, cluster_ids, head_weight)
    rows = lax.all_gather(payload, "cent", axis=0)
    spread = jnp.broadcast_to(payload, (n_dp,) + payload.shape)
    cols = lax.all_to_all(spread, "dp", split_axis=0, concat_axis=0, tiled=True)
    turned, near, own_best = nearest_of(rows, jnp.swapaxes(head_weight, 0, 1), centroids, base)
    partial = peers_of(cols, rows, turned, head_weight, near, own_best, place)
    parts = lax.all_to_all(partial, "cent", split_axis=0, concat_axis=0, tiled=True)
    final = jnp.max(parts, axis=0)
    return (vectors, final[0], final[1], final[2])


def solution(mesh):
    placed = (
        P(("dp", "cent"), None, None, None),
        P(("dp", "cent"), None),
        P(("dp", "cent"), None),
        P(("dp", "cent"), None),
        P(),
        P(),
        P(),
        P(),
        P("cent", None),
    )
    return jax.shard_map(
        local,
        mesh=mesh,
        in_specs=placed,
        out_specs=(
            P(("dp", "cent"), None),
            P(("dp", "cent")),
            P(("dp", "cent")),
            P(("dp", "cent")),
        ),
        check_vma=False,
    )
```

```python
import functools

import jax
import jax.numpy as jnp
from jax import lax
from jax.experimental import pallas as pl
from jax.experimental.pallas import tpu as pltpu
from jax.sharding import PartitionSpec as P

SIDE = 4
SPOTS = SIDE * SIDE
BF = jnp.bfloat16
F32 = jnp.float32


def neighbours(at, extent):
    return [(at + shift - 1, shift) for shift in range(3) if 0 <= at + shift - 1 < extent]


TILES = 3
STEPS = 9


def embed_kernel(
    clip_ref, count_ref, send_ref, expand_ref, depth_ref, reduce_ref, out_ref, *scratch
):
    x_refs, hidden_refs, act_refs = scratch[0:6], scratch[6:12], scratch[12:15]
    pool_ref, packed_pool_ref = scratch[15:17]
    weight_refs = scratch[17:19]
    channels, clips = clip_ref.shape[2], clip_ref.shape[3]
    expanded = expand_ref.shape[1]

    counts = count_ref[...].astype(F32)
    line = lax.broadcasted_iota(jnp.int32, (clips, clips), 0)
    lane = lax.broadcasted_iota(jnp.int32, (clips, clips), 1)
    count_lane = jnp.broadcast_to(counts, (clips, clips))
    count_line = jnp.transpose(count_lane)
    ahead = (count_lane > count_line) | ((count_lane == count_line) & (lane < line))
    rank = jnp.dot(
        ahead.astype(F32).astype(BF), jnp.ones((clips, clips), BF), preferred_element_type=F32
    ).astype(jnp.int32)
    n1, n2, n3 = [jnp.sum((counts > frame).astype(jnp.int32)) for frame in (1, 2, 3)]
    blocks = expanded // 16 // STEPS
    one_hot = lambda mask: mask.astype(F32).astype(BF)
    order = one_hot(rank == lane)
    place = [
        order,
        one_hot((rank == lane) & (count_line > 1)),
        jnp.concatenate(
            [
                one_hot((rank == lane) & (count_line > 2)),
                one_hot((rank + n2 == lane) & (count_line > 3)),
            ],
            axis=0,
        ),
    ]
    row_lane = lax.broadcasted_iota(jnp.int32, (1, clips), 1)
    kept = [None, (row_lane < n1).astype(F32), (row_lane < n2 + n3).astype(F32)]
    tile_lane = lax.broadcasted_iota(jnp.int32, (16, clips), 1)
    in_second, in_third = tile_lane < n2, tile_lane < n3

    def expand(layer, tile, pair, both):
        hidden = jnp.maximum(jnp.dot(expand_ref[layer], both, preferred_element_type=F32), 0.0)
        hidden_refs[3 * layer + tile][2 * pair] = hidden[:, :clips]
        hidden_refs[3 * layer + tile][2 * pair + 1] = hidden[:, clips:]

    def gather(tile, pair):
        if tile < 2:
            spots = jnp.concatenate([clip_ref[tile, 2 * pair], clip_ref[tile, 2 * pair + 1]], axis=0)
        else:
            spots = jnp.concatenate(
                [
                    jnp.concatenate([clip_ref[2, 2 * pair + side], clip_ref[3, 2 * pair + side]], axis=1)
                    for side in range(2)
                ],
                axis=0,
            )
        x = jnp.dot(spots, place[tile], preferred_element_type=F32).astype(BF)
        x_refs[tile][2 * pair] = x[:channels]
        x_refs[tile][2 * pair + 1] = x[channels:]

    def expand_stored(layer, tile, pair):
        x_ref = x_refs[3 * layer + tile]
        expand(layer, tile, pair, jnp.concatenate([x_ref[2 * pair], x_ref[2 * pair + 1]], axis=1))

    def spread_taps(layer, step, first, last):
        rows = [pl.ds(pl.multiple_of((step * blocks + at) * 16, 16), 16) for at in range(blocks)]
        taps = [depth_ref[layer, row, :] for row in rows]
        for tap in range(first, last):
            for at in range(blocks):
                weight_refs[layer][step * blocks + at, tap] = jnp.broadcast_to(
                    taps[at][:, tap : tap + 1], (16, clips)
                )

    def reduce(layer, tile, pair):
        both = jnp.concatenate([act_refs[tile][2 * pair], act_refs[tile][2 * pair + 1]], axis=1)
        branch = jnp.dot(reduce_ref[layer], both, preferred_element_type=F32)
        result = []
        for side in range(2):
            part = branch[:, side * clips : (side + 1) * clips]
            if kept[tile] is not None:
                part = part * kept[tile]
            x = x_refs[3 * layer + tile][2 * pair + side].astype(F32) + part
            result.append(x.astype(BF))
        return result

    def reduce_store(tile, pair):
        x = reduce(0, tile, pair)
        x_refs[3 + tile][2 * pair] = x[0]
        x_refs[3 + tile][2 * pair + 1] = x[1]

    def reduce_pool(tile, pair, live):
        x = reduce(1, tile, pair)
        into = packed_pool_ref if tile == 2 else pool_ref
        into[...] += (x[0].astype(F32) + x[1].astype(F32)) * live

    def depthwise(layer, tile, block):
        rows = pl.ds(pl.multiple_of(block * 16, 16), 16)
        read = lambda source, spot: hidden_refs[3 * layer + source][spot, rows, :]
        if tile == 0:
            sources = [(1, lambda s: read(0, s)), (2, lambda s: read(1, s))]
        elif tile == 1:
            sources = [
                (0, lambda s: read(0, s)),
                (1, lambda s: read(1, s)),
                (2, lambda s: jnp.where(in_second, read(2, s), 0.0)),
            ]
        else:
            sources = [
                (0, lambda s: jnp.where(in_second, read(1, s), pltpu.roll(read(2, s), n2, 1))),
                (1, lambda s: read(2, s)),
                (2, lambda s: jnp.where(in_third, pltpu.roll(read(2, s), clips - n2, 1), 0.0)),
            ]
        mixed = [None] * SPOTS
        for shift_t, source in sources:
            weight = [weight_refs[layer][block, 9 * shift_t + tap].astype(BF) for tap in range(9)]
            hidden = [source(spot).astype(BF) for spot in range(SPOTS)]
            for y in range(SIDE):
                for from_y, shift_y in neighbours(y, SIDE):
                    for z in range(SIDE):
                        for from_z, shift_z in neighbours(z, SIDE):
                            term = hidden[from_y * SIDE + from_z] * weight[3 * shift_y + shift_z]
                            spot = y * SIDE + z
                            mixed[spot] = term if mixed[spot] is None else mixed[spot] + term
        for spot in range(SPOTS):
            half = mixed[spot] * BF(0.5)
            act_refs[tile][spot, rows, :] = half + half * jnp.tanh(half)

    def stage(layer, tile, other):
        @pl.loop(0, STEPS)
        def _(step):
            pair = jnp.minimum(step, SPOTS // 2 - 1)
            before = jnp.maximum(step - 1, 0)
            other(pair, before, (step < SPOTS // 2).astype(F32))
            if layer == 0:
                if tile == 0:
                    spread_taps(0, step, 0, 9)
                spread_taps(1, step, 9 * tile, 9 * tile + 9)
            for at in range(blocks):
                depthwise(layer, tile, step * blocks + at)

    def filler(first, second):
        def other(pair, before, live):
            second(before)
            first(pair)

        return other

    pool_ref[...] = jnp.zeros_like(pool_ref)
    packed_pool_ref[...] = jnp.zeros_like(packed_pool_ref)

    @pl.loop(0, STEPS)
    def _(step):
        pair = jnp.minimum(step, SPOTS // 2 - 1)
        before = jnp.maximum(step - 1, 0)
        for tile in range(2):
            expand_stored(0, tile, before)
            gather(tile, pair)
        spread_taps(0, step, 9, 27)

    stage(0, 0, filler(lambda pair: gather(2, pair), lambda pair: expand_stored(0, 2, pair)))
    stage(0, 1, filler(lambda pair: reduce_store(0, pair), lambda pair: expand_stored(1, 0, pair)))
    stage(0, 2, filler(lambda pair: reduce_store(1, pair), lambda pair: expand_stored(1, 1, pair)))
    stage(1, 0, filler(lambda pair: reduce_store(2, pair), lambda pair: expand_stored(1, 2, pair)))
    stage(1, 1, lambda pair, before, live: reduce_pool(0, pair, live))
    stage(1, 2, lambda pair, before, live: reduce_pool(1, pair, live))

    @pl.loop(0, SPOTS // 2)
    def _(pair):
        reduce_pool(2, pair, 1.0)

    packed = packed_pool_ref[...]
    total = (
        pool_ref[...]
        + jnp.where(row_lane < n2, packed, 0.0)
        + jnp.where(row_lane < n3, pltpu.roll(packed, clips - n2, 1), 0.0)
    )
    lengths = jnp.dot(
        jnp.broadcast_to(counts, (16, clips)).astype(BF), order, preferred_element_type=F32
    )[0:1]
    pooled = (total / (lengths * SPOTS)).astype(BF)
    n_dp, per_peer = out_ref.shape[0], out_ref.shape[1]
    slot = (line % per_peer) * n_dp + line // per_peer
    pick = one_hot(jnp.broadcast_to(send_ref[...], (clips, clips)) == slot)
    pick = lax.dot_general(pick, order, (((1,), (0,)), ((), ())), preferred_element_type=F32).astype(BF)
    rows = lax.dot_general(pick, pooled, (((1,), (1,)), ((), ())), preferred_element_type=F32)
    out_ref[:, :, :channels] = rows.astype(BF).reshape(n_dp, per_peer, channels)
    out_ref[:, :, channels:] = jnp.zeros((n_dp, per_peer, out_ref.shape[2] - channels), BF)


def embed(clip_data, frame_counts, send_list, expand_weight, depth_kernel, reduce_weight, n_dp):
    clips, frames, spots, channels = clip_data.shape
    expanded = expand_weight.shape[2]
    return pl.pallas_call(
        embed_kernel,
        out_shape=jax.ShapeDtypeStruct((n_dp, clips // n_dp, 256), BF),
        in_specs=[pl.BlockSpec(memory_space=pltpu.VMEM)] * 6,
        out_specs=pl.BlockSpec(memory_space=pltpu.VMEM),
        scratch_shapes=[pltpu.VMEM((spots, channels, clips), BF)] * 6
        + [pltpu.VMEM((spots, expanded, clips), F32)] * 6
        + [pltpu.VMEM((spots, expanded, clips), BF)] * 3
        + [pltpu.VMEM((channels, clips), F32)] * 2
        + [pltpu.VMEM((expanded // 16, 27, 16, clips), F32)] * 2,
        compiler_params=pltpu.CompilerParams(vmem_limit_bytes=60 << 20),
        name="embed",
    )(
        jnp.transpose(clip_data, (1, 2, 3, 0)),
        frame_counts,
        send_list,
        jnp.swapaxes(expand_weight, 1, 2),
        jnp.swapaxes(depth_kernel, 1, 2).astype(F32),
        jnp.swapaxes(reduce_weight, 1, 2),
    )


def unit(projected, axis):
    square = jnp.sum(projected * projected, axis=axis, keepdims=True)
    return (projected * lax.rsqrt(square + 1e-06)).astype(BF)


LABEL_ROWS = 16


def own_kernel(arrived_ref, ids_ref, head_ref, payload_ref, vectors_ref):
    n_dp, per_peer, width = arrived_ref.shape
    clips = n_dp * per_peer
    channels = head_ref.shape[0]
    arrived = arrived_ref[...].reshape(clips, width)[:, :channels]
    row = lax.broadcasted_iota(jnp.int32, (clips, clips), 0)
    lane = lax.broadcasted_iota(jnp.int32, (clips, clips), 1)
    pick = (lane == (row % n_dp) * per_peer + row // n_dp).astype(F32).astype(BF)
    rows = jnp.dot(pick, arrived, preferred_element_type=F32).astype(BF)
    projected = jnp.dot(rows, head_ref[...], preferred_element_type=F32)
    vectors_ref[...] = unit(projected, 1)
    payload_ref[0:channels, :] = jnp.transpose(rows.astype(F32)).astype(BF)
    ids = ids_ref[...]
    which = lax.broadcasted_iota(jnp.int32, (LABEL_ROWS, clips), 0)
    high, low = ids // 256, ids % 256
    label = jnp.where(which == 0, high, jnp.where(which == 1, low, 0))
    payload_ref[channels:, :] = label.astype(F32).astype(BF)


def own(arrived, cluster_ids, head_weight):
    n_dp, per_peer, width = arrived.shape
    channels, dims = head_weight.shape
    clips = n_dp * per_peer
    return pl.pallas_call(
        own_kernel,
        out_shape=(
            jax.ShapeDtypeStruct((channels + LABEL_ROWS, clips), BF),
            jax.ShapeDtypeStruct((clips, dims), BF),
        ),
        in_specs=[pl.BlockSpec(memory_space=pltpu.VMEM)] * 3,
        out_specs=(pl.BlockSpec(memory_space=pltpu.VMEM),) * 2,
        name="own",
    )(arrived, cluster_ids, head_weight)


PANEL_ROWS = 784
OCCUR = 64


def nearest_kernel(panel_rows, base_ref, rows_ref, head_ref, panel_ref, turned_ref, near_ref, own_ref, best_ref):
    n_cent, height, clips = rows_ref.shape
    dims, channels = head_ref.shape
    total = n_cent * clips
    step = pl.program_id(0)
    last = pl.num_programs(0) - 1

    @pl.when(step == 0)
    def _():
        @pl.loop(0, n_cent // 2)
        def _(pair):
            both = jnp.concatenate([rows_ref[2 * pair], rows_ref[2 * pair + 1]], axis=1)
            projected = jnp.dot(head_ref[...], both[:channels], preferred_element_type=F32)
            cols = pl.ds(pl.multiple_of(pair * 2 * clips, 2 * clips), 2 * clips)
            turned_ref[:, cols] = unit(projected, 0)

        best_ref[...] = jnp.full_like(best_ref, -jnp.inf)

    def score(cols):
        return jnp.dot(panel_ref[...], turned_ref[:, cols], preferred_element_type=F32)

    def keep(scores, cols):
        rows = scores.shape[0]
        best_ref[:, cols] = jnp.maximum(
            best_ref[:, cols], jnp.max(scores.reshape(rows // 8, 8, scores.shape[1]), axis=0)
        )

    for block in range(total // 256):
        cols = pl.ds(block * 256, 256)

        @pl.when(step < last)
        def _():
            scores = score(cols)
            keep(scores, cols)

            @pl.when(step == 0)
            def _():
                label = jnp.concatenate(
                    [rows_ref[2 * block, channels:, :], rows_ref[2 * block + 1, channels:, :]], axis=1
                ).astype(F32)
                local_id = (label[0:1] * 256.0 + label[1:2]).astype(jnp.int32) - base_ref[0]
                index = lax.broadcasted_iota(jnp.int32, (OCCUR, 256), 0)
                own_ref[:, cols] = jnp.max(
                    jnp.where(index == local_id, scores[:OCCUR], -jnp.inf), axis=0, keepdims=True
                )

        @pl.when(step == last)
        def _():
            scores = score(cols)
            index = lax.broadcasted_iota(jnp.int32, scores.shape, 0) + last * panel_ref.shape[0]
            keep(jnp.where(index < panel_rows, scores, -jnp.inf), cols)
            near_ref[:, cols] = jnp.max(best_ref[:, cols], axis=0, keepdims=True)


def nearest_of(rows, head_turned, centroids, base):
    n_cent, height, clips = rows.shape
    dims, channels = head_turned.shape
    total = n_cent * clips
    panel_rows = centroids.shape[0]
    whole = lambda shape: pl.BlockSpec(shape, lambda step: (0,) * len(shape))
    return pl.pallas_call(
        functools.partial(nearest_kernel, panel_rows),
        grid=(pl.cdiv(panel_rows, PANEL_ROWS),),
        out_shape=(
            jax.ShapeDtypeStruct((dims, total), BF),
            jax.ShapeDtypeStruct((1, total), F32),
            jax.ShapeDtypeStruct((1, total), F32),
        ),
        in_specs=[
            pl.BlockSpec(memory_space=pltpu.SMEM),
            whole(rows.shape),
            whole(head_turned.shape),
            pl.BlockSpec((PANEL_ROWS, dims), lambda step: (step, 0)),
        ],
        out_specs=(whole((dims, total)), whole((1, total)), whole((1, total))),
        scratch_shapes=[pltpu.VMEM((8, total), F32)],
        compiler_params=pltpu.CompilerParams(vmem_limit_bytes=60 << 20),
        name="nearest",
    )(base, rows, head_turned, centroids)


GROUP = 4


def peer_kernel(place_ref, cols_ref, rows_ref, turned_ref, head_ref, near_ref, own_ref, out_ref, best_ref):
    n_dp, height, clips = cols_ref.shape
    n_cent = rows_ref.shape[0]
    channels = head_ref.shape[0]
    total = n_cent * clips
    eye = (
        lax.broadcasted_iota(jnp.int32, (clips, clips), 0)
        == lax.broadcasted_iota(jnp.int32, (clips, clips), 1)
    ).astype(F32).astype(BF)
    best_ref[...] = jnp.full_like(best_ref, -1.0)
    mine_dp, mine_cent = place_ref[0], place_ref[1]

    @pl.loop(0, n_dp // GROUP)
    def _(group):
        flipped = jnp.concatenate(
            [
                lax.dot_general(
                    eye, cols_ref[group * GROUP + at], (((1,), (1,)), ((), ())), preferred_element_type=F32
                )
                for at in range(GROUP)
            ],
            axis=0,
        )
        projected = jnp.dot(flipped[:, :channels].astype(BF), head_ref[...], preferred_element_type=F32)
        vectors = unit(projected, 1)
        ids = flipped[:, channels : channels + 1] * 256.0 + flipped[:, channels + 1 : channels + 2]
        wide = jnp.broadcast_to(ids, (GROUP * clips, 256))
        line = lax.broadcasted_iota(jnp.int32, (GROUP * clips, 256), 0)
        lane = lax.broadcasted_iota(jnp.int32, (GROUP * clips, 256), 1)
        for block in range(total // 256):
            cols = pl.ds(block * 256, 256)
            scores = jnp.dot(vectors, turned_ref[:, cols], preferred_element_type=F32)
            label = jnp.concatenate(
                [rows_ref[2 * block, channels:, :], rows_ref[2 * block + 1, channels:, :]], axis=1
            ).astype(F32)
            row_ids = label[0:1] * 256.0 + label[1:2]
            self_line = lane + (mine_dp - group * GROUP) * clips - (mine_cent - 2 * block) * clips
            inside = (lane // clips) == (mine_cent - 2 * block)
            same = (wide == row_ids) & jnp.logical_not(inside & (line == self_line))
            found = jnp.where(same, scores, -1.0)
            best_ref[:, cols] = jnp.maximum(
                best_ref[:, cols], jnp.max(found.reshape(GROUP * clips // 8, 8, 256), axis=0)
            )

    best = jnp.max(best_ref[...], axis=0, keepdims=True)
    for cent in range(n_cent):
        cols = slice(cent * clips, (cent + 1) * clips)
        out_ref[cent, 0:1, :] = near_ref[:, cols]
        out_ref[cent, 1:2, :] = own_ref[:, cols]
        out_ref[cent, 2:3, :] = best[:, cols]
        out_ref[cent, 3:4, :] = best[:, cols]


def peers_of(cols, rows, turned, head_weight, near, own_best, place):
    n_cent, height, clips = rows.shape
    total = n_cent * clips
    return pl.pallas_call(
        peer_kernel,
        out_shape=jax.ShapeDtypeStruct((n_cent, 4, clips), F32),
        in_specs=[pl.BlockSpec(memory_space=pltpu.SMEM)] + [pl.BlockSpec(memory_space=pltpu.VMEM)] * 6,
        out_specs=pl.BlockSpec(memory_space=pltpu.VMEM),
        scratch_shapes=[pltpu.VMEM((8, total), F32)],
        compiler_params=pltpu.CompilerParams(vmem_limit_bytes=60 << 20),
        name="peers",
    )(place, cols, rows, turned, head_weight, near, own_best)


def local(
    clip_data,
    frame_counts,
    send_list,
    cluster_ids,
    expand_weight,
    depth_kernel,
    reduce_weight,
    head_weight,
    centroids,
):
    n_dp = lax.axis_size("dp")
    n_cent = lax.axis_size("cent")
    panel_rows = centroids.shape[0]
    mine_dp, mine_cent = lax.axis_index("dp"), lax.axis_index("cent")
    base = (mine_cent * panel_rows).astype(jnp.int32)[None]
    place = jnp.stack([mine_dp, mine_cent]).astype(jnp.int32)
    pooled = embed(
        clip_data, frame_counts, send_list, expand_weight, depth_kernel, reduce_weight, n_dp
    )
    arrived = lax.all_to_all(pooled, "dp", split_axis=0, concat_axis=0, tiled=True)
    payload, vectors = own(arrived, cluster_ids, head_weight)
    rows = lax.all_gather(payload, "cent", axis=0)
    spread = jnp.broadcast_to(payload, (n_dp,) + payload.shape)
    cols = lax.all_to_all(spread, "dp", split_axis=0, concat_axis=0, tiled=True)
    turned, near, own_best = nearest_of(rows, jnp.swapaxes(head_weight, 0, 1), centroids, base)
    partial = peers_of(cols, rows, turned, head_weight, near, own_best, place)
    parts = lax.all_to_all(partial, "cent", split_axis=0, concat_axis=0, tiled=True)
    final = jnp.max(parts, axis=0)
    return (vectors, final[0], final[1], final[2])


def solution(mesh):
    placed = (
        P(("dp", "cent"), None, None, None),
        P(("dp", "cent"), None),
        P(("dp", "cent"), None),
        P(("dp", "cent"), None),
        P(),
        P(),
        P(),
        P(),
        P("cent", None),
    )
    return jax.shard_map(
        local,
        mesh=mesh,
        in_specs=placed,
        out_specs=(
            P(("dp", "cent"), None),
            P(("dp", "cent")),
            P(("dp", "cent")),
            P(("dp", "cent")),
        ),
        check_vma=False,
    )
```

```python
import functools

import jax
import jax.numpy as jnp
from jax import lax
from jax.experimental import pallas as pl
from jax.experimental.pallas import tpu as pltpu
from jax.sharding import PartitionSpec as P

SIDE = 4
SPOTS = SIDE * SIDE
BF = jnp.bfloat16
F32 = jnp.float32


def neighbours(at, extent):
    return [(at + shift - 1, shift) for shift in range(3) if 0 <= at + shift - 1 < extent]


STEPS = 9


def identity(size):
    line = lax.broadcasted_iota(jnp.int32, (size, size), 0)
    lane = lax.broadcasted_iota(jnp.int32, (size, size), 1)
    return (line == lane).astype(F32).astype(BF)


def turn(eye, matrix):
    return lax.dot_general(eye, matrix, (((1,), (1,)), ((), ())), preferred_element_type=F32)


def embed_kernel(
    clip_ref, count_ref, send_ref, wide_ref, taps_ref, reduce_ref, out_ref, *scratch
):
    x_refs, hidden_refs, act_refs = scratch[0:6], scratch[6:12], scratch[12:15]
    pool_ref, packed_pool_ref = scratch[15:17]
    weight_refs = scratch[17:19]
    expand_ref, depth_ref = scratch[19:21]
    channels, clips = clip_ref.shape[2], clip_ref.shape[3]
    expanded = wide_ref.shape[2]
    eye = identity(expanded)
    for layer in range(2):
        expand_ref[layer] = turn(eye, wide_ref[layer]).astype(BF)
        depth_ref[layer, :, : taps_ref.shape[1]] = turn(eye, taps_ref[layer])

    counts = count_ref[...].astype(F32)
    line = lax.broadcasted_iota(jnp.int32, (clips, clips), 0)
    lane = lax.broadcasted_iota(jnp.int32, (clips, clips), 1)
    count_lane = jnp.broadcast_to(counts, (clips, clips))
    count_line = jnp.transpose(count_lane)
    ahead = (count_lane > count_line) | ((count_lane == count_line) & (lane < line))
    rank = jnp.dot(
        ahead.astype(F32).astype(BF), jnp.ones((clips, clips), BF), preferred_element_type=F32
    ).astype(jnp.int32)
    n1, n2, n3 = [jnp.sum((counts > frame).astype(jnp.int32)) for frame in (1, 2, 3)]
    blocks = expanded // 16 // STEPS
    one_hot = lambda mask: mask.astype(F32).astype(BF)
    order = one_hot(rank == lane)
    place = [
        order,
        one_hot((rank == lane) & (count_line > 1)),
        jnp.concatenate(
            [
                one_hot((rank == lane) & (count_line > 2)),
                one_hot((rank + n2 == lane) & (count_line > 3)),
            ],
            axis=0,
        ),
    ]
    row_lane = lax.broadcasted_iota(jnp.int32, (1, clips), 1)
    kept = [None, (row_lane < n1).astype(F32), (row_lane < n2 + n3).astype(F32)]
    tile_lane = lax.broadcasted_iota(jnp.int32, (16, clips), 1)
    in_second, in_third = tile_lane < n2, tile_lane < n3

    def expand(layer, tile, pair, both):
        hidden = jnp.maximum(jnp.dot(expand_ref[layer], both, preferred_element_type=F32), 0.0)
        hidden_refs[3 * layer + tile][2 * pair] = hidden[:, :clips]
        hidden_refs[3 * layer + tile][2 * pair + 1] = hidden[:, clips:]

    def gather(tile, pair):
        if tile < 2:
            spots = jnp.concatenate([clip_ref[tile, 2 * pair], clip_ref[tile, 2 * pair + 1]], axis=0)
        else:
            spots = jnp.concatenate(
                [
                    jnp.concatenate([clip_ref[2, 2 * pair + side], clip_ref[3, 2 * pair + side]], axis=1)
                    for side in range(2)
                ],
                axis=0,
            )
        x = jnp.dot(spots, place[tile], preferred_element_type=F32).astype(BF)
        x_refs[tile][2 * pair] = x[:channels]
        x_refs[tile][2 * pair + 1] = x[channels:]

    def expand_stored(layer, tile, pair):
        x_ref = x_refs[3 * layer + tile]
        expand(layer, tile, pair, jnp.concatenate([x_ref[2 * pair], x_ref[2 * pair + 1]], axis=1))

    def spread_taps(layer, step, first, last):
        rows = [pl.ds(pl.multiple_of((step * blocks + at) * 16, 16), 16) for at in range(blocks)]
        taps = [depth_ref[layer, row, :] for row in rows]
        for tap in range(first, last):
            for at in range(blocks):
                weight_refs[layer][step * blocks + at, tap] = jnp.broadcast_to(
                    taps[at][:, tap : tap + 1], (16, clips)
                )

    def reduce(layer, tile, pair):
        both = jnp.concatenate([act_refs[tile][2 * pair], act_refs[tile][2 * pair + 1]], axis=1)
        branch = jnp.dot(reduce_ref[layer], both, preferred_element_type=F32)
        result = []
        for side in range(2):
            part = branch[:, side * clips : (side + 1) * clips]
            if kept[tile] is not None:
                part = part * kept[tile]
            x = x_refs[3 * layer + tile][2 * pair + side].astype(F32) + part
            result.append(x.astype(BF))
        return result

    def reduce_store(tile, pair):
        x = reduce(0, tile, pair)
        x_refs[3 + tile][2 * pair] = x[0]
        x_refs[3 + tile][2 * pair + 1] = x[1]

    def reduce_pool(tile, pair, live):
        x = reduce(1, tile, pair)
        into = packed_pool_ref if tile == 2 else pool_ref
        into[...] += (x[0].astype(F32) + x[1].astype(F32)) * live

    def depthwise(layer, tile, block):
        rows = pl.ds(pl.multiple_of(block * 16, 16), 16)
        read = lambda source, spot: hidden_refs[3 * layer + source][spot, rows, :]
        if tile == 0:
            sources = [(1, lambda s: read(0, s)), (2, lambda s: read(1, s))]
        elif tile == 1:
            sources = [
                (0, lambda s: read(0, s)),
                (1, lambda s: read(1, s)),
                (2, lambda s: jnp.where(in_second, read(2, s), 0.0)),
            ]
        else:
            sources = [
                (0, lambda s: jnp.where(in_second, read(1, s), pltpu.roll(read(2, s), n2, 1))),
                (1, lambda s: read(2, s)),
                (2, lambda s: jnp.where(in_third, pltpu.roll(read(2, s), clips - n2, 1), 0.0)),
            ]
        mixed = [None] * SPOTS
        for shift_t, source in sources:
            weight = [weight_refs[layer][block, 9 * shift_t + tap].astype(BF) for tap in range(9)]
            hidden = [source(spot).astype(BF) for spot in range(SPOTS)]
            for y in range(SIDE):
                for from_y, shift_y in neighbours(y, SIDE):
                    for z in range(SIDE):
                        for from_z, shift_z in neighbours(z, SIDE):
                            term = hidden[from_y * SIDE + from_z] * weight[3 * shift_y + shift_z]
                            spot = y * SIDE + z
                            mixed[spot] = term if mixed[spot] is None else mixed[spot] + term
        for spot in range(SPOTS):
            half = mixed[spot] * BF(0.5)
            act_refs[tile][spot, rows, :] = half + half * jnp.tanh(half)

    def stage(layer, tile, other):
        @pl.loop(0, STEPS)
        def _(step):
            pair = jnp.minimum(step, SPOTS // 2 - 1)
            before = jnp.maximum(step - 1, 0)
            other(pair, before, (step < SPOTS // 2).astype(F32))
            if layer == 0:
                if tile == 0:
                    spread_taps(0, step, 0, 9)
                spread_taps(1, step, 9 * tile, 9 * tile + 9)
            for at in range(blocks):
                depthwise(layer, tile, step * blocks + at)

    def filler(first, second):
        def other(pair, before, live):
            second(before)
            first(pair)

        return other

    pool_ref[...] = jnp.zeros_like(pool_ref)
    packed_pool_ref[...] = jnp.zeros_like(packed_pool_ref)

    @pl.loop(0, STEPS)
    def _(step):
        pair = jnp.minimum(step, SPOTS // 2 - 1)
        before = jnp.maximum(step - 1, 0)
        for tile in range(2):
            expand_stored(0, tile, before)
            gather(tile, pair)
        spread_taps(0, step, 9, 27)

    stage(0, 0, filler(lambda pair: gather(2, pair), lambda pair: expand_stored(0, 2, pair)))
    stage(0, 1, filler(lambda pair: reduce_store(0, pair), lambda pair: expand_stored(1, 0, pair)))
    stage(0, 2, filler(lambda pair: reduce_store(1, pair), lambda pair: expand_stored(1, 1, pair)))
    stage(1, 0, filler(lambda pair: reduce_store(2, pair), lambda pair: expand_stored(1, 2, pair)))
    stage(1, 1, lambda pair, before, live: reduce_pool(0, pair, live))
    stage(1, 2, lambda pair, before, live: reduce_pool(1, pair, live))

    @pl.loop(0, SPOTS // 2)
    def _(pair):
        reduce_pool(2, pair, 1.0)

    packed = packed_pool_ref[...]
    total = (
        pool_ref[...]
        + jnp.where(row_lane < n2, packed, 0.0)
        + jnp.where(row_lane < n3, pltpu.roll(packed, clips - n2, 1), 0.0)
    )
    lengths = jnp.dot(
        jnp.broadcast_to(counts, (16, clips)).astype(BF), order, preferred_element_type=F32
    )[0:1]
    pooled = (total / (lengths * SPOTS)).astype(BF)
    n_dp, per_peer = out_ref.shape[0], out_ref.shape[1]
    slot = (line % per_peer) * n_dp + line // per_peer
    pick = one_hot(jnp.broadcast_to(send_ref[...], (clips, clips)) == slot)
    pick = lax.dot_general(pick, order, (((1,), (0,)), ((), ())), preferred_element_type=F32).astype(BF)
    rows = lax.dot_general(pick, pooled, (((1,), (1,)), ((), ())), preferred_element_type=F32)
    out_ref[:, :, :channels] = rows.astype(BF).reshape(n_dp, per_peer, channels)
    out_ref[:, :, channels:] = jnp.zeros((n_dp, per_peer, out_ref.shape[2] - channels), BF)


def embed(clip_data, frame_counts, send_list, expand_weight, depth_kernel, reduce_weight, n_dp):
    clips, frames, spots, channels = clip_data.shape
    expanded = expand_weight.shape[2]
    return pl.pallas_call(
        embed_kernel,
        out_shape=jax.ShapeDtypeStruct((n_dp, clips // n_dp, 256), BF),
        in_specs=[pl.BlockSpec(memory_space=pltpu.VMEM)] * 6,
        out_specs=pl.BlockSpec(memory_space=pltpu.VMEM),
        scratch_shapes=[pltpu.VMEM((spots, channels, clips), BF)] * 6
        + [pltpu.VMEM((spots, expanded, clips), F32)] * 6
        + [pltpu.VMEM((spots, expanded, clips), BF)] * 3
        + [pltpu.VMEM((channels, clips), F32)] * 2
        + [pltpu.VMEM((expanded // 16, 27, 16, clips), F32)] * 2
        + [pltpu.VMEM((2, expanded, channels), BF), pltpu.VMEM((2, expanded, clips), F32)],
        compiler_params=pltpu.CompilerParams(vmem_limit_bytes=60 << 20),
        name="embed",
    )(
        jnp.transpose(clip_data, (1, 2, 3, 0)),
        frame_counts,
        send_list,
        expand_weight,
        depth_kernel,
        jnp.swapaxes(reduce_weight, 1, 2),
    )


def unit(projected, axis):
    square = jnp.sum(projected * projected, axis=axis, keepdims=True)
    return (projected * lax.rsqrt(square + 1e-06)).astype(BF)


LABEL_ROWS = 16


def own_kernel(arrived_ref, ids_ref, payload_ref, spread_ref, rows_ref):
    n_dp, per_peer, width = arrived_ref.shape
    clips = n_dp * per_peer
    channels = rows_ref.shape[1]
    arrived = arrived_ref[...].reshape(clips, width)[:, :channels]
    row = lax.broadcasted_iota(jnp.int32, (clips, clips), 0)
    lane = lax.broadcasted_iota(jnp.int32, (clips, clips), 1)
    pick = (lane == (row % n_dp) * per_peer + row // n_dp).astype(F32).astype(BF)
    rows = jnp.dot(pick, arrived, preferred_element_type=F32)
    rows_ref[...] = rows.astype(BF)
    ids = ids_ref[...]
    which = lax.broadcasted_iota(jnp.int32, (LABEL_ROWS, clips), 0)
    high, low = ids // 256, ids % 256
    label = jnp.where(which == 0, high, jnp.where(which == 1, low, 0))
    payload = jnp.concatenate([jnp.transpose(rows), label.astype(F32)], axis=0).astype(BF)
    payload_ref[...] = payload
    for peer in range(n_dp):
        spread_ref[peer] = payload


def own(arrived, cluster_ids, channels):
    n_dp, per_peer, width = arrived.shape
    clips = n_dp * per_peer
    height = channels + LABEL_ROWS
    return pl.pallas_call(
        own_kernel,
        out_shape=(
            jax.ShapeDtypeStruct((height, clips), BF),
            jax.ShapeDtypeStruct((n_dp, height, clips), BF),
            jax.ShapeDtypeStruct((clips, channels), BF),
        ),
        in_specs=[pl.BlockSpec(memory_space=pltpu.VMEM)] * 2,
        out_specs=(pl.BlockSpec(memory_space=pltpu.VMEM),) * 3,
        name="own",
    )(arrived, cluster_ids)


def vectors_kernel(rows_ref, head_ref, vectors_ref):
    projected = jnp.dot(rows_ref[...], head_ref[...], preferred_element_type=F32)
    vectors_ref[...] = unit(projected, 1)


def vectors_of(rows, head_weight):
    clips, channels = rows.shape
    dims = head_weight.shape[1]
    return pl.pallas_call(
        vectors_kernel,
        out_shape=jax.ShapeDtypeStruct((clips, dims), BF),
        in_specs=[pl.BlockSpec(memory_space=pltpu.VMEM)] * 2,
        out_specs=pl.BlockSpec(memory_space=pltpu.VMEM),
        cost_estimate=pl.CostEstimate(
            flops=2 * clips * dims * channels, bytes_accessed=2 * dims * (clips + channels), transcendentals=0
        ),
        name="vectors",
    )(rows, head_weight)


PANEL_ROWS = 784
OCCUR = 64


def label_of(rows_ref, block, channels):
    label = jnp.concatenate(
        [rows_ref[2 * block, channels:, :], rows_ref[2 * block + 1, channels:, :]], axis=1
    ).astype(F32)
    return label[0:1] * 256.0 + label[1:2]


def nearest_kernel(panel_rows, rows_ref, head_ref, panel_ref, turned_ref, near_ref, own_ref, best_ref, flip_ref):
    blocks, height, clips = rows_ref.shape
    channels, dims = head_ref.shape
    total = blocks * clips
    step = pl.program_id(0)
    last = pl.num_programs(0) - 1
    base = lax.axis_index("cent") * panel_rows

    @pl.when(step == 0)
    def _():
        eye = identity(256)
        for part in range(dims // 256):
            part = slice(part * 256, (part + 1) * 256)
            flip_ref[part, :] = turn(eye, head_ref[:, part]).astype(BF)

        @pl.loop(0, blocks // 2)
        def _(pair):
            both = jnp.concatenate([rows_ref[2 * pair], rows_ref[2 * pair + 1]], axis=1)
            projected = jnp.dot(flip_ref[...], both[:channels], preferred_element_type=F32)
            cols = pl.ds(pl.multiple_of(pair * 2 * clips, 2 * clips), 2 * clips)
            turned_ref[:, cols] = unit(projected, 0)

        best_ref[...] = jnp.full_like(best_ref, -jnp.inf)

    def score(cols):
        return jnp.dot(panel_ref[...], turned_ref[:, cols], preferred_element_type=F32)

    def keep(scores, cols):
        rows = scores.shape[0]
        best_ref[:, cols] = jnp.maximum(
            best_ref[:, cols], jnp.max(scores.reshape(rows // 8, 8, scores.shape[1]), axis=0)
        )

    for block in range(total // 256):
        cols = pl.ds(block * 256, 256)

        @pl.when(step < last)
        def _():
            scores = score(cols)
            keep(scores, cols)

            @pl.when(step == 0)
            def _():
                local_id = label_of(rows_ref, block, channels).astype(jnp.int32) - base
                index = lax.broadcasted_iota(jnp.int32, (OCCUR, 256), 0)
                own_ref[:, cols] = jnp.max(
                    jnp.where(index == local_id, scores[:OCCUR], -jnp.inf), axis=0, keepdims=True
                )

        @pl.when(step == last)
        def _():
            scores = score(cols)
            index = lax.broadcasted_iota(jnp.int32, scores.shape, 0) + last * panel_ref.shape[0]
            keep(jnp.where(index < panel_rows, scores, -jnp.inf), cols)
            near_ref[:, cols] = jnp.max(best_ref[:, cols], axis=0, keepdims=True)


def nearest_of(rows, head_weight, centroids):
    blocks, height, clips = rows.shape
    channels, dims = head_weight.shape
    total = blocks * clips
    panel_rows = centroids.shape[0]
    whole = lambda shape: pl.BlockSpec(shape, lambda step: (0,) * len(shape))
    return pl.pallas_call(
        functools.partial(nearest_kernel, panel_rows),
        grid=(pl.cdiv(panel_rows, PANEL_ROWS),),
        out_shape=(
            jax.ShapeDtypeStruct((dims, total), BF),
            jax.ShapeDtypeStruct((1, total), F32),
            jax.ShapeDtypeStruct((1, total), F32),
        ),
        in_specs=[
            whole(rows.shape),
            whole(head_weight.shape),
            pl.BlockSpec((PANEL_ROWS, dims), lambda step: (step, 0)),
        ],
        out_specs=(whole((dims, total)), whole((1, total)), whole((1, total))),
        scratch_shapes=[pltpu.VMEM((8, total), F32), pltpu.VMEM((dims, channels), BF)],
        compiler_params=pltpu.CompilerParams(vmem_limit_bytes=48 << 20),
        cost_estimate=pl.CostEstimate(
            flops=2 * total * panel_rows * dims, bytes_accessed=2 * panel_rows * dims, transcendentals=0
        ),
        name="nearest",
    )(rows, head_weight, centroids)


GROUP = 4


def peer_kernel(
    cols_ref, near_rows_ref, far_rows_ref, near_turned_ref, far_turned_ref, head_ref,
    near_best_ref, far_best_ref, near_own_ref, far_own_ref, out_ref, best_ref,
):
    n_dp, height, clips = cols_ref.shape
    n_cent = out_ref.shape[0]
    channels = head_ref.shape[0]
    eye = identity(clips)
    best_ref[...] = jnp.full_like(best_ref, -1.0)
    mine_dp, mine_cent = lax.axis_index("dp"), lax.axis_index("cent")

    @pl.loop(0, n_dp // GROUP)
    def _(group):
        flipped = jnp.concatenate([turn(eye, cols_ref[group * GROUP + at]) for at in range(GROUP)], axis=0)
        projected = jnp.dot(flipped[:, :channels].astype(BF), head_ref[...], preferred_element_type=F32)
        vectors = unit(projected, 1)
        ids = flipped[:, channels : channels + 1] * 256.0 + flipped[:, channels + 1 : channels + 2]
        wide = jnp.broadcast_to(ids, (GROUP * clips, 2 * clips))
        for block in range(n_cent // 2):
            cols = slice(block * 2 * clips, (block + 1) * 2 * clips)
            if block == 0:
                turned, row_ids = near_turned_ref[...], label_of(near_rows_ref, 0, channels)
            else:
                far = slice((block - 1) * 2 * clips, block * 2 * clips)
                turned, row_ids = far_turned_ref[:, far], label_of(far_rows_ref, block - 1, channels)
            scores = jnp.dot(vectors, turned, preferred_element_type=F32)
            same = wide == row_ids
            if block == 0:
                line = lax.broadcasted_iota(jnp.int32, same.shape, 0)
                lane = lax.broadcasted_iota(jnp.int32, same.shape, 1)
                itself = jnp.where(lane < clips, lane + (mine_dp - group * GROUP) * clips, -1)
                same = same & (line != itself)
            found = jnp.where(same, scores, -1.0)
            best_ref[:, cols] = jnp.maximum(
                best_ref[:, cols], jnp.max(found.reshape(GROUP * clips // 8, 8, 2 * clips), axis=0)
            )

    best = jnp.max(best_ref[...], axis=0, keepdims=True)
    for block in range(n_cent // 2):
        for side in range(2):
            chip = (mine_cent // 2 + block) % (n_cent // 2)
            cent = 2 * chip + (mine_cent + side) % 2
            at = slice((2 * block + side) * clips, (2 * block + side + 1) * clips)
            if block == 0:
                part = slice(side * clips, (side + 1) * clips)
                nearest, own_best = near_best_ref[:, part], near_own_ref[:, part]
            else:
                part = slice((2 * block + side - 2) * clips, (2 * block + side - 1) * clips)
                nearest, own_best = far_best_ref[:, part], far_own_ref[:, part]
            out_ref[cent, 0:1, :] = nearest
            out_ref[cent, 1:2, :] = own_best
            out_ref[cent, 2:3, :] = best[:, at]
            out_ref[cent, 3:4, :] = best[:, at]


def peers_of(cols, near_rows, far_rows, near_found, far_found, head_weight):
    n_dp, height, clips = cols.shape
    n_cent = near_rows.shape[0] + far_rows.shape[0]
    dims = head_weight.shape[1]
    return pl.pallas_call(
        peer_kernel,
        out_shape=jax.ShapeDtypeStruct((n_cent, 4, clips), F32),
        in_specs=[pl.BlockSpec(memory_space=pltpu.VMEM)] * 10,
        out_specs=pl.BlockSpec(memory_space=pltpu.VMEM),
        scratch_shapes=[pltpu.VMEM((8, n_cent * clips), F32)],
        compiler_params=pltpu.CompilerParams(vmem_limit_bytes=48 << 20),
        cost_estimate=pl.CostEstimate(
            flops=2 * n_dp * n_cent * clips * clips * dims, bytes_accessed=4 << 20, transcendentals=0
        ),
        name="peers",
    )(
        cols, near_rows, far_rows, near_found[0], far_found[0], head_weight,
        near_found[1], far_found[1], near_found[2], far_found[2],
    )


def local(
    clip_data,
    frame_counts,
    send_list,
    cluster_ids,
    expand_weight,
    depth_kernel,
    reduce_weight,
    head_weight,
    centroids,
):
    n_dp = lax.axis_size("dp")
    n_cent = lax.axis_size("cent")
    pooled = embed(
        clip_data, frame_counts, send_list, expand_weight, depth_kernel, reduce_weight, n_dp
    )
    arrived = lax.all_to_all(pooled, "dp", split_axis=0, concat_axis=0, tiled=True)
    payload, spread, rows = own(arrived, cluster_ids, head_weight.shape[0])
    partner = lax.ppermute(payload, "cent", [(at, at ^ 1) for at in range(n_cent)])
    near_rows = jnp.stack([payload, partner])
    far_rows = jnp.concatenate(
        [
            lax.ppermute(near_rows, "cent", [((at + 2 * chip) % n_cent, at) for at in range(n_cent)])
            for chip in range(1, n_cent // 2)
        ]
    )
    cols = lax.all_to_all(spread, "dp", split_axis=0, concat_axis=0, tiled=True)
    vectors = vectors_of(rows, head_weight)
    near_found = nearest_of(near_rows, head_weight, centroids)
    far_found = nearest_of(far_rows, head_weight, centroids)
    partial = peers_of(cols, near_rows, far_rows, near_found, far_found, head_weight)
    parts = lax.all_to_all(partial, "cent", split_axis=0, concat_axis=0, tiled=True)
    final = jnp.max(parts, axis=0)
    return (vectors, final[0], final[1], final[2])


def solution(mesh):
    placed = (
        P(("dp", "cent"), None, None, None),
        P(("dp", "cent"), None),
        P(("dp", "cent"), None),
        P(("dp", "cent"), None),
        P(),
        P(),
        P(),
        P(),
        P("cent", None),
    )
    return jax.shard_map(
        local,
        mesh=mesh,
        in_specs=placed,
        out_specs=(
            P(("dp", "cent"), None),
            P(("dp", "cent")),
            P(("dp", "cent")),
            P(("dp", "cent")),
        ),
        check_vma=False,
    )
```

```python
import functools

import jax
import jax.numpy as jnp
from jax import lax
from jax.experimental import pallas as pl
from jax.experimental.pallas import tpu as pltpu
from jax.sharding import PartitionSpec as P

SIDE = 4
SPOTS = SIDE * SIDE
BF = jnp.bfloat16
F32 = jnp.float32


def neighbours(at, extent):
    return [(at + shift - 1, shift) for shift in range(3) if 0 <= at + shift - 1 < extent]


STEPS = 9


def identity(size):
    line = lax.broadcasted_iota(jnp.int32, (size, size), 0)
    lane = lax.broadcasted_iota(jnp.int32, (size, size), 1)
    return (line == lane).astype(F32).astype(BF)


def turn(eye, matrix):
    return lax.dot_general(eye, matrix, (((1,), (1,)), ((), ())), preferred_element_type=F32)


def embed_kernel(
    stored_ref, count_ref, send_ref, wide_ref, taps_ref, reduce_ref, out_ref, *scratch
):
    x_refs, hidden_refs, act_refs = scratch[0:6], scratch[6:12], scratch[12:15]
    pool_ref, packed_pool_ref = scratch[15:17]
    weight_refs = scratch[17:19]
    expand_ref, depth_ref = scratch[19:21]
    clip_ref, arrival = scratch[21:23]
    channels, clips = clip_ref.shape[2], clip_ref.shape[3]
    copies = [
        pltpu.make_async_copy(stored_ref.at[frame], clip_ref.at[frame], arrival.at[frame])
        for frame in range(clip_ref.shape[0])
    ]
    for copy in copies:
        copy.start()
    expanded = wide_ref.shape[2]
    eye = identity(expanded)
    for layer in range(2):
        expand_ref[layer] = turn(eye, wide_ref[layer]).astype(BF)
        depth_ref[layer, :, : taps_ref.shape[1]] = turn(eye, taps_ref[layer])

    counts = count_ref[...].astype(F32)
    line = lax.broadcasted_iota(jnp.int32, (clips, clips), 0)
    lane = lax.broadcasted_iota(jnp.int32, (clips, clips), 1)
    count_lane = jnp.broadcast_to(counts, (clips, clips))
    count_line = jnp.transpose(count_lane)
    ahead = (count_lane > count_line) | ((count_lane == count_line) & (lane < line))
    rank = jnp.dot(
        ahead.astype(F32).astype(BF), jnp.ones((clips, clips), BF), preferred_element_type=F32
    ).astype(jnp.int32)
    n1, n2, n3 = [jnp.sum((counts > frame).astype(jnp.int32)) for frame in (1, 2, 3)]
    blocks = expanded // 16 // STEPS
    one_hot = lambda mask: mask.astype(F32).astype(BF)
    order = one_hot(rank == lane)
    place = [
        order,
        one_hot((rank == lane) & (count_line > 1)),
        jnp.concatenate(
            [
                one_hot((rank == lane) & (count_line > 2)),
                one_hot((rank + n2 == lane) & (count_line > 3)),
            ],
            axis=0,
        ),
    ]
    row_lane = lax.broadcasted_iota(jnp.int32, (1, clips), 1)
    kept = [None, (row_lane < n1).astype(F32), (row_lane < n2 + n3).astype(F32)]
    tile_lane = lax.broadcasted_iota(jnp.int32, (16, clips), 1)
    in_second, in_third = tile_lane < n2, tile_lane < n3

    def expand(layer, tile, pair, both):
        hidden = jnp.maximum(jnp.dot(expand_ref[layer], both, preferred_element_type=F32), 0.0)
        hidden_refs[3 * layer + tile][2 * pair] = hidden[:, :clips]
        hidden_refs[3 * layer + tile][2 * pair + 1] = hidden[:, clips:]

    def gather(tile, pair):
        if tile < 2:
            spots = jnp.concatenate([clip_ref[tile, 2 * pair], clip_ref[tile, 2 * pair + 1]], axis=0)
        else:
            spots = jnp.concatenate(
                [
                    jnp.concatenate([clip_ref[2, 2 * pair + side], clip_ref[3, 2 * pair + side]], axis=1)
                    for side in range(2)
                ],
                axis=0,
            )
        x = jnp.dot(spots, place[tile], preferred_element_type=F32).astype(BF)
        x_refs[tile][2 * pair] = x[:channels]
        x_refs[tile][2 * pair + 1] = x[channels:]

    def expand_stored(layer, tile, pair):
        x_ref = x_refs[3 * layer + tile]
        expand(layer, tile, pair, jnp.concatenate([x_ref[2 * pair], x_ref[2 * pair + 1]], axis=1))

    def spread_taps(layer, step, first, last):
        rows = [pl.ds(pl.multiple_of((step * blocks + at) * 16, 16), 16) for at in range(blocks)]
        taps = [depth_ref[layer, row, :] for row in rows]
        for tap in range(first, last):
            for at in range(blocks):
                weight_refs[layer][step * blocks + at, tap] = jnp.broadcast_to(
                    taps[at][:, tap : tap + 1], (16, clips)
                )

    def reduce(layer, tile, pair):
        both = jnp.concatenate([act_refs[tile][2 * pair], act_refs[tile][2 * pair + 1]], axis=1)
        branch = jnp.dot(reduce_ref[layer], both, preferred_element_type=F32)
        result = []
        for side in range(2):
            part = branch[:, side * clips : (side + 1) * clips]
            if kept[tile] is not None:
                part = part * kept[tile]
            x = x_refs[3 * layer + tile][2 * pair + side].astype(F32) + part
            result.append(x.astype(BF))
        return result

    def reduce_store(tile, pair):
        x = reduce(0, tile, pair)
        x_refs[3 + tile][2 * pair] = x[0]
        x_refs[3 + tile][2 * pair + 1] = x[1]

    def reduce_pool(tile, pair, live):
        x = reduce(1, tile, pair)
        into = packed_pool_ref if tile == 2 else pool_ref
        into[...] += (x[0].astype(F32) + x[1].astype(F32)) * live

    def depthwise(layer, tile, block):
        rows = pl.ds(pl.multiple_of(block * 16, 16), 16)
        read = lambda source, spot: hidden_refs[3 * layer + source][spot, rows, :]
        if tile == 0:
            sources = [(1, lambda s: read(0, s)), (2, lambda s: read(1, s))]
        elif tile == 1:
            sources = [
                (0, lambda s: read(0, s)),
                (1, lambda s: read(1, s)),
                (2, lambda s: jnp.where(in_second, read(2, s), 0.0)),
            ]
        else:
            sources = [
                (0, lambda s: jnp.where(in_second, read(1, s), pltpu.roll(read(2, s), n2, 1))),
                (1, lambda s: read(2, s)),
                (2, lambda s: jnp.where(in_third, pltpu.roll(read(2, s), clips - n2, 1), 0.0)),
            ]
        mixed = [None] * SPOTS
        for shift_t, source in sources:
            weight = [weight_refs[layer][block, 9 * shift_t + tap].astype(BF) for tap in range(9)]
            hidden = [source(spot).astype(BF) for spot in range(SPOTS)]
            for y in range(SIDE):
                for from_y, shift_y in neighbours(y, SIDE):
                    for z in range(SIDE):
                        for from_z, shift_z in neighbours(z, SIDE):
                            term = hidden[from_y * SIDE + from_z] * weight[3 * shift_y + shift_z]
                            spot = y * SIDE + z
                            mixed[spot] = term if mixed[spot] is None else mixed[spot] + term
        for spot in range(SPOTS):
            half = mixed[spot] * BF(0.5)
            act_refs[tile][spot, rows, :] = half + half * jnp.tanh(half)

    def stage(layer, tile, other):
        @pl.loop(0, STEPS)
        def _(step):
            pair = jnp.minimum(step, SPOTS // 2 - 1)
            before = jnp.maximum(step - 1, 0)
            other(pair, before, (step < SPOTS // 2).astype(F32))
            if layer == 0:
                if tile == 0:
                    spread_taps(0, step, 0, 9)
                spread_taps(1, step, 9 * tile, 9 * tile + 9)
            for at in range(blocks):
                depthwise(layer, tile, step * blocks + at)

    def filler(first, second):
        def other(pair, before, live):
            second(before)
            first(pair)

        return other

    pool_ref[...] = jnp.zeros_like(pool_ref)
    packed_pool_ref[...] = jnp.zeros_like(packed_pool_ref)
    copies[0].wait()
    copies[1].wait()

    @pl.loop(0, STEPS)
    def _(step):
        pair = jnp.minimum(step, SPOTS // 2 - 1)
        before = jnp.maximum(step - 1, 0)
        for tile in range(2):
            expand_stored(0, tile, before)
            gather(tile, pair)
        spread_taps(0, step, 9, 27)

    copies[2].wait()
    copies[3].wait()
    stage(0, 0, filler(lambda pair: gather(2, pair), lambda pair: expand_stored(0, 2, pair)))
    stage(0, 1, filler(lambda pair: reduce_store(0, pair), lambda pair: expand_stored(1, 0, pair)))
    stage(0, 2, filler(lambda pair: reduce_store(1, pair), lambda pair: expand_stored(1, 1, pair)))
    stage(1, 0, filler(lambda pair: reduce_store(2, pair), lambda pair: expand_stored(1, 2, pair)))
    stage(1, 1, lambda pair, before, live: reduce_pool(0, pair, live))
    stage(1, 2, lambda pair, before, live: reduce_pool(1, pair, live))

    @pl.loop(0, SPOTS // 2)
    def _(pair):
        reduce_pool(2, pair, 1.0)

    packed = packed_pool_ref[...]
    total = (
        pool_ref[...]
        + jnp.where(row_lane < n2, packed, 0.0)
        + jnp.where(row_lane < n3, pltpu.roll(packed, clips - n2, 1), 0.0)
    )
    lengths = jnp.dot(
        jnp.broadcast_to(counts, (16, clips)).astype(BF), order, preferred_element_type=F32
    )[0:1]
    pooled = (total / (lengths * SPOTS)).astype(BF)
    n_dp, per_peer = out_ref.shape[0], out_ref.shape[1]
    slot = (line % per_peer) * n_dp + line // per_peer
    pick = one_hot(jnp.broadcast_to(send_ref[...], (clips, clips)) == slot)
    pick = lax.dot_general(pick, order, (((1,), (0,)), ((), ())), preferred_element_type=F32).astype(BF)
    rows = lax.dot_general(pick, pooled, (((1,), (1,)), ((), ())), preferred_element_type=F32)
    out_ref[:, :, :channels] = rows.astype(BF).reshape(n_dp, per_peer, channels)
    out_ref[:, :, channels:] = jnp.zeros((n_dp, per_peer, out_ref.shape[2] - channels), BF)


def embed(clip_data, frame_counts, send_list, expand_weight, depth_kernel, reduce_weight, n_dp):
    clips, frames, spots, channels = clip_data.shape
    expanded = expand_weight.shape[2]
    return pl.pallas_call(
        embed_kernel,
        out_shape=jax.ShapeDtypeStruct((n_dp, clips // n_dp, 256), BF),
        in_specs=[pl.BlockSpec(memory_space=pltpu.HBM)] + [pl.BlockSpec(memory_space=pltpu.VMEM)] * 5,
        out_specs=pl.BlockSpec(memory_space=pltpu.VMEM),
        scratch_shapes=[pltpu.VMEM((spots, channels, clips), BF)] * 6
        + [pltpu.VMEM((spots, expanded, clips), F32)] * 6
        + [pltpu.VMEM((spots, expanded, clips), BF)] * 3
        + [pltpu.VMEM((channels, clips), F32)] * 2
        + [pltpu.VMEM((expanded // 16, 27, 16, clips), F32)] * 2
        + [pltpu.VMEM((2, expanded, channels), BF), pltpu.VMEM((2, expanded, clips), F32)]
        + [pltpu.VMEM((frames, spots, channels, clips), BF), pltpu.SemaphoreType.DMA((frames,))],
        compiler_params=pltpu.CompilerParams(vmem_limit_bytes=52 << 20),
        name="embed",
    )(
        jnp.transpose(clip_data, (1, 2, 3, 0)),
        frame_counts,
        send_list,
        expand_weight,
        depth_kernel,
        jnp.swapaxes(reduce_weight, 1, 2),
    )


def unit(projected, axis):
    square = jnp.sum(projected * projected, axis=axis, keepdims=True)
    return (projected * lax.rsqrt(square + 1e-06)).astype(BF)


LABEL_ROWS = 16


def own_kernel(arrived_ref, ids_ref, payload_ref, spread_ref, rows_ref):
    n_dp, per_peer, width = arrived_ref.shape
    clips = n_dp * per_peer
    channels = rows_ref.shape[1]
    arrived = arrived_ref[...].reshape(clips, width)[:, :channels]
    row = lax.broadcasted_iota(jnp.int32, (clips, clips), 0)
    lane = lax.broadcasted_iota(jnp.int32, (clips, clips), 1)
    pick = (lane == (row % n_dp) * per_peer + row // n_dp).astype(F32).astype(BF)
    rows = jnp.dot(pick, arrived, preferred_element_type=F32)
    rows_ref[...] = rows.astype(BF)
    ids = ids_ref[...]
    which = lax.broadcasted_iota(jnp.int32, (LABEL_ROWS, clips), 0)
    high, low = ids // 256, ids % 256
    label = jnp.where(which == 0, high, jnp.where(which == 1, low, 0))
    payload = jnp.concatenate([jnp.transpose(rows), label.astype(F32)], axis=0).astype(BF)
    payload_ref[...] = payload
    for peer in range(n_dp):
        spread_ref[peer] = payload


def own(arrived, cluster_ids, channels):
    n_dp, per_peer, width = arrived.shape
    clips = n_dp * per_peer
    height = channels + LABEL_ROWS
    return pl.pallas_call(
        own_kernel,
        out_shape=(
            jax.ShapeDtypeStruct((height, clips), BF),
            jax.ShapeDtypeStruct((n_dp, height, clips), BF),
            jax.ShapeDtypeStruct((clips, channels), BF),
        ),
        in_specs=[pl.BlockSpec(memory_space=pltpu.VMEM)] * 2,
        out_specs=(pl.BlockSpec(memory_space=pltpu.VMEM),) * 3,
        name="own",
    )(arrived, cluster_ids)


def vectors_kernel(rows_ref, head_ref, vectors_ref):
    projected = jnp.dot(rows_ref[...], head_ref[...], preferred_element_type=F32)
    vectors_ref[...] = unit(projected, 1)


def vectors_of(rows, head_weight):
    clips, channels = rows.shape
    dims = head_weight.shape[1]
    return pl.pallas_call(
        vectors_kernel,
        out_shape=jax.ShapeDtypeStruct((clips, dims), BF),
        in_specs=[pl.BlockSpec(memory_space=pltpu.VMEM)] * 2,
        out_specs=pl.BlockSpec(memory_space=pltpu.VMEM),
        cost_estimate=pl.CostEstimate(
            flops=2 * clips * dims * channels, bytes_accessed=2 * dims * (clips + channels), transcendentals=0
        ),
        name="vectors",
    )(rows, head_weight)


PANEL_ROWS = 784
OCCUR = 64


def label_of(rows_ref, block, channels):
    label = jnp.concatenate(
        [rows_ref[2 * block, channels:, :], rows_ref[2 * block + 1, channels:, :]], axis=1
    ).astype(F32)
    return label[0:1] * 256.0 + label[1:2]


def fetch(stored_ref, panel_ref, arrival):
    even = panel_ref.shape[0]
    copies = []
    for part in range(arrival.shape[0]):
        at = slice(part * PANEL_ROWS, min(even, (part + 1) * PANEL_ROWS))
        copy = pltpu.make_async_copy(stored_ref.at[at], panel_ref.at[at], arrival.at[part])
        copy.start()
        copies.append((at, copy))
    return copies


def score_rows(
    rows_ref, head_ref, tail_ref, panel_rows, panel_ref, copies, turned_ref, near_ref, own_ref, best_ref, flip_ref
):
    blocks, height, clips = rows_ref.shape
    channels, dims = head_ref.shape
    base = lax.axis_index("cent") * panel_rows
    eye = identity(256)
    for part in range(dims // 256):
        part = slice(part * 256, (part + 1) * 256)
        flip_ref[part, :] = turn(eye, head_ref[:, part]).astype(BF)

    @pl.loop(0, blocks // 2)
    def _(pair):
        both = jnp.concatenate([rows_ref[2 * pair], rows_ref[2 * pair + 1]], axis=1)
        projected = jnp.dot(flip_ref[...], both[:channels], preferred_element_type=F32)
        turned_ref[pair] = unit(projected, 0)
        scores = jnp.dot(tail_ref[...], turned_ref[pair], preferred_element_type=F32)
        index = lax.broadcasted_iota(jnp.int32, scores.shape, 0)
        best_ref[pair] = jnp.where(index < panel_rows - panel_ref.shape[0], scores, -jnp.inf)

    copies[0][1].wait()

    @pl.loop(0, blocks // 2)
    def _(pair):
        scores = jnp.dot(panel_ref[:OCCUR, :], turned_ref[pair], preferred_element_type=F32)
        local_id = label_of(rows_ref, pair, channels).astype(jnp.int32) - base
        index = lax.broadcasted_iota(jnp.int32, (OCCUR, 2 * clips), 0)
        own_ref[pair] = jnp.max(jnp.where(index == local_id, scores, -jnp.inf), axis=0, keepdims=True)

    for part, (at, copy) in enumerate(copies):
        if part > 0:
            copy.wait()

        @pl.loop(0, blocks // 2)
        def _(pair):
            scores = jnp.dot(panel_ref[at, :], turned_ref[pair], preferred_element_type=F32)
            best_ref[pair] = jnp.maximum(
                best_ref[pair], jnp.max(scores.reshape((at.stop - at.start) // 8, 8, 2 * clips), axis=0)
            )

    for pair in range(blocks // 2):
        near_ref[pair] = jnp.max(best_ref[pair], axis=0, keepdims=True)


def near_kernel(
    rows_ref, head_ref, tail_ref, stored_ref, turned_ref, near_ref, own_ref, best_ref, flip_ref, panel_ref, arrival
):
    copies = fetch(stored_ref, panel_ref, arrival)
    score_rows(
        rows_ref, head_ref, tail_ref, stored_ref.shape[0], panel_ref, copies,
        turned_ref, near_ref, own_ref, best_ref, flip_ref,
    )


def panel_specs(panel_rows, dims):
    even = panel_rows // 8 * 8
    return (
        [pl.BlockSpec((8, dims), lambda step: (even // 8, 0)), pl.BlockSpec(memory_space=pltpu.HBM)],
        [pltpu.VMEM((even, dims), BF), pltpu.SemaphoreType.DMA((pl.cdiv(even, PANEL_ROWS),))],
    )


def scores_shape(pairs, dims, width):
    return [
        jax.ShapeDtypeStruct((pairs, dims, width), BF),
        jax.ShapeDtypeStruct((pairs, 1, width), F32),
        jax.ShapeDtypeStruct((pairs, 1, width), F32),
    ]


def near_of(rows, head_weight, centroids):
    blocks, height, clips = rows.shape
    channels, dims = head_weight.shape
    pairs = blocks // 2
    panel_rows = centroids.shape[0]
    specs, scratch = panel_specs(panel_rows, dims)
    return pl.pallas_call(
        near_kernel,
        grid=(1,),
        out_shape=scores_shape(pairs, dims, 2 * clips),
        in_specs=[pl.BlockSpec(memory_space=pltpu.VMEM)] * 2 + specs,
        out_specs=[pl.BlockSpec(memory_space=pltpu.VMEM)] * 3,
        scratch_shapes=[pltpu.VMEM((pairs, 8, 2 * clips), F32), pltpu.VMEM((dims, channels), BF)] + scratch,
        compiler_params=pltpu.CompilerParams(vmem_limit_bytes=52 << 20),
        cost_estimate=pl.CostEstimate(
            flops=2 * blocks * clips * panel_rows * dims, bytes_accessed=2 * panel_rows * dims, transcendentals=0
        ),
        name="near",
    )(rows, head_weight, centroids, centroids)


GROUP = 4


def far_kernel(
    near_rows_ref, near_turned_ref, near_best_ref, near_own_ref, far_rows_ref, cols_ref, head_ref, tail_ref, stored_ref,
    out_ref, far_turned_ref, far_best_ref, far_own_ref, running_ref, flip_ref, panel_ref, arrival, best_ref,
):
    copies = fetch(stored_ref, panel_ref, arrival)
    score_rows(
        far_rows_ref, head_ref, tail_ref, stored_ref.shape[0], panel_ref, copies,
        far_turned_ref, far_best_ref, far_own_ref, running_ref, flip_ref,
    )
    n_dp, height, clips = cols_ref.shape
    n_cent = out_ref.shape[0]
    channels = head_ref.shape[0]
    eye = identity(clips)
    best_ref[...] = jnp.full_like(best_ref, -1.0)
    mine_dp, mine_cent = lax.axis_index("dp"), lax.axis_index("cent")

    @pl.loop(0, n_dp // GROUP)
    def _(group):
        flipped = jnp.concatenate([turn(eye, cols_ref[group * GROUP + at]) for at in range(GROUP)], axis=0)
        projected = jnp.dot(flipped[:, :channels].astype(BF), head_ref[...], preferred_element_type=F32)
        vectors = unit(projected, 1)
        ids = flipped[:, channels : channels + 1] * 256.0 + flipped[:, channels + 1 : channels + 2]
        wide = jnp.broadcast_to(ids, (GROUP * clips, 2 * clips))
        for block in range(n_cent // 2):
            cols = slice(block * 2 * clips, (block + 1) * 2 * clips)
            if block == 0:
                turned, row_ids = near_turned_ref[0], label_of(near_rows_ref, 0, channels)
            else:
                turned, row_ids = far_turned_ref[block - 1], label_of(far_rows_ref, block - 1, channels)
            scores = jnp.dot(vectors, turned, preferred_element_type=F32)
            same = wide == row_ids
            if block == 0:
                line = lax.broadcasted_iota(jnp.int32, same.shape, 0)
                lane = lax.broadcasted_iota(jnp.int32, same.shape, 1)
                itself = jnp.where(lane < clips, lane + (mine_dp - group * GROUP) * clips, -1)
                same = same & (line != itself)
            found = jnp.where(same, scores, -1.0)
            best_ref[:, cols] = jnp.maximum(
                best_ref[:, cols], jnp.max(found.reshape(GROUP * clips // 8, 8, 2 * clips), axis=0)
            )

    best = jnp.max(best_ref[...], axis=0, keepdims=True)
    for block in range(n_cent // 2):
        for side in range(2):
            chip = (mine_cent // 2 + block) % (n_cent // 2)
            cent = 2 * chip + (mine_cent + side) % 2
            at = slice((2 * block + side) * clips, (2 * block + side + 1) * clips)
            part = slice(side * clips, (side + 1) * clips)
            if block == 0:
                nearest, own_best = near_best_ref[0, :, part], near_own_ref[0, :, part]
            else:
                nearest, own_best = far_best_ref[block - 1, :, part], far_own_ref[block - 1, :, part]
            out_ref[cent, 0:1, :] = nearest
            out_ref[cent, 1:2, :] = own_best
            out_ref[cent, 2:3, :] = best[:, at]
            out_ref[cent, 3:4, :] = best[:, at]


def far_of(near_rows, near_found, far_rows, cols, head_weight, centroids):
    n_dp, height, clips = cols.shape
    n_cent = near_rows.shape[0] + far_rows.shape[0]
    channels, dims = head_weight.shape
    pairs = far_rows.shape[0] // 2
    panel_rows = centroids.shape[0]
    specs, scratch = panel_specs(panel_rows, dims)
    found = [pltpu.VMEM(part.shape, part.dtype) for part in scores_shape(pairs, dims, 2 * clips)]
    return pl.pallas_call(
        far_kernel,
        grid=(1,),
        out_shape=jax.ShapeDtypeStruct((n_cent, 4, clips), F32),
        in_specs=[pl.BlockSpec(memory_space=pltpu.VMEM)] * 7 + specs,
        out_specs=pl.BlockSpec(memory_space=pltpu.VMEM),
        scratch_shapes=found
        + [pltpu.VMEM((pairs, 8, 2 * clips), F32), pltpu.VMEM((dims, channels), BF)]
        + scratch
        + [pltpu.VMEM((8, n_cent * clips), F32)],
        compiler_params=pltpu.CompilerParams(vmem_limit_bytes=44 << 20),
        cost_estimate=pl.CostEstimate(
            flops=2 * clips * dims * (2 * pairs * panel_rows + n_dp * n_cent * clips),
            bytes_accessed=2 * panel_rows * dims,
            transcendentals=0,
        ),
        name="far",
    )(near_rows, *near_found, far_rows, cols, head_weight, centroids, centroids)


def local(
    clip_data,
    frame_counts,
    send_list,
    cluster_ids,
    expand_weight,
    depth_kernel,
    reduce_weight,
    head_weight,
    centroids,
):
    n_dp = lax.axis_size("dp")
    n_cent = lax.axis_size("cent")
    pooled = embed(
        clip_data, frame_counts, send_list, expand_weight, depth_kernel, reduce_weight, n_dp
    )
    arrived = lax.all_to_all(pooled, "dp", split_axis=0, concat_axis=0, tiled=True)
    payload, spread, rows = own(arrived, cluster_ids, head_weight.shape[0])
    partner = lax.ppermute(payload, "cent", [(at, at ^ 1) for at in range(n_cent)])
    near_rows = jnp.stack([payload, partner])
    far_rows = jnp.concatenate(
        [
            lax.ppermute(near_rows, "cent", [((at + 2 * chip) % n_cent, at) for at in range(n_cent)])
            for chip in range(1, n_cent // 2)
        ]
    )
    cols = lax.all_to_all(spread, "dp", split_axis=0, concat_axis=0, tiled=True)
    vectors = vectors_of(rows, head_weight)
    near_found = near_of(near_rows, head_weight, centroids)
    partial = far_of(near_rows, near_found, far_rows, cols, head_weight, centroids)
    parts = lax.all_to_all(partial, "cent", split_axis=0, concat_axis=0, tiled=True)
    final = jnp.max(parts, axis=0)
    return (vectors, final[0], final[1], final[2])


def solution(mesh):
    placed = (
        P(("dp", "cent"), None, None, None),
        P(("dp", "cent"), None),
        P(("dp", "cent"), None),
        P(("dp", "cent"), None),
        P(),
        P(),
        P(),
        P(),
        P("cent", None),
    )
    return jax.shard_map(
        local,
        mesh=mesh,
        in_specs=placed,
        out_specs=(
            P(("dp", "cent"), None),
            P(("dp", "cent")),
            P(("dp", "cent")),
            P(("dp", "cent")),
        ),
        check_vma=False,
    )
```

```python
import functools

import jax
import jax.numpy as jnp
from jax import lax
from jax.experimental import pallas as pl
from jax.experimental.pallas import tpu as pltpu
from jax.sharding import PartitionSpec as P

SIDE = 4
SPOTS = SIDE * SIDE
BF = jnp.bfloat16
F32 = jnp.float32


def neighbours(at, extent):
    return [(at + shift - 1, shift) for shift in range(3) if 0 <= at + shift - 1 < extent]


STEPS = 9


def identity(size):
    line = lax.broadcasted_iota(jnp.int32, (size, size), 0)
    lane = lax.broadcasted_iota(jnp.int32, (size, size), 1)
    return (line == lane).astype(F32).astype(BF)


def turn(eye, matrix):
    return lax.dot_general(eye, matrix, (((1,), (1,)), ((), ())), preferred_element_type=F32)


def embed_kernel(
    stored_ref, counts_hbm, send_hbm, wide_hbm, taps_ref, reduce_hbm, head_hbm, panel_hbm,
    out_ref, panel_ref, head_ref, flip_ref, *scratch,
):
    x_refs, act_refs = scratch[0:6], scratch[10:13]
    hidden_refs = scratch[6:10] + scratch[6:8]
    pool_ref, packed_pool_ref = scratch[13:15]
    weight_refs = scratch[15:17]
    expand_ref, depth_ref, clip_ref, arrival = scratch[17:21]
    count_ref, send_ref, wide_ref, reduce_ref, ready = scratch[21:26]
    channels, clips = clip_ref.shape[2], clip_ref.shape[3]
    early = [
        pltpu.make_async_copy(source, target, ready.at[at])
        for at, (source, target) in enumerate(
            [(counts_hbm, count_ref), (send_hbm, send_ref), (wide_hbm, wide_ref), (reduce_hbm, reduce_ref)]
        )
    ]
    late = [
        pltpu.make_async_copy(source, target, ready.at[4 + at])
        for at, (source, target) in enumerate([(head_hbm, head_ref), (panel_hbm, panel_ref)])
    ]
    for copy in early:
        copy.start()
    copies = [
        pltpu.make_async_copy(stored_ref.at[frame], clip_ref.at[frame], arrival.at[frame])
        for frame in range(clip_ref.shape[0])
    ]
    for copy in copies:
        copy.start()
    for copy in early:
        copy.wait()
    expanded = wide_ref.shape[2]
    eye = identity(expanded)
    for layer in range(2):
        expand_ref[layer] = turn(eye, wide_ref[layer]).astype(BF)
        depth_ref[layer, :, : taps_ref.shape[1]] = turn(eye, taps_ref[layer])

    counts = count_ref[...].astype(F32)
    line = lax.broadcasted_iota(jnp.int32, (clips, clips), 0)
    lane = lax.broadcasted_iota(jnp.int32, (clips, clips), 1)
    count_lane = jnp.broadcast_to(counts, (clips, clips))
    count_line = jnp.transpose(count_lane)
    ahead = (count_lane > count_line) | ((count_lane == count_line) & (lane < line))
    rank = jnp.dot(
        ahead.astype(F32).astype(BF), jnp.ones((clips, clips), BF), preferred_element_type=F32
    ).astype(jnp.int32)
    n1, n2, n3 = [jnp.sum((counts > frame).astype(jnp.int32)) for frame in (1, 2, 3)]
    blocks = expanded // 16 // STEPS
    one_hot = lambda mask: mask.astype(F32).astype(BF)
    order = one_hot(rank == lane)
    place = [
        order,
        one_hot((rank == lane) & (count_line > 1)),
        jnp.concatenate(
            [
                one_hot((rank == lane) & (count_line > 2)),
                one_hot((rank + n2 == lane) & (count_line > 3)),
            ],
            axis=0,
        ),
    ]
    row_lane = lax.broadcasted_iota(jnp.int32, (1, clips), 1)
    kept = [None, (row_lane < n1).astype(F32), (row_lane < n2 + n3).astype(F32)]
    tile_lane = lax.broadcasted_iota(jnp.int32, (16, clips), 1)
    in_second, in_third = tile_lane < n2, tile_lane < n3

    def expand(layer, tile, pair, both):
        hidden = jnp.maximum(jnp.dot(expand_ref[layer], both, preferred_element_type=F32), 0.0)
        hidden_refs[3 * layer + tile][2 * pair] = hidden[:, :clips]
        hidden_refs[3 * layer + tile][2 * pair + 1] = hidden[:, clips:]

    def gather(tile, pair):
        if tile < 2:
            spots = jnp.concatenate([clip_ref[tile, 2 * pair], clip_ref[tile, 2 * pair + 1]], axis=0)
        else:
            spots = jnp.concatenate(
                [
                    jnp.concatenate([clip_ref[2, 2 * pair + side], clip_ref[3, 2 * pair + side]], axis=1)
                    for side in range(2)
                ],
                axis=0,
            )
        x = jnp.dot(spots, place[tile], preferred_element_type=F32).astype(BF)
        x_refs[tile][2 * pair] = x[:channels]
        x_refs[tile][2 * pair + 1] = x[channels:]

    def expand_stored(layer, tile, pair):
        x_ref = x_refs[3 * layer + tile]
        expand(layer, tile, pair, jnp.concatenate([x_ref[2 * pair], x_ref[2 * pair + 1]], axis=1))

    def spread_taps(layer, step, first, last):
        rows = [pl.ds(pl.multiple_of((step * blocks + at) * 16, 16), 16) for at in range(blocks)]
        taps = [depth_ref[layer, row, :] for row in rows]
        for tap in range(first, last):
            for at in range(blocks):
                weight_refs[layer][step * blocks + at, tap] = jnp.broadcast_to(
                    taps[at][:, tap : tap + 1], (16, clips)
                )

    def reduce(layer, tile, pair):
        both = jnp.concatenate([act_refs[tile][2 * pair], act_refs[tile][2 * pair + 1]], axis=1)
        branch = jnp.dot(reduce_ref[layer], both, preferred_element_type=F32)
        result = []
        for side in range(2):
            part = branch[:, side * clips : (side + 1) * clips]
            if kept[tile] is not None:
                part = part * kept[tile]
            x = x_refs[3 * layer + tile][2 * pair + side].astype(F32) + part
            result.append(x.astype(BF))
        return result

    def reduce_store(tile, pair):
        x = reduce(0, tile, pair)
        x_refs[3 + tile][2 * pair] = x[0]
        x_refs[3 + tile][2 * pair + 1] = x[1]

    def reduce_pool(tile, pair, live):
        x = reduce(1, tile, pair)
        into = packed_pool_ref if tile == 2 else pool_ref
        into[...] += (x[0].astype(F32) + x[1].astype(F32)) * live

    def depthwise(layer, tile, block):
        rows = pl.ds(pl.multiple_of(block * 16, 16), 16)
        read = lambda source, spot: hidden_refs[3 * layer + source][spot, rows, :]
        if tile == 0:
            sources = [(1, lambda s: read(0, s)), (2, lambda s: read(1, s))]
        elif tile == 1:
            sources = [
                (0, lambda s: read(0, s)),
                (1, lambda s: read(1, s)),
                (2, lambda s: jnp.where(in_second, read(2, s), 0.0)),
            ]
        else:
            sources = [
                (0, lambda s: jnp.where(in_second, read(1, s), pltpu.roll(read(2, s), n2, 1))),
                (1, lambda s: read(2, s)),
                (2, lambda s: jnp.where(in_third, pltpu.roll(read(2, s), clips - n2, 1), 0.0)),
            ]
        mixed = [None] * SPOTS
        for shift_t, source in sources:
            weight = [weight_refs[layer][block, 9 * shift_t + tap].astype(BF) for tap in range(9)]
            hidden = [source(spot).astype(BF) for spot in range(SPOTS)]
            for y in range(SIDE):
                for from_y, shift_y in neighbours(y, SIDE):
                    for z in range(SIDE):
                        for from_z, shift_z in neighbours(z, SIDE):
                            term = hidden[from_y * SIDE + from_z] * weight[3 * shift_y + shift_z]
                            spot = y * SIDE + z
                            mixed[spot] = term if mixed[spot] is None else mixed[spot] + term
        for spot in range(SPOTS):
            half = mixed[spot] * BF(0.5)
            act_refs[tile][spot, rows, :] = half + half * jnp.tanh(half)

    def stage(layer, tile, other):
        @pl.loop(0, STEPS)
        def _(step):
            pair = jnp.minimum(step, SPOTS // 2 - 1)
            before = jnp.maximum(step - 1, 0)
            other(pair, before, (step < SPOTS // 2).astype(F32))
            if layer == 0:
                if tile == 0:
                    spread_taps(0, step, 0, 9)
                spread_taps(1, step, 9 * tile, 9 * tile + 9)
            for at in range(blocks):
                depthwise(layer, tile, step * blocks + at)

    def filler(first, second):
        def other(pair, before, live):
            second(before)
            first(pair)

        return other

    pool_ref[...] = jnp.zeros_like(pool_ref)
    packed_pool_ref[...] = jnp.zeros_like(packed_pool_ref)
    copies[0].wait()
    copies[1].wait()

    @pl.loop(0, STEPS)
    def _(step):
        pair = jnp.minimum(step, SPOTS // 2 - 1)
        before = jnp.maximum(step - 1, 0)
        for tile in range(2):
            expand_stored(0, tile, before)
            gather(tile, pair)
        spread_taps(0, step, 9, 27)

    copies[2].wait()
    copies[3].wait()
    for copy in late:
        copy.start()
    stage(0, 0, filler(lambda pair: gather(2, pair), lambda pair: expand_stored(0, 2, pair)))
    stage(0, 1, filler(lambda pair: reduce_store(0, pair), lambda pair: expand_stored(1, 0, pair)))
    stage(0, 2, filler(lambda pair: reduce_store(1, pair), lambda pair: expand_stored(1, 1, pair)))
    stage(1, 0, filler(lambda pair: reduce_store(2, pair), lambda pair: expand_stored(1, 2, pair)))
    stage(1, 1, lambda pair, before, live: reduce_pool(0, pair, live))
    stage(1, 2, lambda pair, before, live: reduce_pool(1, pair, live))

    @pl.loop(0, SPOTS // 2)
    def _(pair):
        reduce_pool(2, pair, 1.0)

    late[0].wait()
    small = identity(256)
    for part in range(flip_ref.shape[0] // 256):
        part = slice(part * 256, (part + 1) * 256)
        flip_ref[part, :] = turn(small, head_ref[:, part]).astype(BF)
    packed = packed_pool_ref[...]
    total = (
        pool_ref[...]
        + jnp.where(row_lane < n2, packed, 0.0)
        + jnp.where(row_lane < n3, pltpu.roll(packed, clips - n2, 1), 0.0)
    )
    lengths = jnp.dot(
        jnp.broadcast_to(counts, (16, clips)).astype(BF), order, preferred_element_type=F32
    )[0:1]
    pooled = (total / (lengths * SPOTS)).astype(BF)
    n_dp, per_peer = out_ref.shape[0], out_ref.shape[1]
    slot = (line % per_peer) * n_dp + line // per_peer
    pick = one_hot(jnp.broadcast_to(send_ref[...], (clips, clips)) == slot)
    pick = lax.dot_general(pick, order, (((1,), (0,)), ((), ())), preferred_element_type=F32).astype(BF)
    rows = lax.dot_general(pick, pooled, (((1,), (1,)), ((), ())), preferred_element_type=F32)
    out_ref[:, :, :channels] = rows.astype(BF).reshape(n_dp, per_peer, channels)
    out_ref[:, :, channels:] = jnp.zeros((n_dp, per_peer, out_ref.shape[2] - channels), BF)
    late[1].wait()


def embed(
    clip_data, frame_counts, send_list, expand_weight, depth_kernel, reduce_weight, head_weight, centroids, n_dp
):
    clips, frames, spots, channels = clip_data.shape
    expanded = expand_weight.shape[2]
    dims = head_weight.shape[1]
    stored = pl.BlockSpec(memory_space=pltpu.HBM)
    local_ref = pl.BlockSpec(memory_space=pltpu.VMEM)
    return pl.pallas_call(
        embed_kernel,
        out_shape=(
            jax.ShapeDtypeStruct((n_dp, clips // n_dp, 256), BF),
            pltpu.VMEM(centroids.shape, BF),
            pltpu.VMEM(head_weight.shape, BF),
            pltpu.VMEM((dims, channels), BF),
        ),
        in_specs=[stored] * 4 + [local_ref] + [stored] * 3,
        out_specs=(local_ref,) * 4,
        scratch_shapes=[pltpu.VMEM((spots, channels, clips), BF)] * 6
        + [pltpu.VMEM((spots, expanded, clips), F32)] * 4
        + [pltpu.VMEM((spots, expanded, clips), BF)] * 3
        + [pltpu.VMEM((channels, clips), F32)] * 2
        + [pltpu.VMEM((expanded // 16, 27, 16, clips), F32)] * 2
        + [pltpu.VMEM((2, expanded, channels), BF), pltpu.VMEM((2, expanded, clips), F32)]
        + [pltpu.VMEM((frames, spots, channels, clips), BF), pltpu.SemaphoreType.DMA((frames,))]
        + [pltpu.VMEM((1, clips), jnp.int32)] * 2
        + [
            pltpu.VMEM((2, channels, expanded), BF),
            pltpu.VMEM((2, channels, expanded), BF),
            pltpu.SemaphoreType.DMA((6,)),
        ],
        compiler_params=pltpu.CompilerParams(vmem_limit_bytes=48 << 20),
        name="embed",
    )(
        jnp.transpose(clip_data, (1, 2, 3, 0)),
        frame_counts,
        send_list,
        expand_weight,
        depth_kernel,
        jnp.swapaxes(reduce_weight, 1, 2),
        head_weight,
        centroids,
    )


def unit(projected, axis):
    square = jnp.sum(projected * projected, axis=axis, keepdims=True)
    return (projected * lax.rsqrt(square + 1e-06)).astype(BF)


LABEL_ROWS = 16


def own_kernel(arrived_ref, ids_ref, payload_ref, rows_ref):
    n_dp, per_peer, width = arrived_ref.shape
    clips = n_dp * per_peer
    channels = rows_ref.shape[1]
    arrived = arrived_ref[...].reshape(clips, width)[:, :channels]
    row = lax.broadcasted_iota(jnp.int32, (clips, clips), 0)
    lane = lax.broadcasted_iota(jnp.int32, (clips, clips), 1)
    pick = (lane == (row % n_dp) * per_peer + row // n_dp).astype(F32).astype(BF)
    rows = jnp.dot(pick, arrived, preferred_element_type=F32)
    rows_ref[...] = rows.astype(BF)
    ids = ids_ref[...]
    which = lax.broadcasted_iota(jnp.int32, (LABEL_ROWS, clips), 0)
    high, low = ids // 256, ids % 256
    label = jnp.where(which == 0, high, jnp.where(which == 1, low, 0))
    payload = jnp.concatenate([jnp.transpose(rows), label.astype(F32)], axis=0).astype(BF)
    payload_ref[...] = payload


def own(arrived, cluster_ids, channels):
    n_dp, per_peer, width = arrived.shape
    clips = n_dp * per_peer
    height = channels + LABEL_ROWS
    return pl.pallas_call(
        own_kernel,
        out_shape=(
            jax.ShapeDtypeStruct((height, clips), BF),
            jax.ShapeDtypeStruct((clips, channels), BF),
        ),
        in_specs=[pl.BlockSpec(memory_space=pltpu.VMEM)] * 2,
        out_specs=(pl.BlockSpec(memory_space=pltpu.VMEM),) * 2,
        compiler_params=pltpu.CompilerParams(vmem_limit_bytes=8 << 20),
        name="own",
    )(arrived, cluster_ids)


def vectors_kernel(rows_ref, head_ref, vectors_ref):
    projected = jnp.dot(rows_ref[...], head_ref[...], preferred_element_type=F32)
    vectors_ref[...] = unit(projected, 1)


def vectors_of(rows, head_weight):
    clips, channels = rows.shape
    dims = head_weight.shape[1]
    return pl.pallas_call(
        vectors_kernel,
        out_shape=jax.ShapeDtypeStruct((clips, dims), BF),
        in_specs=[pl.BlockSpec(memory_space=pltpu.VMEM)] * 2,
        out_specs=pl.BlockSpec(memory_space=pltpu.VMEM),
        compiler_params=pltpu.CompilerParams(vmem_limit_bytes=8 << 20),
        cost_estimate=pl.CostEstimate(
            flops=2 * clips * dims * channels, bytes_accessed=2 * dims * (clips + channels), transcendentals=0
        ),
        name="vectors",
    )(rows, head_weight)


PANEL_ROWS = 784
OCCUR = 64


def label_of(rows_ref, block, channels):
    label = jnp.concatenate(
        [rows_ref[2 * block, channels:, :], rows_ref[2 * block + 1, channels:, :]], axis=1
    ).astype(F32)
    return label[0:1] * 256.0 + label[1:2]


def score_rows(rows_ref, flip_ref, panel_ref, turned_ref, near_ref, own_ref, best_ref, send_turned, arrive):
    blocks, height, clips = rows_ref.shape
    channels = flip_ref.shape[1]
    panel_rows = panel_ref.shape[0]
    base = lax.axis_index("cent") * panel_rows

    @pl.loop(0, blocks // 2)
    def _(pair):
        both = jnp.concatenate([rows_ref[2 * pair], rows_ref[2 * pair + 1]], axis=1)
        projected = jnp.dot(flip_ref[...], both[:channels], preferred_element_type=F32)
        turned_ref[pair] = unit(projected, 0)
        best_ref[pair] = jnp.full((8, 2 * clips), -jnp.inf, F32)

    send_turned()
    full = panel_rows // PANEL_ROWS
    left = panel_rows - full * PANEL_ROWS
    whole = left // 8 * 8
    for step in range(full):
        arrive(step)
        rows = slice(step * PANEL_ROWS, (step + 1) * PANEL_ROWS)

        @pl.loop(0, blocks // 2)
        def _(pair):
            scores = jnp.dot(panel_ref[rows, :], turned_ref[pair], preferred_element_type=F32)
            best_ref[pair] = jnp.maximum(
                best_ref[pair], jnp.max(scores.reshape(PANEL_ROWS // 8, 8, 2 * clips), axis=0)
            )
            if step == 0:
                local_id = label_of(rows_ref, pair, channels).astype(jnp.int32) - base
                index = lax.broadcasted_iota(jnp.int32, (OCCUR, 2 * clips), 0)
                own_ref[pair] = jnp.max(
                    jnp.where(index == local_id, scores[:OCCUR], -jnp.inf), axis=0, keepdims=True
                )

    arrive(full)

    @pl.loop(0, blocks // 2)
    def _(pair):
        scores = jnp.dot(
            panel_ref[full * PANEL_ROWS : panel_rows, :], turned_ref[pair], preferred_element_type=F32
        )
        best = jnp.maximum(
            best_ref[pair], jnp.max(scores[:whole].reshape(whole // 8, 8, 2 * clips), axis=0)
        )
        near_ref[pair] = jnp.maximum(
            jnp.max(best, axis=0, keepdims=True), jnp.max(scores[whole:], axis=0, keepdims=True)
        )


def near_kernel(
    rows_ref, flip_ref, panel_ref, turned_hbm, near_ref, own_ref, spread_ref, turned_ref, best_ref, done
):
    for peer in range(spread_ref.shape[0]):
        spread_ref[peer] = rows_ref[0]
    copy = pltpu.make_async_copy(turned_ref, turned_hbm, done)
    score_rows(
        rows_ref, flip_ref, panel_ref, turned_ref, near_ref, own_ref, best_ref, copy.start, lambda step: None
    )
    copy.wait()


def far_kernel(
    rows_ref, flip_ref, stored_ref, turned_hbm, near_ref, own_ref, turned_ref, best_ref, done, panel_ref, arrival
):
    panel_copy = pltpu.make_async_copy(stored_ref, panel_ref, arrival)
    panel_copy.start()
    copy = pltpu.make_async_copy(turned_ref, turned_hbm, done)

    def arrive(step):
        if step == 0:
            panel_copy.wait()

    score_rows(rows_ref, flip_ref, panel_ref, turned_ref, near_ref, own_ref, best_ref, copy.start, arrive)
    copy.wait()


def scored(kernel, name, rows, flip, panel, limit, spread=None):
    blocks, height, clips = rows.shape
    dims, channels = flip.shape
    pairs, width = blocks // 2, 2 * clips
    panel_rows = panel.shape[0]
    here = pl.BlockSpec(memory_space=pltpu.VMEM)
    stored = pl.BlockSpec(memory_space=pltpu.HBM)
    shapes = [
        pltpu.HBM((pairs, dims, width), BF),
        jax.ShapeDtypeStruct((pairs, 1, width), F32),
        jax.ShapeDtypeStruct((pairs, 1, width), F32),
    ]
    scratch = [
        pltpu.VMEM((pairs, dims, width), BF),
        pltpu.VMEM((pairs, 8, width), F32),
        pltpu.SemaphoreType.DMA(()),
    ]
    if spread is None:
        scratch += [pltpu.VMEM(panel.shape, BF), pltpu.SemaphoreType.DMA(())]
    else:
        shapes.append(jax.ShapeDtypeStruct((spread, height, clips), BF))
    return pl.pallas_call(
        kernel,
        out_shape=shapes,
        in_specs=[here, here, stored if spread is None else here],
        out_specs=[stored] + [here] * (len(shapes) - 1),
        scratch_shapes=scratch,
        compiler_params=pltpu.CompilerParams(vmem_limit_bytes=limit << 20),
        cost_estimate=pl.CostEstimate(
            flops=2 * blocks * clips * panel_rows * dims, bytes_accessed=2 * panel_rows * dims, transcendentals=0
        ),
        name=name,
    )(rows, flip, panel)


GROUP = 4


def peer_kernel(
    near_rows_ref, near_turned_hbm, near_best_ref, near_own_ref, far_rows_ref, far_turned_hbm, far_best_ref, far_own_ref,
    cols_ref, head_ref, out_ref, near_turned_ref, far_turned_ref, best_ref, arrival,
):
    copies = [
        pltpu.make_async_copy(near_turned_hbm, near_turned_ref, arrival.at[0]),
        pltpu.make_async_copy(far_turned_hbm, far_turned_ref, arrival.at[1]),
    ]
    for copy in copies:
        copy.start()
    n_dp, height, clips = cols_ref.shape
    n_cent = out_ref.shape[0]
    channels = head_ref.shape[0]
    eye = identity(clips)
    best_ref[...] = jnp.full_like(best_ref, -1.0)
    mine_dp, mine_cent = lax.axis_index("dp"), lax.axis_index("cent")
    for copy in copies:
        copy.wait()

    @pl.loop(0, n_dp // GROUP)
    def _(group):
        flipped = jnp.concatenate([turn(eye, cols_ref[group * GROUP + at]) for at in range(GROUP)], axis=0)
        projected = jnp.dot(flipped[:, :channels].astype(BF), head_ref[...], preferred_element_type=F32)
        vectors = unit(projected, 1)
        ids = flipped[:, channels : channels + 1] * 256.0 + flipped[:, channels + 1 : channels + 2]
        wide = jnp.broadcast_to(ids, (GROUP * clips, 2 * clips))
        for block in range(n_cent // 2):
            cols = slice(block * 2 * clips, (block + 1) * 2 * clips)
            if block == 0:
                turned, row_ids = near_turned_ref[0], label_of(near_rows_ref, 0, channels)
            else:
                turned, row_ids = far_turned_ref[block - 1], label_of(far_rows_ref, block - 1, channels)
            scores = jnp.dot(vectors, turned, preferred_element_type=F32)
            same = wide == row_ids
            if block == 0:
                line = lax.broadcasted_iota(jnp.int32, same.shape, 0)
                lane = lax.broadcasted_iota(jnp.int32, same.shape, 1)
                itself = jnp.where(lane < clips, lane + (mine_dp - group * GROUP) * clips, -1)
                same = same & (line != itself)
            found = jnp.where(same, scores, -1.0)
            best_ref[:, cols] = jnp.maximum(
                best_ref[:, cols], jnp.max(found.reshape(GROUP * clips // 8, 8, 2 * clips), axis=0)
            )

    best = jnp.max(best_ref[...], axis=0, keepdims=True)
    for block in range(n_cent // 2):
        for side in range(2):
            chip = (mine_cent // 2 + block) % (n_cent // 2)
            cent = 2 * chip + (mine_cent + side) % 2
            at = slice((2 * block + side) * clips, (2 * block + side + 1) * clips)
            part = slice(side * clips, (side + 1) * clips)
            if block == 0:
                nearest, own_best = near_best_ref[0, :, part], near_own_ref[0, :, part]
            else:
                nearest, own_best = far_best_ref[block - 1, :, part], far_own_ref[block - 1, :, part]
            out_ref[cent, 0:1, :] = nearest
            out_ref[cent, 1:2, :] = own_best
            out_ref[cent, 2:3, :] = best[:, at]
            out_ref[cent, 3:4, :] = best[:, at]


def peers_of(near_rows, near_found, far_rows, far_found, cols, head_weight):
    n_dp, height, clips = cols.shape
    n_cent = near_rows.shape[0] + far_rows.shape[0]
    dims = head_weight.shape[1]
    here = pl.BlockSpec(memory_space=pltpu.VMEM)
    stored = pl.BlockSpec(memory_space=pltpu.HBM)
    near_found, far_found = [
        [pltpu.with_memory_space_constraint(found[0], pltpu.HBM), *found[1:]] for found in (near_found, far_found)
    ]
    return pl.pallas_call(
        peer_kernel,
        out_shape=jax.ShapeDtypeStruct((n_cent, 4, clips), F32),
        in_specs=[here, stored, here, here] * 2 + [here] * 2,
        out_specs=here,
        scratch_shapes=[
            pltpu.VMEM(near_found[0].shape, BF),
            pltpu.VMEM(far_found[0].shape, BF),
            pltpu.VMEM((8, n_cent * clips), F32),
            pltpu.SemaphoreType.DMA((2,)),
        ],
        compiler_params=pltpu.CompilerParams(vmem_limit_bytes=16 << 20),
        cost_estimate=pl.CostEstimate(
            flops=2 * n_dp * n_cent * clips * clips * dims, bytes_accessed=4 << 20, transcendentals=0
        ),
        name="peers",
    )(near_rows, *near_found, far_rows, *far_found, cols, head_weight)


def local(
    clip_data,
    frame_counts,
    send_list,
    cluster_ids,
    expand_weight,
    depth_kernel,
    reduce_weight,
    head_weight,
    centroids,
):
    n_dp = lax.axis_size("dp")
    n_cent = lax.axis_size("cent")
    pooled, panel, head, flip = embed(
        clip_data, frame_counts, send_list, expand_weight, depth_kernel, reduce_weight, head_weight, centroids, n_dp
    )
    arrived = lax.all_to_all(pooled, "dp", split_axis=0, concat_axis=0, tiled=True)
    payload, rows = own(arrived, cluster_ids, head_weight.shape[0])
    partner = lax.ppermute(payload, "cent", [(at, at ^ 1) for at in range(n_cent)])
    near_rows = jnp.stack([payload, partner])
    far_rows = jnp.concatenate(
        [
            lax.ppermute(near_rows, "cent", [((at + 2 * chip) % n_cent, at) for at in range(n_cent)])
            for chip in range(1, n_cent // 2)
        ]
    )
    *near_found, spread = scored(near_kernel, "near", near_rows, flip, panel, 16, n_dp)
    cols = lax.all_to_all(spread, "dp", split_axis=0, concat_axis=0, tiled=True)
    vectors = vectors_of(rows, head)
    far_found = scored(
        far_kernel, "far", far_rows, flip, pltpu.with_memory_space_constraint(centroids, pltpu.HBM), 32
    )
    partial = peers_of(near_rows, near_found, far_rows, far_found, cols, head)
    parts = lax.all_to_all(partial, "cent", split_axis=0, concat_axis=0, tiled=True)
    final = jnp.max(parts, axis=0)
    return (vectors, final[0], final[1], final[2])


def solution(mesh):
    placed = (
        P(("dp", "cent"), None, None, None),
        P(("dp", "cent"), None),
        P(("dp", "cent"), None),
        P(("dp", "cent"), None),
        P(),
        P(),
        P(),
        P(),
        P("cent", None),
    )
    return jax.shard_map(
        local,
        mesh=mesh,
        in_specs=placed,
        out_specs=(
            P(("dp", "cent"), None),
            P(("dp", "cent")),
            P(("dp", "cent")),
            P(("dp", "cent")),
        ),
        check_vma=False,
    )
```

```python
import functools

import jax
import jax.numpy as jnp
from jax import lax
from jax.experimental import pallas as pl
from jax.experimental.pallas import tpu as pltpu
from jax.sharding import PartitionSpec as P

SIDE = 4
SPOTS = SIDE * SIDE
BF = jnp.bfloat16
F32 = jnp.float32


def neighbours(at, extent):
    return [(at + shift - 1, shift) for shift in range(3) if 0 <= at + shift - 1 < extent]


STEPS = 9


def identity(size):
    line = lax.broadcasted_iota(jnp.int32, (size, size), 0)
    lane = lax.broadcasted_iota(jnp.int32, (size, size), 1)
    return (line == lane).astype(F32).astype(BF)


def turn(eye, matrix):
    return lax.dot_general(eye, matrix, (((1,), (1,)), ((), ())), preferred_element_type=F32)


def embed_kernel(
    stored_ref, counts_hbm, send_hbm, wide_hbm, taps_ref, reduce_hbm, head_hbm, panel_hbm,
    out_ref, panel_ref, head_ref, flip_ref, *scratch,
):
    x_refs, act_refs = scratch[0:6], scratch[10:13]
    hidden_refs = scratch[6:10] + scratch[6:8]
    pool_ref, packed_pool_ref = scratch[13:15]
    weight_refs = scratch[15:17]
    expand_ref, depth_ref, clip_ref, arrival = scratch[17:21]
    count_ref, send_ref, wide_ref, reduce_ref, ready = scratch[21:26]
    channels, clips = clip_ref.shape[2], clip_ref.shape[3]
    early = [
        pltpu.make_async_copy(source, target, ready.at[at])
        for at, (source, target) in enumerate(
            [(counts_hbm, count_ref), (send_hbm, send_ref), (wide_hbm, wide_ref), (reduce_hbm, reduce_ref)]
        )
    ]
    late = [
        pltpu.make_async_copy(source, target, ready.at[4 + at])
        for at, (source, target) in enumerate([(head_hbm, head_ref), (panel_hbm, panel_ref)])
    ]
    for copy in early:
        copy.start()
    copies = [
        pltpu.make_async_copy(stored_ref.at[frame], clip_ref.at[frame], arrival.at[frame])
        for frame in range(clip_ref.shape[0])
    ]
    for copy in copies:
        copy.start()
    for copy in early:
        copy.wait()
    expanded = wide_ref.shape[2]
    eye = identity(expanded)
    for layer in range(2):
        expand_ref[layer] = turn(eye, wide_ref[layer]).astype(BF)
        depth_ref[layer, :, : taps_ref.shape[1]] = turn(eye, taps_ref[layer])

    counts = count_ref[...].astype(F32)
    line = lax.broadcasted_iota(jnp.int32, (clips, clips), 0)
    lane = lax.broadcasted_iota(jnp.int32, (clips, clips), 1)
    count_lane = jnp.broadcast_to(counts, (clips, clips))
    count_line = jnp.transpose(count_lane)
    ahead = (count_lane > count_line) | ((count_lane == count_line) & (lane < line))
    rank = jnp.dot(
        ahead.astype(F32).astype(BF), jnp.ones((clips, clips), BF), preferred_element_type=F32
    ).astype(jnp.int32)
    n1, n2, n3 = [jnp.sum((counts > frame).astype(jnp.int32)) for frame in (1, 2, 3)]
    blocks = expanded // 16 // STEPS
    one_hot = lambda mask: mask.astype(F32).astype(BF)
    order = one_hot(rank == lane)
    place = [
        order,
        one_hot((rank == lane) & (count_line > 1)),
        jnp.concatenate(
            [
                one_hot((rank == lane) & (count_line > 2)),
                one_hot((rank + n2 == lane) & (count_line > 3)),
            ],
            axis=0,
        ),
    ]
    row_lane = lax.broadcasted_iota(jnp.int32, (1, clips), 1)
    kept = [None, (row_lane < n1).astype(F32), (row_lane < n2 + n3).astype(F32)]
    tile_lane = lax.broadcasted_iota(jnp.int32, (16, clips), 1)
    in_second, in_third = tile_lane < n2, tile_lane < n3

    def expand(layer, tile, pair, both):
        hidden = jnp.maximum(jnp.dot(expand_ref[layer], both, preferred_element_type=F32), 0.0)
        hidden_refs[3 * layer + tile][2 * pair] = hidden[:, :clips]
        hidden_refs[3 * layer + tile][2 * pair + 1] = hidden[:, clips:]

    def gather(tile, pair):
        if tile < 2:
            spots = jnp.concatenate([clip_ref[tile, 2 * pair], clip_ref[tile, 2 * pair + 1]], axis=0)
        else:
            spots = jnp.concatenate(
                [
                    jnp.concatenate([clip_ref[2, 2 * pair + side], clip_ref[3, 2 * pair + side]], axis=1)
                    for side in range(2)
                ],
                axis=0,
            )
        x = jnp.dot(spots, place[tile], preferred_element_type=F32).astype(BF)
        x_refs[tile][2 * pair] = x[:channels]
        x_refs[tile][2 * pair + 1] = x[channels:]

    def expand_stored(layer, tile, pair):
        x_ref = x_refs[3 * layer + tile]
        expand(layer, tile, pair, jnp.concatenate([x_ref[2 * pair], x_ref[2 * pair + 1]], axis=1))

    def spread_taps(layer, step, first, last):
        rows = [pl.ds(pl.multiple_of((step * blocks + at) * 16, 16), 16) for at in range(blocks)]
        taps = [depth_ref[layer, row, :] for row in rows]
        for tap in range(first, last):
            for at in range(blocks):
                weight_refs[layer][step * blocks + at, tap] = jnp.broadcast_to(
                    taps[at][:, tap : tap + 1], (16, clips)
                )

    def reduce(layer, tile, pair):
        both = jnp.concatenate([act_refs[tile][2 * pair], act_refs[tile][2 * pair + 1]], axis=1)
        branch = jnp.dot(reduce_ref[layer], both, preferred_element_type=F32)
        result = []
        for side in range(2):
            part = branch[:, side * clips : (side + 1) * clips]
            if kept[tile] is not None:
                part = part * kept[tile]
            x = x_refs[3 * layer + tile][2 * pair + side].astype(F32) + part
            result.append(x.astype(BF))
        return result

    def reduce_store(tile, pair):
        x = reduce(0, tile, pair)
        x_refs[3 + tile][2 * pair] = x[0]
        x_refs[3 + tile][2 * pair + 1] = x[1]

    def reduce_pool(tile, pair, live):
        x = reduce(1, tile, pair)
        into = packed_pool_ref if tile == 2 else pool_ref
        into[...] += (x[0].astype(F32) + x[1].astype(F32)) * live

    def depthwise(layer, tile, block):
        rows = pl.ds(pl.multiple_of(block * 16, 16), 16)
        read = lambda source, spot: hidden_refs[3 * layer + source][spot, rows, :]
        if tile == 0:
            sources = [(1, lambda s: read(0, s)), (2, lambda s: read(1, s))]
        elif tile == 1:
            sources = [
                (0, lambda s: read(0, s)),
                (1, lambda s: read(1, s)),
                (2, lambda s: jnp.where(in_second, read(2, s), 0.0)),
            ]
        else:
            sources = [
                (0, lambda s: jnp.where(in_second, read(1, s), pltpu.roll(read(2, s), n2, 1))),
                (1, lambda s: read(2, s)),
                (2, lambda s: jnp.where(in_third, pltpu.roll(read(2, s), clips - n2, 1), 0.0)),
            ]
        mixed = [None] * SPOTS
        for shift_t, source in sources:
            weight = [weight_refs[layer][block, 9 * shift_t + tap].astype(BF) for tap in range(9)]
            hidden = [source(spot).astype(BF) for spot in range(SPOTS)]
            for y in range(SIDE):
                for from_y, shift_y in neighbours(y, SIDE):
                    for z in range(SIDE):
                        for from_z, shift_z in neighbours(z, SIDE):
                            term = hidden[from_y * SIDE + from_z] * weight[3 * shift_y + shift_z]
                            spot = y * SIDE + z
                            mixed[spot] = term if mixed[spot] is None else mixed[spot] + term
        for spot in range(SPOTS):
            half = mixed[spot] * BF(0.5)
            act_refs[tile][spot, rows, :] = half + half * jnp.tanh(half)

    def stage(layer, tile, other):
        @pl.loop(0, STEPS)
        def _(step):
            pair = jnp.minimum(step, SPOTS // 2 - 1)
            before = jnp.maximum(step - 1, 0)
            other(pair, before, (step < SPOTS // 2).astype(F32))
            if layer == 0:
                if tile == 0:
                    spread_taps(0, step, 0, 9)
                spread_taps(1, step, 9 * tile, 9 * tile + 9)
            for at in range(blocks):
                depthwise(layer, tile, step * blocks + at)

    def filler(first, second):
        def other(pair, before, live):
            second(before)
            first(pair)

        return other

    pool_ref[...] = jnp.zeros_like(pool_ref)
    packed_pool_ref[...] = jnp.zeros_like(packed_pool_ref)
    copies[0].wait()
    copies[1].wait()

    @pl.loop(0, STEPS)
    def _(step):
        pair = jnp.minimum(step, SPOTS // 2 - 1)
        before = jnp.maximum(step - 1, 0)
        for tile in range(2):
            expand_stored(0, tile, before)
            gather(tile, pair)
        spread_taps(0, step, 9, 27)

    copies[2].wait()
    copies[3].wait()
    for copy in late:
        copy.start()
    stage(0, 0, filler(lambda pair: gather(2, pair), lambda pair: expand_stored(0, 2, pair)))
    stage(0, 1, filler(lambda pair: reduce_store(0, pair), lambda pair: expand_stored(1, 0, pair)))
    stage(0, 2, filler(lambda pair: reduce_store(1, pair), lambda pair: expand_stored(1, 1, pair)))
    stage(1, 0, filler(lambda pair: reduce_store(2, pair), lambda pair: expand_stored(1, 2, pair)))
    stage(1, 1, lambda pair, before, live: reduce_pool(0, pair, live))
    stage(1, 2, lambda pair, before, live: reduce_pool(1, pair, live))

    @pl.loop(0, SPOTS // 2)
    def _(pair):
        reduce_pool(2, pair, 1.0)

    late[0].wait()
    small = identity(256)
    for part in range(flip_ref.shape[0] // 256):
        part = slice(part * 256, (part + 1) * 256)
        flip_ref[part, :] = turn(small, head_ref[:, part]).astype(BF)
    packed = packed_pool_ref[...]
    total = (
        pool_ref[...]
        + jnp.where(row_lane < n2, packed, 0.0)
        + jnp.where(row_lane < n3, pltpu.roll(packed, clips - n2, 1), 0.0)
    )
    lengths = jnp.dot(
        jnp.broadcast_to(counts, (16, clips)).astype(BF), order, preferred_element_type=F32
    )[0:1]
    pooled = (total / (lengths * SPOTS)).astype(BF)
    n_dp, per_peer = out_ref.shape[0], out_ref.shape[1]
    slot = (line % per_peer) * n_dp + line // per_peer
    pick = one_hot(jnp.broadcast_to(send_ref[...], (clips, clips)) == slot)
    pick = lax.dot_general(pick, order, (((1,), (0,)), ((), ())), preferred_element_type=F32).astype(BF)
    rows = lax.dot_general(pick, pooled, (((1,), (1,)), ((), ())), preferred_element_type=F32)
    out_ref[:, :, :channels] = rows.astype(BF).reshape(n_dp, per_peer, channels)
    out_ref[:, :, channels:] = jnp.zeros((n_dp, per_peer, out_ref.shape[2] - channels), BF)
    late[1].wait()


def embed(
    clip_data, frame_counts, send_list, expand_weight, depth_kernel, reduce_weight, head_weight, centroids, n_dp
):
    clips, frames, spots, channels = clip_data.shape
    expanded = expand_weight.shape[2]
    dims = head_weight.shape[1]
    stored = pl.BlockSpec(memory_space=pltpu.HBM)
    local_ref = pl.BlockSpec(memory_space=pltpu.VMEM)
    return pl.pallas_call(
        embed_kernel,
        out_shape=(
            jax.ShapeDtypeStruct((n_dp, clips // n_dp, 256), BF),
            pltpu.VMEM(centroids.shape, BF),
            pltpu.VMEM(head_weight.shape, BF),
            pltpu.VMEM((dims, channels), BF),
        ),
        in_specs=[stored] * 4 + [local_ref] + [stored] * 3,
        out_specs=(local_ref,) * 4,
        scratch_shapes=[pltpu.VMEM((spots, channels, clips), BF)] * 6
        + [pltpu.VMEM((spots, expanded, clips), F32)] * 4
        + [pltpu.VMEM((spots, expanded, clips), BF)] * 3
        + [pltpu.VMEM((channels, clips), F32)] * 2
        + [pltpu.VMEM((expanded // 16, 27, 16, clips), F32)] * 2
        + [pltpu.VMEM((2, expanded, channels), BF), pltpu.VMEM((2, expanded, clips), F32)]
        + [pltpu.VMEM((frames, spots, channels, clips), BF), pltpu.SemaphoreType.DMA((frames,))]
        + [pltpu.VMEM((1, clips), jnp.int32)] * 2
        + [
            pltpu.VMEM((2, channels, expanded), BF),
            pltpu.VMEM((2, channels, expanded), BF),
            pltpu.SemaphoreType.DMA((6,)),
        ],
        compiler_params=pltpu.CompilerParams(vmem_limit_bytes=48 << 20),
        name="embed",
    )(
        jnp.transpose(clip_data, (1, 2, 3, 0)),
        frame_counts,
        send_list,
        expand_weight,
        depth_kernel,
        jnp.swapaxes(reduce_weight, 1, 2),
        head_weight,
        centroids,
    )


def unit(projected, axis):
    square = jnp.sum(projected * projected, axis=axis, keepdims=True)
    return (projected * lax.rsqrt(square + 1e-06)).astype(BF)


LABEL_ROWS = 16


def own_kernel(arrived_ref, ids_ref, payload_ref, rows_ref):
    n_dp, per_peer, width = arrived_ref.shape
    clips = n_dp * per_peer
    channels = rows_ref.shape[1]
    arrived = arrived_ref[...].reshape(clips, width)[:, :channels]
    row = lax.broadcasted_iota(jnp.int32, (clips, clips), 0)
    lane = lax.broadcasted_iota(jnp.int32, (clips, clips), 1)
    pick = (lane == (row % n_dp) * per_peer + row // n_dp).astype(F32).astype(BF)
    rows = jnp.dot(pick, arrived, preferred_element_type=F32)
    rows_ref[...] = rows.astype(BF)
    ids = ids_ref[...]
    which = lax.broadcasted_iota(jnp.int32, (LABEL_ROWS, clips), 0)
    high, low = ids // 256, ids % 256
    label = jnp.where(which == 0, high, jnp.where(which == 1, low, 0))
    payload = jnp.concatenate([jnp.transpose(rows), label.astype(F32)], axis=0).astype(BF)
    payload_ref[...] = payload


def own(arrived, cluster_ids, channels):
    n_dp, per_peer, width = arrived.shape
    clips = n_dp * per_peer
    height = channels + LABEL_ROWS
    return pl.pallas_call(
        own_kernel,
        out_shape=(
            jax.ShapeDtypeStruct((height, clips), BF),
            jax.ShapeDtypeStruct((clips, channels), BF),
        ),
        in_specs=[pl.BlockSpec(memory_space=pltpu.VMEM)] * 2,
        out_specs=(pl.BlockSpec(memory_space=pltpu.VMEM),) * 2,
        compiler_params=pltpu.CompilerParams(vmem_limit_bytes=8 << 20),
        name="own",
    )(arrived, cluster_ids)


def vectors_kernel(rows_ref, head_ref, vectors_ref):
    projected = jnp.dot(rows_ref[...], head_ref[...], preferred_element_type=F32)
    vectors_ref[...] = unit(projected, 1)


def vectors_of(rows, head_weight):
    clips, channels = rows.shape
    dims = head_weight.shape[1]
    return pl.pallas_call(
        vectors_kernel,
        out_shape=jax.ShapeDtypeStruct((clips, dims), BF),
        in_specs=[pl.BlockSpec(memory_space=pltpu.VMEM)] * 2,
        out_specs=pl.BlockSpec(memory_space=pltpu.VMEM),
        compiler_params=pltpu.CompilerParams(vmem_limit_bytes=8 << 20),
        cost_estimate=pl.CostEstimate(
            flops=2 * clips * dims * channels, bytes_accessed=2 * dims * (clips + channels), transcendentals=0
        ),
        name="vectors",
    )(rows, head_weight)


PANEL_ROWS = 784
OCCUR = 64
LEFT = 2


def label_of(rows_ref, block, channels):
    label = jnp.concatenate(
        [rows_ref[2 * block, channels:, :], rows_ref[2 * block + 1, channels:, :]], axis=1
    ).astype(F32)
    return label[0:1] * 256.0 + label[1:2]


def score_rows(rows_ref, flip_ref, panel_ref, turned_ref, near_ref, own_ref, best_ref, send_turned, arrive, extra):
    blocks, height, clips = rows_ref.shape
    channels = flip_ref.shape[1]
    panel_rows = panel_ref.shape[0] // 8 * 8

    @pl.loop(0, blocks // 2)
    def _(pair):
        both = jnp.concatenate([rows_ref[2 * pair], rows_ref[2 * pair + 1]], axis=1)
        projected = jnp.dot(flip_ref[...], both[:channels], preferred_element_type=F32)
        turned_ref[pair] = unit(projected, 0)
        best_ref[pair] = jnp.dot(extra, turned_ref[pair], preferred_element_type=F32)

    send_turned()
    base = lax.axis_index("cent") * (panel_rows + LEFT)
    for step in range(pl.cdiv(panel_rows, PANEL_ROWS)):
        arrive(step)
        rows = slice(step * PANEL_ROWS, min(panel_rows, (step + 1) * PANEL_ROWS))

        @pl.loop(0, blocks // 2)
        def _(pair):
            scores = jnp.dot(panel_ref[rows, :], turned_ref[pair], preferred_element_type=F32)
            best_ref[pair] = jnp.maximum(
                best_ref[pair], jnp.max(scores.reshape((rows.stop - rows.start) // 8, 8, 2 * clips), axis=0)
            )
            if step == 0:
                local_id = label_of(rows_ref, pair, channels).astype(jnp.int32) - base
                index = lax.broadcasted_iota(jnp.int32, (OCCUR, 2 * clips), 0)
                own_ref[pair] = jnp.max(
                    jnp.where(index == local_id, scores[:OCCUR], -jnp.inf), axis=0, keepdims=True
                )

    for pair in range(blocks // 2):
        near_ref[pair] = jnp.max(best_ref[pair], axis=0, keepdims=True)


def near_kernel(
    rows_ref, flip_ref, panel_ref, turned_hbm, near_ref, own_ref, spread_ref, extra_ref, turned_ref, best_ref, done
):
    for peer in range(spread_ref.shape[0]):
        spread_ref[peer] = rows_ref[0]
    panel_rows = panel_ref.shape[0]
    left = panel_ref[panel_rows - LEFT : panel_rows, :]
    extra = jnp.concatenate([left] * (8 // LEFT), axis=0)
    extra_ref[...] = extra
    copy = pltpu.make_async_copy(turned_ref, turned_hbm, done)
    score_rows(
        rows_ref, flip_ref, panel_ref, turned_ref, near_ref, own_ref, best_ref, copy.start, lambda step: None, extra
    )
    copy.wait()


def far_kernel(
    rows_ref, flip_ref, stored_ref, extra_ref, turned_hbm, near_ref, own_ref, turned_ref, best_ref, done, panel_ref, arrival
):
    copies = []
    for step in range(arrival.shape[0]):
        rows = slice(step * PANEL_ROWS, min(panel_ref.shape[0], (step + 1) * PANEL_ROWS))
        copies.append(pltpu.make_async_copy(stored_ref.at[rows], panel_ref.at[rows], arrival.at[step]))
        copies[-1].start()
    copy = pltpu.make_async_copy(turned_ref, turned_hbm, done)
    score_rows(
        rows_ref, flip_ref, panel_ref, turned_ref, near_ref, own_ref, best_ref,
        copy.start, lambda step: copies[step].wait(), extra_ref[...],
    )
    copy.wait()


def scored(kernel, name, rows, flip, panel, limit, spread=None, extra=None):
    blocks, height, clips = rows.shape
    dims, channels = flip.shape
    pairs, width = blocks // 2, 2 * clips
    panel_rows = panel.shape[0]
    here = pl.BlockSpec(memory_space=pltpu.VMEM)
    stored = pl.BlockSpec(memory_space=pltpu.HBM)
    shapes = [
        pltpu.HBM((pairs, dims, width), BF),
        jax.ShapeDtypeStruct((pairs, 1, width), F32),
        jax.ShapeDtypeStruct((pairs, 1, width), F32),
    ]
    scratch = [
        pltpu.VMEM((pairs, dims, width), BF),
        pltpu.VMEM((pairs, 8, width), F32),
        pltpu.SemaphoreType.DMA(()),
    ]
    if spread is None:
        even = panel_rows // 8 * 8
        scratch += [
            pltpu.VMEM((even, dims), BF), pltpu.SemaphoreType.DMA((pl.cdiv(even, PANEL_ROWS),))
        ]
    else:
        assert panel_rows % 8 == LEFT
        shapes.append(jax.ShapeDtypeStruct((spread, height, clips), BF))
        shapes.append(jax.ShapeDtypeStruct((8, dims), BF))
    return pl.pallas_call(
        kernel,
        out_shape=shapes,
        in_specs=[here, here] + ([stored, here] if spread is None else [here]),
        out_specs=[stored] + [here] * (len(shapes) - 1),
        scratch_shapes=scratch,
        compiler_params=pltpu.CompilerParams(vmem_limit_bytes=limit << 20),
        cost_estimate=pl.CostEstimate(
            flops=2 * blocks * clips * panel_rows * dims, bytes_accessed=2 * panel_rows * dims, transcendentals=0
        ),
        name=name,
    )(rows, flip, panel, *([extra] if spread is None else []))


GROUP = 4


def peer_kernel(
    near_rows_ref, near_turned_hbm, near_best_ref, near_own_ref, far_rows_ref, far_turned_hbm, far_best_ref, far_own_ref,
    cols_ref, head_ref, out_ref, near_turned_ref, far_turned_ref, best_ref, arrival,
):
    copies = [
        pltpu.make_async_copy(near_turned_hbm, near_turned_ref, arrival.at[0]),
        pltpu.make_async_copy(far_turned_hbm, far_turned_ref, arrival.at[1]),
    ]
    for copy in copies:
        copy.start()
    n_dp, height, clips = cols_ref.shape
    n_cent = out_ref.shape[0]
    channels = head_ref.shape[0]
    eye = identity(clips)
    best_ref[...] = jnp.full_like(best_ref, -1.0)
    mine_dp, mine_cent = lax.axis_index("dp"), lax.axis_index("cent")

    @pl.loop(0, n_dp // GROUP)
    def _(group):
        flipped = jnp.concatenate([turn(eye, cols_ref[group * GROUP + at]) for at in range(GROUP)], axis=0)
        projected = jnp.dot(flipped[:, :channels].astype(BF), head_ref[...], preferred_element_type=F32)
        vectors = unit(projected, 1)
        ids = flipped[:, channels : channels + 1] * 256.0 + flipped[:, channels + 1 : channels + 2]
        wide = jnp.broadcast_to(ids, (GROUP * clips, 2 * clips))
        for block in range(n_cent // 2):
            cols = slice(block * 2 * clips, (block + 1) * 2 * clips)
            if block < 2:
                pl.when(group == 0)(copies[block].wait)
            if block == 0:
                turned, row_ids = near_turned_ref[0], label_of(near_rows_ref, 0, channels)
            else:
                turned, row_ids = far_turned_ref[block - 1], label_of(far_rows_ref, block - 1, channels)
            scores = jnp.dot(vectors, turned, preferred_element_type=F32)
            same = wide == row_ids
            if block == 0:
                line = lax.broadcasted_iota(jnp.int32, same.shape, 0)
                lane = lax.broadcasted_iota(jnp.int32, same.shape, 1)
                itself = jnp.where(lane < clips, lane + (mine_dp - group * GROUP) * clips, -1)
                same = same & (line != itself)
            found = jnp.where(same, scores, -1.0)
            best_ref[:, cols] = jnp.maximum(
                best_ref[:, cols], jnp.max(found.reshape(GROUP * clips // 8, 8, 2 * clips), axis=0)
            )

    best = jnp.max(best_ref[...], axis=0, keepdims=True)
    for block in range(n_cent // 2):
        for side in range(2):
            chip = (mine_cent // 2 + block) % (n_cent // 2)
            cent = 2 * chip + (mine_cent + side) % 2
            at = slice((2 * block + side) * clips, (2 * block + side + 1) * clips)
            part = slice(side * clips, (side + 1) * clips)
            if block == 0:
                nearest, own_best = near_best_ref[0, :, part], near_own_ref[0, :, part]
            else:
                nearest, own_best = far_best_ref[block - 1, :, part], far_own_ref[block - 1, :, part]
            out_ref[cent, 0:1, :] = nearest
            out_ref[cent, 1:2, :] = own_best
            out_ref[cent, 2:3, :] = best[:, at]
            out_ref[cent, 3:4, :] = best[:, at]


def peers_of(near_rows, near_found, far_rows, far_found, cols, head_weight):
    n_dp, height, clips = cols.shape
    n_cent = near_rows.shape[0] + far_rows.shape[0]
    dims = head_weight.shape[1]
    here = pl.BlockSpec(memory_space=pltpu.VMEM)
    stored = pl.BlockSpec(memory_space=pltpu.HBM)
    near_found, far_found = [
        [pltpu.with_memory_space_constraint(found[0], pltpu.HBM), *found[1:]] for found in (near_found, far_found)
    ]
    return pl.pallas_call(
        peer_kernel,
        out_shape=jax.ShapeDtypeStruct((n_cent, 4, clips), F32),
        in_specs=[here, stored, here, here] * 2 + [here] * 2,
        out_specs=here,
        scratch_shapes=[
            pltpu.VMEM(near_found[0].shape, BF),
            pltpu.VMEM(far_found[0].shape, BF),
            pltpu.VMEM((8, n_cent * clips), F32),
            pltpu.SemaphoreType.DMA((2,)),
        ],
        compiler_params=pltpu.CompilerParams(vmem_limit_bytes=16 << 20),
        cost_estimate=pl.CostEstimate(
            flops=2 * n_dp * n_cent * clips * clips * dims, bytes_accessed=4 << 20, transcendentals=0
        ),
        name="peers",
    )(near_rows, *near_found, far_rows, *far_found, cols, head_weight)


def local(
    clip_data,
    frame_counts,
    send_list,
    cluster_ids,
    expand_weight,
    depth_kernel,
    reduce_weight,
    head_weight,
    centroids,
):
    n_dp = lax.axis_size("dp")
    n_cent = lax.axis_size("cent")
    pooled, panel, head, flip = embed(
        clip_data, frame_counts, send_list, expand_weight, depth_kernel, reduce_weight, head_weight, centroids, n_dp
    )
    arrived = lax.all_to_all(pooled, "dp", split_axis=0, concat_axis=0, tiled=True)
    payload, rows = own(arrived, cluster_ids, head_weight.shape[0])
    partner = lax.ppermute(payload, "cent", [(at, at ^ 1) for at in range(n_cent)])
    near_rows = jnp.stack([payload, partner])
    far_rows = jnp.concatenate(
        [
            lax.ppermute(near_rows, "cent", [((at + 2 * chip) % n_cent, at) for at in range(n_cent)])
            for chip in range(1, n_cent // 2)
        ]
    )
    *near_found, spread, extra = scored(near_kernel, "near", near_rows, flip, panel, 16, n_dp)
    cols = lax.all_to_all(spread, "dp", split_axis=0, concat_axis=0, tiled=True)
    vectors = vectors_of(rows, head)
    far_found = scored(
        far_kernel, "far", far_rows, flip, pltpu.with_memory_space_constraint(centroids, pltpu.HBM), 32, extra=extra
    )
    partial = peers_of(near_rows, near_found, far_rows, far_found, cols, head)
    parts = lax.all_to_all(partial, "cent", split_axis=0, concat_axis=0, tiled=True)
    final = jnp.max(parts, axis=0)
    return (vectors, final[0], final[1], final[2])


def solution(mesh):
    placed = (
        P(("dp", "cent"), None, None, None),
        P(("dp", "cent"), None),
        P(("dp", "cent"), None),
        P(("dp", "cent"), None),
        P(),
        P(),
        P(),
        P(),
        P("cent", None),
    )
    return jax.shard_map(
        local,
        mesh=mesh,
        in_specs=placed,
        out_specs=(
            P(("dp", "cent"), None),
            P(("dp", "cent")),
            P(("dp", "cent")),
            P(("dp", "cent")),
        ),
        check_vma=False,
    )
```

```python
import functools

import jax
import jax.numpy as jnp
from jax import lax
from jax.experimental import pallas as pl
from jax.experimental.pallas import tpu as pltpu
from jax.sharding import PartitionSpec as P

SIDE = 4
SPOTS = SIDE * SIDE
BF = jnp.bfloat16
F32 = jnp.float32


def neighbours(at, extent):
    return [(at + shift - 1, shift) for shift in range(3) if 0 <= at + shift - 1 < extent]


STEPS = 9


def identity(size):
    line = lax.broadcasted_iota(jnp.int32, (size, size), 0)
    lane = lax.broadcasted_iota(jnp.int32, (size, size), 1)
    return (line == lane).astype(F32).astype(BF)


def turn(eye, matrix):
    return lax.dot_general(eye, matrix, (((1,), (1,)), ((), ())), preferred_element_type=F32)


def embed_kernel(
    stored_ref, counts_hbm, send_hbm, wide_hbm, taps_ref, reduce_hbm, head_hbm, panel_hbm,
    out_ref, panel_ref, head_ref, flip_ref, *scratch,
):
    x_refs, act_refs = scratch[0:6], scratch[10:13]
    hidden_refs = scratch[6:10] + scratch[6:8]
    pool_ref, packed_pool_ref = scratch[13:15]
    weight_refs = scratch[15:17]
    expand_ref, depth_ref, clip_ref, arrival = scratch[17:21]
    count_ref, send_ref, wide_ref, reduce_ref, ready = scratch[21:26]
    channels, clips = clip_ref.shape[2], clip_ref.shape[3]
    early = [
        pltpu.make_async_copy(source, target, ready.at[at])
        for at, (source, target) in enumerate(
            [(counts_hbm, count_ref), (send_hbm, send_ref), (wide_hbm, wide_ref), (reduce_hbm, reduce_ref)]
        )
    ]
    late = [
        pltpu.make_async_copy(source, target, ready.at[4 + at])
        for at, (source, target) in enumerate([(head_hbm, head_ref), (panel_hbm, panel_ref)])
    ]
    for copy in early:
        copy.start()
    copies = [
        pltpu.make_async_copy(stored_ref.at[frame], clip_ref.at[frame], arrival.at[frame])
        for frame in range(clip_ref.shape[0])
    ]
    for copy in copies:
        copy.start()
    expanded = wide_ref.shape[2]
    eye = identity(expanded)
    early[0].wait()
    early[2].wait()
    for layer in range(2):
        expand_ref[layer] = turn(eye, wide_ref[layer]).astype(BF)
        depth_ref[layer, :, : taps_ref.shape[0]] = turn(eye, taps_ref[:, layer, :])

    counts = count_ref[...].astype(F32)
    line = lax.broadcasted_iota(jnp.int32, (clips, clips), 0)
    lane = lax.broadcasted_iota(jnp.int32, (clips, clips), 1)
    count_lane = jnp.broadcast_to(counts, (clips, clips))
    count_line = jnp.transpose(count_lane)
    ahead = (count_lane > count_line) | ((count_lane == count_line) & (lane < line))
    rank = jnp.dot(
        ahead.astype(F32).astype(BF), jnp.ones((clips, clips), BF), preferred_element_type=F32
    ).astype(jnp.int32)
    n1, n2, n3 = [jnp.sum((counts > frame).astype(jnp.int32)) for frame in (1, 2, 3)]
    blocks = expanded // 16 // STEPS
    one_hot = lambda mask: mask.astype(F32).astype(BF)
    order = one_hot(rank == lane)
    place = [
        order,
        one_hot((rank == lane) & (count_line > 1)),
        jnp.concatenate(
            [
                one_hot((rank == lane) & (count_line > 2)),
                one_hot((rank + n2 == lane) & (count_line > 3)),
            ],
            axis=0,
        ),
    ]
    row_lane = lax.broadcasted_iota(jnp.int32, (1, clips), 1)
    kept = [None, (row_lane < n1).astype(F32), (row_lane < n2 + n3).astype(F32)]
    tile_lane = lax.broadcasted_iota(jnp.int32, (16, clips), 1)
    in_second, in_third = tile_lane < n2, tile_lane < n3

    def expand(layer, tile, pair, both):
        hidden = jnp.maximum(jnp.dot(expand_ref[layer], both, preferred_element_type=F32), 0.0)
        hidden_refs[3 * layer + tile][2 * pair] = hidden[:, :clips]
        hidden_refs[3 * layer + tile][2 * pair + 1] = hidden[:, clips:]

    def gather(tile, pair):
        if tile < 2:
            spots = jnp.concatenate([clip_ref[tile, 2 * pair], clip_ref[tile, 2 * pair + 1]], axis=0)
        else:
            spots = jnp.concatenate(
                [
                    jnp.concatenate([clip_ref[2, 2 * pair + side], clip_ref[3, 2 * pair + side]], axis=1)
                    for side in range(2)
                ],
                axis=0,
            )
        x = jnp.dot(spots, place[tile], preferred_element_type=F32).astype(BF)
        x_refs[tile][2 * pair] = x[:channels]
        x_refs[tile][2 * pair + 1] = x[channels:]

    def expand_stored(layer, tile, pair):
        x_ref = x_refs[3 * layer + tile]
        expand(layer, tile, pair, jnp.concatenate([x_ref[2 * pair], x_ref[2 * pair + 1]], axis=1))

    def spread_taps(layer, step, first, last):
        rows = [pl.ds(pl.multiple_of((step * blocks + at) * 16, 16), 16) for at in range(blocks)]
        taps = [depth_ref[layer, row, :] for row in rows]
        for tap in range(first, last):
            for at in range(blocks):
                weight_refs[layer][step * blocks + at, tap] = jnp.broadcast_to(
                    taps[at][:, tap : tap + 1], (16, clips)
                )

    def reduce(layer, tile, pair):
        both = jnp.concatenate([act_refs[tile][2 * pair], act_refs[tile][2 * pair + 1]], axis=1)
        branch = jnp.dot(reduce_ref[layer], both, preferred_element_type=F32)
        result = []
        for side in range(2):
            part = branch[:, side * clips : (side + 1) * clips]
            if kept[tile] is not None:
                part = part * kept[tile]
            x = x_refs[3 * layer + tile][2 * pair + side].astype(F32) + part
            result.append(x.astype(BF))
        return result

    def reduce_store(tile, pair):
        x = reduce(0, tile, pair)
        x_refs[3 + tile][2 * pair] = x[0]
        x_refs[3 + tile][2 * pair + 1] = x[1]

    def reduce_pool(tile, pair, live):
        x = reduce(1, tile, pair)
        into = packed_pool_ref if tile == 2 else pool_ref
        into[...] += (x[0].astype(F32) + x[1].astype(F32)) * live

    def depthwise(layer, tile, block):
        rows = pl.ds(pl.multiple_of(block * 16, 16), 16)
        read = lambda source, spot: hidden_refs[3 * layer + source][spot, rows, :]
        if tile == 0:
            sources = [(1, lambda s: read(0, s)), (2, lambda s: read(1, s))]
        elif tile == 1:
            sources = [
                (0, lambda s: read(0, s)),
                (1, lambda s: read(1, s)),
                (2, lambda s: jnp.where(in_second, read(2, s), 0.0)),
            ]
        else:
            sources = [
                (0, lambda s: jnp.where(in_second, read(1, s), pltpu.roll(read(2, s), n2, 1))),
                (1, lambda s: read(2, s)),
                (2, lambda s: jnp.where(in_third, pltpu.roll(read(2, s), clips - n2, 1), 0.0)),
            ]
        mixed = [None] * SPOTS
        for shift_t, source in sources:
            weight = [weight_refs[layer][block, 9 * shift_t + tap].astype(BF) for tap in range(9)]
            hidden = [source(spot).astype(BF) for spot in range(SPOTS)]
            for y in range(SIDE):
                for from_y, shift_y in neighbours(y, SIDE):
                    for z in range(SIDE):
                        for from_z, shift_z in neighbours(z, SIDE):
                            term = hidden[from_y * SIDE + from_z] * weight[3 * shift_y + shift_z]
                            spot = y * SIDE + z
                            mixed[spot] = term if mixed[spot] is None else mixed[spot] + term
        for spot in range(SPOTS):
            half = mixed[spot] * BF(0.5)
            act_refs[tile][spot, rows, :] = half + half * jnp.tanh(half)

    def stage(layer, tile, other):
        @pl.loop(0, STEPS)
        def _(step):
            pair = jnp.minimum(step, SPOTS // 2 - 1)
            before = jnp.maximum(step - 1, 0)
            other(pair, before, (step < SPOTS // 2).astype(F32))
            if layer == 0:
                if tile == 0:
                    spread_taps(0, step, 0, 9)
                spread_taps(1, step, 9 * tile, 9 * tile + 9)
            for at in range(blocks):
                depthwise(layer, tile, step * blocks + at)

    def filler(first, second):
        def other(pair, before, live):
            second(before)
            first(pair)

        return other

    pool_ref[...] = jnp.zeros_like(pool_ref)
    packed_pool_ref[...] = jnp.zeros_like(packed_pool_ref)
    copies[0].wait()
    copies[1].wait()

    @pl.loop(0, STEPS)
    def _(step):
        pair = jnp.minimum(step, SPOTS // 2 - 1)
        before = jnp.maximum(step - 1, 0)
        for tile in range(2):
            expand_stored(0, tile, before)
            gather(tile, pair)
        spread_taps(0, step, 9, 27)

    copies[2].wait()
    copies[3].wait()
    early[1].wait()
    early[3].wait()
    for copy in late:
        copy.start()
    stage(0, 0, filler(lambda pair: gather(2, pair), lambda pair: expand_stored(0, 2, pair)))
    stage(0, 1, filler(lambda pair: reduce_store(0, pair), lambda pair: expand_stored(1, 0, pair)))
    stage(0, 2, filler(lambda pair: reduce_store(1, pair), lambda pair: expand_stored(1, 1, pair)))
    stage(1, 0, filler(lambda pair: reduce_store(2, pair), lambda pair: expand_stored(1, 2, pair)))
    stage(1, 1, lambda pair, before, live: reduce_pool(0, pair, live))
    stage(1, 2, lambda pair, before, live: reduce_pool(1, pair, live))

    @pl.loop(0, SPOTS // 2)
    def _(pair):
        reduce_pool(2, pair, 1.0)

    late[0].wait()
    small = identity(256)
    for part in range(flip_ref.shape[0] // 256):
        part = slice(part * 256, (part + 1) * 256)
        flip_ref[part, :] = turn(small, head_ref[:, part]).astype(BF)
    packed = packed_pool_ref[...]
    total = (
        pool_ref[...]
        + jnp.where(row_lane < n2, packed, 0.0)
        + jnp.where(row_lane < n3, pltpu.roll(packed, clips - n2, 1), 0.0)
    )
    lengths = jnp.dot(
        jnp.broadcast_to(counts, (16, clips)).astype(BF), order, preferred_element_type=F32
    )[0:1]
    pooled = (total / (lengths * SPOTS)).astype(BF)
    n_dp, per_peer = out_ref.shape[0], out_ref.shape[1]
    slot = (line % per_peer) * n_dp + line // per_peer
    pick = one_hot(jnp.broadcast_to(send_ref[...], (clips, clips)) == slot)
    pick = lax.dot_general(pick, order, (((1,), (0,)), ((), ())), preferred_element_type=F32).astype(BF)
    rows = lax.dot_general(pick, pooled, (((1,), (1,)), ((), ())), preferred_element_type=F32)
    out_ref[:, :, :channels] = rows.astype(BF).reshape(n_dp, per_peer, channels)
    out_ref[:, :, channels:] = jnp.zeros((n_dp, per_peer, out_ref.shape[2] - channels), BF)
    late[1].wait()


def embed(
    clip_data, frame_counts, send_list, expand_weight, depth_kernel, reduce_weight, head_weight, centroids, n_dp
):
    clips, frames, spots, channels = clip_data.shape
    expanded = expand_weight.shape[2]
    dims = head_weight.shape[1]
    stored = pl.BlockSpec(memory_space=pltpu.HBM)
    local_ref = pl.BlockSpec(memory_space=pltpu.VMEM)
    return pl.pallas_call(
        embed_kernel,
        out_shape=(
            jax.ShapeDtypeStruct((n_dp, clips // n_dp, 256), BF),
            pltpu.VMEM(centroids.shape, BF),
            pltpu.VMEM(head_weight.shape, BF),
            pltpu.VMEM((dims, channels), BF),
        ),
        in_specs=[stored] * 4 + [local_ref] + [stored] * 3,
        out_specs=(local_ref,) * 4,
        scratch_shapes=[pltpu.VMEM((spots, channels, clips), BF)] * 6
        + [pltpu.VMEM((spots, expanded, clips), F32)] * 4
        + [pltpu.VMEM((spots, expanded, clips), BF)] * 3
        + [pltpu.VMEM((channels, clips), F32)] * 2
        + [pltpu.VMEM((expanded // 16, 27, 16, clips), F32)] * 2
        + [pltpu.VMEM((2, expanded, channels), BF), pltpu.VMEM((2, expanded, clips), F32)]
        + [pltpu.VMEM((frames, spots, channels, clips), BF), pltpu.SemaphoreType.DMA((frames,))]
        + [pltpu.VMEM((1, clips), jnp.int32)] * 2
        + [
            pltpu.VMEM((2, channels, expanded), BF),
            pltpu.VMEM((2, channels, expanded), BF),
            pltpu.SemaphoreType.DMA((6,)),
        ],
        compiler_params=pltpu.CompilerParams(vmem_limit_bytes=48 << 20),
        name="embed",
    )(
        jnp.transpose(clip_data, (1, 2, 3, 0)),
        frame_counts,
        send_list,
        expand_weight,
        jnp.transpose(depth_kernel, (1, 0, 2)),
        jnp.swapaxes(reduce_weight, 1, 2),
        head_weight,
        centroids,
    )


def unit(projected, axis):
    square = jnp.sum(projected * projected, axis=axis, keepdims=True)
    return (projected * lax.rsqrt(square + 1e-06)).astype(BF)


LABEL_ROWS = 16


def own_kernel(arrived_ref, ids_ref, payload_ref, rows_ref):
    n_dp, per_peer, width = arrived_ref.shape
    clips = n_dp * per_peer
    channels = rows_ref.shape[1]
    arrived = arrived_ref[...].reshape(clips, width)[:, :channels]
    row = lax.broadcasted_iota(jnp.int32, (clips, clips), 0)
    lane = lax.broadcasted_iota(jnp.int32, (clips, clips), 1)
    pick = (lane == (row % n_dp) * per_peer + row // n_dp).astype(F32).astype(BF)
    rows = jnp.dot(pick, arrived, preferred_element_type=F32)
    rows_ref[...] = rows.astype(BF)
    ids = ids_ref[...]
    which = lax.broadcasted_iota(jnp.int32, (LABEL_ROWS, clips), 0)
    high, low = ids // 256, ids % 256
    label = jnp.where(which == 0, high, jnp.where(which == 1, low, 0))
    payload = jnp.concatenate([jnp.transpose(rows), label.astype(F32)], axis=0).astype(BF)
    payload_ref[...] = payload


def own(arrived, cluster_ids, channels):
    n_dp, per_peer, width = arrived.shape
    clips = n_dp * per_peer
    height = channels + LABEL_ROWS
    return pl.pallas_call(
        own_kernel,
        out_shape=(
            jax.ShapeDtypeStruct((height, clips), BF),
            jax.ShapeDtypeStruct((clips, channels), BF),
        ),
        in_specs=[pl.BlockSpec(memory_space=pltpu.VMEM)] * 2,
        out_specs=(pl.BlockSpec(memory_space=pltpu.VMEM),) * 2,
        compiler_params=pltpu.CompilerParams(vmem_limit_bytes=8 << 20),
        name="own",
    )(arrived, cluster_ids)


def vectors_kernel(rows_ref, head_ref, vectors_ref):
    projected = jnp.dot(rows_ref[...], head_ref[...], preferred_element_type=F32)
    vectors_ref[...] = unit(projected, 1)


def vectors_of(rows, head_weight):
    clips, channels = rows.shape
    dims = head_weight.shape[1]
    return pl.pallas_call(
        vectors_kernel,
        out_shape=jax.ShapeDtypeStruct((clips, dims), BF),
        in_specs=[pl.BlockSpec(memory_space=pltpu.VMEM)] * 2,
        out_specs=pl.BlockSpec(memory_space=pltpu.VMEM),
        compiler_params=pltpu.CompilerParams(vmem_limit_bytes=8 << 20),
        cost_estimate=pl.CostEstimate(
            flops=2 * clips * dims * channels, bytes_accessed=2 * dims * (clips + channels), transcendentals=0
        ),
        name="vectors",
    )(rows, head_weight)


PANEL_ROWS = 784
OCCUR = 64
LEFT = 2


def label_of(rows_ref, block, channels):
    label = jnp.concatenate(
        [rows_ref[2 * block, channels:, :], rows_ref[2 * block + 1, channels:, :]], axis=1
    ).astype(F32)
    return label[0:1] * 256.0 + label[1:2]


def score_rows(
    rows_ref, flip_ref, panel_ref, turned_ref, near_ref, own_ref, best_ref, line_ref, send_turned, arrive, extra
):
    blocks, height, clips = rows_ref.shape
    channels = flip_ref.shape[1]
    panel_rows = panel_ref.shape[0] // 8 * 8

    @pl.loop(0, blocks // 2)
    def _(pair):
        both = jnp.concatenate([rows_ref[2 * pair], rows_ref[2 * pair + 1]], axis=1)
        parts = [slice(at, at + 256) for at in range(0, flip_ref.shape[0], 256)]
        square = jnp.zeros((8, 2 * clips), F32)
        for part in parts:
            projected = jnp.dot(flip_ref[part, :], both[:channels], preferred_element_type=F32)
            line_ref[part, :] = projected
            square += jnp.sum((projected * projected).reshape(32, 8, 2 * clips), axis=0)
        scale = lax.rsqrt(jnp.sum(square, axis=0, keepdims=True) + 1e-06)
        for part in parts:
            turned_ref[pair, part, :] = (line_ref[part, :] * scale).astype(BF)
        best_ref[pair] = jnp.dot(extra, turned_ref[pair], preferred_element_type=F32)

    send_turned()
    base = lax.axis_index("cent") * (panel_rows + LEFT)
    for step in range(pl.cdiv(panel_rows, PANEL_ROWS)):
        arrive(step)
        rows = slice(step * PANEL_ROWS, min(panel_rows, (step + 1) * PANEL_ROWS))

        @pl.loop(0, blocks // 2)
        def _(pair):
            scores = jnp.dot(panel_ref[rows, :], turned_ref[pair], preferred_element_type=F32)
            best_ref[pair] = jnp.maximum(
                best_ref[pair], jnp.max(scores.reshape((rows.stop - rows.start) // 8, 8, 2 * clips), axis=0)
            )
            if step == 0:
                local_id = label_of(rows_ref, pair, channels).astype(jnp.int32) - base
                index = lax.broadcasted_iota(jnp.int32, (OCCUR, 2 * clips), 0)
                own_ref[pair] = jnp.max(
                    jnp.where(index == local_id, scores[:OCCUR], -jnp.inf), axis=0, keepdims=True
                )

    for pair in range(blocks // 2):
        near_ref[pair] = jnp.max(best_ref[pair], axis=0, keepdims=True)


def near_kernel(
    rows_ref, flip_ref, panel_ref, turned_hbm, near_ref, own_ref, spread_ref, extra_ref, turned_ref, best_ref, line_ref, done
):
    for peer in range(spread_ref.shape[0]):
        spread_ref[peer] = rows_ref[0]
    panel_rows = panel_ref.shape[0]
    left = panel_ref[panel_rows - LEFT : panel_rows, :]
    extra = jnp.concatenate([left] * (8 // LEFT), axis=0)
    extra_ref[...] = extra
    copy = pltpu.make_async_copy(turned_ref, turned_hbm, done)
    score_rows(
        rows_ref, flip_ref, panel_ref, turned_ref, near_ref, own_ref, best_ref, line_ref,
        copy.start, lambda step: None, extra
    )
    copy.wait()


def far_kernel(
    rows_ref, flip_ref, stored_ref, extra_ref, turned_hbm, near_ref, own_ref, turned_ref, best_ref, line_ref, done,
    panel_ref, arrival,
):
    copies = []
    for step in range(arrival.shape[0]):
        rows = slice(step * PANEL_ROWS, min(panel_ref.shape[0], (step + 1) * PANEL_ROWS))
        copies.append(pltpu.make_async_copy(stored_ref.at[rows], panel_ref.at[rows], arrival.at[step]))
        copies[-1].start()
    copy = pltpu.make_async_copy(turned_ref, turned_hbm, done)
    score_rows(
        rows_ref, flip_ref, panel_ref, turned_ref, near_ref, own_ref, best_ref, line_ref,
        copy.start, lambda step: copies[step].wait(), extra_ref[...],
    )
    copy.wait()


def scored(kernel, name, rows, flip, panel, limit, spread=None, extra=None):
    blocks, height, clips = rows.shape
    dims, channels = flip.shape
    pairs, width = blocks // 2, 2 * clips
    panel_rows = panel.shape[0]
    here = pl.BlockSpec(memory_space=pltpu.VMEM)
    stored = pl.BlockSpec(memory_space=pltpu.HBM)
    shapes = [
        pltpu.HBM((pairs, dims, width), BF),
        jax.ShapeDtypeStruct((pairs, 1, width), F32),
        jax.ShapeDtypeStruct((pairs, 1, width), F32),
    ]
    scratch = [
        pltpu.VMEM((pairs, dims, width), BF),
        pltpu.VMEM((pairs, 8, width), F32),
        pltpu.VMEM((dims, width), F32),
        pltpu.SemaphoreType.DMA(()),
    ]
    if spread is None:
        even = panel_rows // 8 * 8
        scratch += [
            pltpu.VMEM((even, dims), BF), pltpu.SemaphoreType.DMA((pl.cdiv(even, PANEL_ROWS),))
        ]
    else:
        assert panel_rows % 8 == LEFT
        shapes.append(jax.ShapeDtypeStruct((spread, height, clips), BF))
        shapes.append(jax.ShapeDtypeStruct((8, dims), BF))
    return pl.pallas_call(
        kernel,
        out_shape=shapes,
        in_specs=[here, here] + ([stored, here] if spread is None else [here]),
        out_specs=[stored] + [here] * (len(shapes) - 1),
        scratch_shapes=scratch,
        compiler_params=pltpu.CompilerParams(vmem_limit_bytes=limit << 20),
        cost_estimate=pl.CostEstimate(
            flops=2 * blocks * clips * panel_rows * dims, bytes_accessed=2 * panel_rows * dims, transcendentals=0
        ),
        name=name,
    )(rows, flip, panel, *([extra] if spread is None else []))


GROUP = 4


def peer_kernel(
    near_rows_ref, near_turned_hbm, near_best_ref, near_own_ref, far_rows_ref, far_turned_hbm, far_best_ref, far_own_ref,
    cols_ref, head_ref, out_ref, near_turned_ref, far_turned_ref, best_ref, arrival,
):
    copies = [
        pltpu.make_async_copy(near_turned_hbm, near_turned_ref, arrival.at[0]),
        pltpu.make_async_copy(far_turned_hbm, far_turned_ref, arrival.at[1]),
    ]
    for copy in copies:
        copy.start()
    n_dp, height, clips = cols_ref.shape
    n_cent = out_ref.shape[0]
    channels = head_ref.shape[0]
    eye = identity(clips)
    best_ref[...] = jnp.full_like(best_ref, -1.0)
    mine_dp, mine_cent = lax.axis_index("dp"), lax.axis_index("cent")

    def visit(group, first):
        flipped = jnp.concatenate([turn(eye, cols_ref[group * GROUP + at]) for at in range(GROUP)], axis=0)
        projected = jnp.dot(flipped[:, :channels].astype(BF), head_ref[...], preferred_element_type=F32)
        vectors = unit(projected, 1)
        ids = flipped[:, channels : channels + 1] * 256.0 + flipped[:, channels + 1 : channels + 2]
        wide = jnp.broadcast_to(ids, (GROUP * clips, 2 * clips))
        for block in range(n_cent // 2):
            cols = slice(block * 2 * clips, (block + 1) * 2 * clips)
            if first and block < 2:
                copies[block].wait()
            if block == 0:
                turned, row_ids = near_turned_ref[0], label_of(near_rows_ref, 0, channels)
            else:
                turned, row_ids = far_turned_ref[block - 1], label_of(far_rows_ref, block - 1, channels)
            scores = jnp.dot(vectors, turned, preferred_element_type=F32)
            same = wide == row_ids
            if block == 0:
                line = lax.broadcasted_iota(jnp.int32, same.shape, 0)
                lane = lax.broadcasted_iota(jnp.int32, same.shape, 1)
                itself = jnp.where(lane < clips, lane + (mine_dp - group * GROUP) * clips, -1)
                same = same & (line != itself)
            found = jnp.where(same, scores, -1.0)
            best_ref[:, cols] = jnp.maximum(
                best_ref[:, cols], jnp.max(found.reshape(GROUP * clips // 8, 8, 2 * clips), axis=0)
            )

    visit(0, True)

    @pl.loop(1, n_dp // GROUP)
    def _(group):
        visit(group, False)

    best = jnp.max(best_ref[...], axis=0, keepdims=True)
    for block in range(n_cent // 2):
        for side in range(2):
            chip = (mine_cent // 2 + block) % (n_cent // 2)
            cent = 2 * chip + (mine_cent + side) % 2
            at = slice((2 * block + side) * clips, (2 * block + side + 1) * clips)
            part = slice(side * clips, (side + 1) * clips)
            if block == 0:
                nearest, own_best = near_best_ref[0, :, part], near_own_ref[0, :, part]
            else:
                nearest, own_best = far_best_ref[block - 1, :, part], far_own_ref[block - 1, :, part]
            out_ref[cent, 0:1, :] = nearest
            out_ref[cent, 1:2, :] = own_best
            out_ref[cent, 2:3, :] = best[:, at]
            out_ref[cent, 3:4, :] = best[:, at]


def peers_of(near_rows, near_found, far_rows, far_found, cols, head_weight):
    n_dp, height, clips = cols.shape
    n_cent = near_rows.shape[0] + far_rows.shape[0]
    dims = head_weight.shape[1]
    here = pl.BlockSpec(memory_space=pltpu.VMEM)
    stored = pl.BlockSpec(memory_space=pltpu.HBM)
    near_found, far_found = [
        [pltpu.with_memory_space_constraint(found[0], pltpu.HBM), *found[1:]] for found in (near_found, far_found)
    ]
    return pl.pallas_call(
        peer_kernel,
        out_shape=jax.ShapeDtypeStruct((n_cent, 4, clips), F32),
        in_specs=[here, stored, here, here] * 2 + [here] * 2,
        out_specs=here,
        scratch_shapes=[
            pltpu.VMEM(near_found[0].shape, BF),
            pltpu.VMEM(far_found[0].shape, BF),
            pltpu.VMEM((8, n_cent * clips), F32),
            pltpu.SemaphoreType.DMA((2,)),
        ],
        compiler_params=pltpu.CompilerParams(vmem_limit_bytes=16 << 20),
        cost_estimate=pl.CostEstimate(
            flops=2 * n_dp * n_cent * clips * clips * dims, bytes_accessed=4 << 20, transcendentals=0
        ),
        name="peers",
    )(near_rows, *near_found, far_rows, *far_found, cols, head_weight)


def local(
    clip_data,
    frame_counts,
    send_list,
    cluster_ids,
    expand_weight,
    depth_kernel,
    reduce_weight,
    head_weight,
    centroids,
):
    n_dp = lax.axis_size("dp")
    n_cent = lax.axis_size("cent")
    pooled, panel, head, flip = embed(
        clip_data, frame_counts, send_list, expand_weight, depth_kernel, reduce_weight, head_weight, centroids, n_dp
    )
    arrived = lax.all_to_all(pooled, "dp", split_axis=0, concat_axis=0, tiled=True)
    payload, rows = own(arrived, cluster_ids, head_weight.shape[0])
    partner = lax.ppermute(payload, "cent", [(at, at ^ 1) for at in range(n_cent)])
    near_rows = jnp.stack([payload, partner])
    far_rows = jnp.concatenate(
        [
            lax.ppermute(near_rows, "cent", [((at + 2 * chip) % n_cent, at) for at in range(n_cent)])
            for chip in range(1, n_cent // 2)
        ]
    )
    *near_found, spread, extra = scored(near_kernel, "near", near_rows, flip, panel, 16, n_dp)
    cols = lax.all_to_all(spread, "dp", split_axis=0, concat_axis=0, tiled=True)
    vectors = vectors_of(rows, head)
    far_found = scored(
        far_kernel, "far", far_rows, flip, pltpu.with_memory_space_constraint(centroids, pltpu.HBM), 32, extra=extra
    )
    partial = peers_of(near_rows, near_found, far_rows, far_found, cols, head)
    parts = lax.all_to_all(partial, "cent", split_axis=0, concat_axis=0, tiled=True)
    final = jnp.max(parts, axis=0)
    return (vectors, final[0], final[1], final[2])


def solution(mesh):
    placed = (
        P(("dp", "cent"), None, None, None),
        P(("dp", "cent"), None),
        P(("dp", "cent"), None),
        P(("dp", "cent"), None),
        P(),
        P(),
        P(),
        P(),
        P("cent", None),
    )
    return jax.shard_map(
        local,
        mesh=mesh,
        in_specs=placed,
        out_specs=(
            P(("dp", "cent"), None),
            P(("dp", "cent")),
            P(("dp", "cent")),
            P(("dp", "cent")),
        ),
        check_vma=False,
    )
```

```python
import functools

import jax
import jax.numpy as jnp
from jax import lax
from jax.experimental import pallas as pl
from jax.experimental.pallas import tpu as pltpu
from jax.sharding import PartitionSpec as P

SIDE = 4
SPOTS = SIDE * SIDE
BF = jnp.bfloat16
F32 = jnp.float32


def neighbours(at, extent):
    return [(at + shift - 1, shift) for shift in range(3) if 0 <= at + shift - 1 < extent]


STEPS = 9


def identity(size):
    line = lax.broadcasted_iota(jnp.int32, (size, size), 0)
    lane = lax.broadcasted_iota(jnp.int32, (size, size), 1)
    return (line == lane).astype(F32).astype(BF)


def turn(eye, matrix):
    return lax.dot_general(eye, matrix, (((1,), (1,)), ((), ())), preferred_element_type=F32)


def embed_kernel(
    stored_ref, counts_hbm, send_hbm, wide_hbm, taps_ref, reduce_hbm, head_hbm, panel_hbm,
    out_ref, panel_ref, head_ref, flip_ref, *scratch,
):
    x_refs, act_refs = scratch[0:6], scratch[10:13]
    hidden_refs = scratch[6:10] + scratch[6:8]
    pool_ref, packed_pool_ref = scratch[13:15]
    weight_refs = scratch[15:17]
    expand_ref, depth_ref, clip_ref, arrival = scratch[17:21]
    count_ref, send_ref, wide_ref, reduce_ref, ready = scratch[21:26]
    channels, clips = clip_ref.shape[2], clip_ref.shape[3]
    early = [
        pltpu.make_async_copy(source, target, ready.at[at])
        for at, (source, target) in enumerate(
            [(counts_hbm, count_ref), (send_hbm, send_ref), (wide_hbm, wide_ref), (reduce_hbm, reduce_ref)]
        )
    ]
    late = [
        pltpu.make_async_copy(source, target, ready.at[4 + at])
        for at, (source, target) in enumerate([(head_hbm, head_ref), (panel_hbm, panel_ref)])
    ]
    for copy in early:
        copy.start()
    copies = [
        pltpu.make_async_copy(stored_ref.at[frame], clip_ref.at[frame], arrival.at[frame])
        for frame in range(clip_ref.shape[0])
    ]
    for copy in copies:
        copy.start()
    expanded = wide_ref.shape[2]
    eye = identity(expanded)
    early[0].wait()
    early[2].wait()
    for layer in range(2):
        expand_ref[layer] = turn(eye, wide_ref[layer]).astype(BF)
        depth_ref[layer, :, : taps_ref.shape[0]] = turn(eye, taps_ref[:, layer, :])

    counts = count_ref[...].astype(F32)
    line = lax.broadcasted_iota(jnp.int32, (clips, clips), 0)
    lane = lax.broadcasted_iota(jnp.int32, (clips, clips), 1)
    count_lane = jnp.broadcast_to(counts, (clips, clips))
    count_line = jnp.transpose(count_lane)
    ahead = (count_lane > count_line) | ((count_lane == count_line) & (lane < line))
    rank = jnp.dot(
        ahead.astype(F32).astype(BF), jnp.ones((clips, clips), BF), preferred_element_type=F32
    ).astype(jnp.int32)
    n1, n2, n3 = [jnp.sum((counts > frame).astype(jnp.int32)) for frame in (1, 2, 3)]
    blocks = expanded // 16 // STEPS
    one_hot = lambda mask: mask.astype(F32).astype(BF)
    order = one_hot(rank == lane)
    none = jnp.zeros((clips, clips), BF)
    place = [
        jnp.concatenate(
            [
                jnp.concatenate([order, none], axis=1),
                jnp.concatenate([none, one_hot((rank == lane) & (count_line > 1))], axis=1),
            ],
            axis=0,
        ),
        jnp.concatenate(
            [
                one_hot((rank == lane) & (count_line > 2)),
                one_hot((rank + n2 == lane) & (count_line > 3)),
            ],
            axis=0,
        ),
    ]
    row_lane = lax.broadcasted_iota(jnp.int32, (1, clips), 1)
    kept = [None, (row_lane < n1).astype(F32), (row_lane < n2 + n3).astype(F32)]
    tile_lane = lax.broadcasted_iota(jnp.int32, (16, clips), 1)
    in_second, in_third = tile_lane < n2, tile_lane < n3

    def expand(layer, tile, pair, both):
        hidden = jnp.maximum(jnp.dot(expand_ref[layer], both, preferred_element_type=F32), 0.0)
        hidden_refs[3 * layer + tile][2 * pair] = hidden[:, :clips]
        hidden_refs[3 * layer + tile][2 * pair + 1] = hidden[:, clips:]

    def gather(first, pair):
        spots = jnp.concatenate(
            [
                jnp.concatenate([clip_ref[first, 2 * pair + side], clip_ref[first + 1, 2 * pair + side]], axis=1)
                for side in range(2)
            ],
            axis=0,
        )
        x = jnp.dot(spots, place[first // 2], preferred_element_type=F32).astype(BF)
        for side in range(2):
            rows = slice(side * channels, (side + 1) * channels)
            for at in range(x.shape[1] // clips):
                x_refs[first + at][2 * pair + side] = x[rows, at * clips : (at + 1) * clips]

    def expand_stored(layer, tile, pair):
        x_ref = x_refs[3 * layer + tile]
        expand(layer, tile, pair, jnp.concatenate([x_ref[2 * pair], x_ref[2 * pair + 1]], axis=1))

    def spread_taps(layer, step, first, last):
        rows = [pl.ds(pl.multiple_of((step * blocks + at) * 16, 16), 16) for at in range(blocks)]
        taps = [depth_ref[layer, row, :] for row in rows]
        for tap in range(first, last):
            for at in range(blocks):
                weight_refs[layer][step * blocks + at, tap] = jnp.broadcast_to(
                    taps[at][:, tap : tap + 1], (16, clips)
                )

    def reduce(layer, tile, pair):
        both = jnp.concatenate([act_refs[tile][2 * pair], act_refs[tile][2 * pair + 1]], axis=1)
        branch = jnp.dot(reduce_ref[layer], both, preferred_element_type=F32)
        result = []
        for side in range(2):
            part = branch[:, side * clips : (side + 1) * clips]
            if kept[tile] is not None:
                part = part * kept[tile]
            x = x_refs[3 * layer + tile][2 * pair + side].astype(F32) + part
            result.append(x.astype(BF))
        return result

    def reduce_store(tile, pair):
        x = reduce(0, tile, pair)
        x_refs[3 + tile][2 * pair] = x[0]
        x_refs[3 + tile][2 * pair + 1] = x[1]

    def reduce_pool(tile, pair, live):
        x = reduce(1, tile, pair)
        into = packed_pool_ref if tile == 2 else pool_ref
        into[...] += (x[0].astype(F32) + x[1].astype(F32)) * live

    def depthwise(layer, tile, block):
        rows = pl.ds(pl.multiple_of(block * 16, 16), 16)
        read = lambda source, spot: hidden_refs[3 * layer + source][spot, rows, :]
        if tile == 0:
            sources = [(1, lambda s: read(0, s)), (2, lambda s: read(1, s))]
        elif tile == 1:
            sources = [
                (0, lambda s: read(0, s)),
                (1, lambda s: read(1, s)),
                (2, lambda s: jnp.where(in_second, read(2, s), 0.0)),
            ]
        else:
            sources = [
                (0, lambda s: jnp.where(in_second, read(1, s), pltpu.roll(read(2, s), n2, 1))),
                (1, lambda s: read(2, s)),
                (2, lambda s: jnp.where(in_third, pltpu.roll(read(2, s), clips - n2, 1), 0.0)),
            ]
        mixed = [None] * SPOTS
        for shift_t, source in sources:
            weight = [weight_refs[layer][block, 9 * shift_t + tap].astype(BF) for tap in range(9)]
            hidden = [source(spot).astype(BF) for spot in range(SPOTS)]
            for y in range(SIDE):
                for from_y, shift_y in neighbours(y, SIDE):
                    for z in range(SIDE):
                        for from_z, shift_z in neighbours(z, SIDE):
                            term = hidden[from_y * SIDE + from_z] * weight[3 * shift_y + shift_z]
                            spot = y * SIDE + z
                            mixed[spot] = term if mixed[spot] is None else mixed[spot] + term
        for spot in range(SPOTS):
            half = mixed[spot] * BF(0.5)
            act_refs[tile][spot, rows, :] = half + half * jnp.tanh(half)

    def stage(layer, tile, other):
        @pl.loop(0, STEPS)
        def _(step):
            pair = jnp.minimum(step, SPOTS // 2 - 1)
            before = jnp.maximum(step - 1, 0)
            other(pair, before, (step < SPOTS // 2).astype(F32))
            if layer == 0:
                if tile == 0:
                    spread_taps(0, step, 0, 9)
                spread_taps(1, step, 9 * tile, 9 * tile + 9)
            for at in range(blocks):
                depthwise(layer, tile, step * blocks + at)

    def filler(first, second):
        def other(pair, before, live):
            second(before)
            first(pair)

        return other

    pool_ref[...] = jnp.zeros_like(pool_ref)
    packed_pool_ref[...] = jnp.zeros_like(packed_pool_ref)
    copies[0].wait()
    copies[1].wait()

    @pl.loop(0, STEPS)
    def _(step):
        pair = jnp.minimum(step, SPOTS // 2 - 1)
        before = jnp.maximum(step - 1, 0)
        for tile in range(2):
            expand_stored(0, tile, before)
        gather(0, pair)
        spread_taps(0, step, 9, 27)

    copies[2].wait()
    copies[3].wait()
    early[1].wait()
    early[3].wait()
    for copy in late:
        copy.start()
    stage(0, 0, filler(lambda pair: gather(2, pair), lambda pair: expand_stored(0, 2, pair)))
    stage(0, 1, filler(lambda pair: reduce_store(0, pair), lambda pair: expand_stored(1, 0, pair)))
    stage(0, 2, filler(lambda pair: reduce_store(1, pair), lambda pair: expand_stored(1, 1, pair)))
    stage(1, 0, filler(lambda pair: reduce_store(2, pair), lambda pair: expand_stored(1, 2, pair)))
    stage(1, 1, lambda pair, before, live: reduce_pool(0, pair, live))
    stage(1, 2, lambda pair, before, live: reduce_pool(1, pair, live))

    @pl.loop(0, SPOTS // 2)
    def _(pair):
        reduce_pool(2, pair, 1.0)

    late[0].wait()
    small = identity(256)
    for part in range(flip_ref.shape[0] // 256):
        part = slice(part * 256, (part + 1) * 256)
        flip_ref[part, :] = turn(small, head_ref[:, part]).astype(BF)
    packed = packed_pool_ref[...]
    total = (
        pool_ref[...]
        + jnp.where(row_lane < n2, packed, 0.0)
        + jnp.where(row_lane < n3, pltpu.roll(packed, clips - n2, 1), 0.0)
    )
    lengths = jnp.dot(
        jnp.broadcast_to(counts, (16, clips)).astype(BF), order, preferred_element_type=F32
    )[0:1]
    pooled = (total / (lengths * SPOTS)).astype(BF)
    n_dp, per_peer = out_ref.shape[0], out_ref.shape[1]
    slot = (line % per_peer) * n_dp + line // per_peer
    pick = one_hot(jnp.broadcast_to(send_ref[...], (clips, clips)) == slot)
    pick = lax.dot_general(pick, order, (((1,), (0,)), ((), ())), preferred_element_type=F32).astype(BF)
    rows = lax.dot_general(pick, pooled, (((1,), (1,)), ((), ())), preferred_element_type=F32)
    out_ref[:, :, :channels] = rows.astype(BF).reshape(n_dp, per_peer, channels)
    out_ref[:, :, channels:] = jnp.zeros((n_dp, per_peer, out_ref.shape[2] - channels), BF)
    late[1].wait()


def embed(
    clip_data, frame_counts, send_list, expand_weight, depth_kernel, reduce_weight, head_weight, centroids, n_dp
):
    clips, frames, spots, channels = clip_data.shape
    expanded = expand_weight.shape[2]
    dims = head_weight.shape[1]
    stored = pl.BlockSpec(memory_space=pltpu.HBM)
    local_ref = pl.BlockSpec(memory_space=pltpu.VMEM)
    return pl.pallas_call(
        embed_kernel,
        out_shape=(
            jax.ShapeDtypeStruct((n_dp, clips // n_dp, 256), BF),
            pltpu.VMEM(centroids.shape, BF),
            pltpu.VMEM(head_weight.shape, BF),
            pltpu.VMEM((dims, channels), BF),
        ),
        in_specs=[stored] * 4 + [local_ref] + [stored] * 3,
        out_specs=(local_ref,) * 4,
        scratch_shapes=[pltpu.VMEM((spots, channels, clips), BF)] * 6
        + [pltpu.VMEM((spots, expanded, clips), F32)] * 4
        + [pltpu.VMEM((spots, expanded, clips), BF)] * 3
        + [pltpu.VMEM((channels, clips), F32)] * 2
        + [pltpu.VMEM((expanded // 16, 27, 16, clips), F32)] * 2
        + [pltpu.VMEM((2, expanded, channels), BF), pltpu.VMEM((2, expanded, clips), F32)]
        + [pltpu.VMEM((frames, spots, channels, clips), BF), pltpu.SemaphoreType.DMA((frames,))]
        + [pltpu.VMEM((1, clips), jnp.int32)] * 2
        + [
            pltpu.VMEM((2, channels, expanded), BF),
            pltpu.VMEM((2, channels, expanded), BF),
            pltpu.SemaphoreType.DMA((6,)),
        ],
        compiler_params=pltpu.CompilerParams(vmem_limit_bytes=48 << 20),
        name="embed",
    )(
        jnp.transpose(clip_data, (1, 2, 3, 0)),
        frame_counts,
        send_list,
        expand_weight,
        jnp.transpose(depth_kernel, (1, 0, 2)),
        jnp.swapaxes(reduce_weight, 1, 2),
        head_weight,
        centroids,
    )


def unit(projected, axis):
    square = jnp.sum(projected * projected, axis=axis, keepdims=True)
    return (projected * lax.rsqrt(square + 1e-06)).astype(BF)


LABEL_ROWS = 16


def own_kernel(arrived_ref, ids_ref, payload_ref, rows_ref):
    n_dp, per_peer, width = arrived_ref.shape
    clips = n_dp * per_peer
    channels = rows_ref.shape[1]
    arrived = arrived_ref[...].reshape(clips, width)[:, :channels]
    row = lax.broadcasted_iota(jnp.int32, (clips, clips), 0)
    lane = lax.broadcasted_iota(jnp.int32, (clips, clips), 1)
    pick = (lane == (row % n_dp) * per_peer + row // n_dp).astype(F32).astype(BF)
    rows = jnp.dot(pick, arrived, preferred_element_type=F32)
    rows_ref[...] = rows.astype(BF)
    ids = ids_ref[...]
    which = lax.broadcasted_iota(jnp.int32, (LABEL_ROWS, clips), 0)
    high, low = ids // 256, ids % 256
    label = jnp.where(which == 0, high, jnp.where(which == 1, low, 0))
    payload = jnp.concatenate([jnp.transpose(rows), label.astype(F32)], axis=0).astype(BF)
    payload_ref[...] = payload


def own(arrived, cluster_ids, channels):
    n_dp, per_peer, width = arrived.shape
    clips = n_dp * per_peer
    height = channels + LABEL_ROWS
    return pl.pallas_call(
        own_kernel,
        out_shape=(
            jax.ShapeDtypeStruct((height, clips), BF),
            jax.ShapeDtypeStruct((clips, channels), BF),
        ),
        in_specs=[pl.BlockSpec(memory_space=pltpu.VMEM)] * 2,
        out_specs=(pl.BlockSpec(memory_space=pltpu.VMEM),) * 2,
        compiler_params=pltpu.CompilerParams(vmem_limit_bytes=8 << 20),
        name="own",
    )(arrived, cluster_ids)


def vectors_kernel(rows_ref, head_ref, vectors_ref):
    projected = jnp.dot(rows_ref[...], head_ref[...], preferred_element_type=F32)
    vectors_ref[...] = unit(projected, 1)


def vectors_of(rows, head_weight):
    clips, channels = rows.shape
    dims = head_weight.shape[1]
    return pl.pallas_call(
        vectors_kernel,
        out_shape=jax.ShapeDtypeStruct((clips, dims), BF),
        in_specs=[pl.BlockSpec(memory_space=pltpu.VMEM)] * 2,
        out_specs=pl.BlockSpec(memory_space=pltpu.VMEM),
        compiler_params=pltpu.CompilerParams(vmem_limit_bytes=8 << 20),
        cost_estimate=pl.CostEstimate(
            flops=2 * clips * dims * channels, bytes_accessed=2 * dims * (clips + channels), transcendentals=0
        ),
        name="vectors",
    )(rows, head_weight)


PANEL_ROWS = 784
OCCUR = 64
LEFT = 2


def label_of(rows_ref, block, channels):
    label = jnp.concatenate(
        [rows_ref[2 * block, channels:, :], rows_ref[2 * block + 1, channels:, :]], axis=1
    ).astype(F32)
    return label[0:1] * 256.0 + label[1:2]


def score_rows(
    rows_ref, flip_ref, panel_ref, turned_ref, near_ref, own_ref, best_ref, line_ref, send_turned, arrive, extra
):
    blocks, height, clips = rows_ref.shape
    channels = flip_ref.shape[1]
    panel_rows = panel_ref.shape[0] // 8 * 8

    @pl.loop(0, blocks // 2)
    def _(pair):
        both = jnp.concatenate([rows_ref[2 * pair], rows_ref[2 * pair + 1]], axis=1)
        parts = [slice(at, at + 256) for at in range(0, flip_ref.shape[0], 256)]
        square = jnp.zeros((8, 2 * clips), F32)
        for part in parts:
            projected = jnp.dot(flip_ref[part, :], both[:channels], preferred_element_type=F32)
            line_ref[part, :] = projected
            square += jnp.sum((projected * projected).reshape(32, 8, 2 * clips), axis=0)
        scale = lax.rsqrt(jnp.sum(square, axis=0, keepdims=True) + 1e-06)
        for part in parts:
            turned_ref[pair, part, :] = (line_ref[part, :] * scale).astype(BF)
        best_ref[pair] = jnp.dot(extra, turned_ref[pair], preferred_element_type=F32)

    send_turned()
    base = lax.axis_index("cent") * (panel_rows + LEFT)
    for step in range(pl.cdiv(panel_rows, PANEL_ROWS)):
        arrive(step)
        rows = slice(step * PANEL_ROWS, min(panel_rows, (step + 1) * PANEL_ROWS))

        @pl.loop(0, blocks // 2)
        def _(pair):
            scores = jnp.dot(panel_ref[rows, :], turned_ref[pair], preferred_element_type=F32)
            best_ref[pair] = jnp.maximum(
                best_ref[pair], jnp.max(scores.reshape((rows.stop - rows.start) // 8, 8, 2 * clips), axis=0)
            )
            if step == 0:
                local_id = label_of(rows_ref, pair, channels).astype(jnp.int32) - base
                index = lax.broadcasted_iota(jnp.int32, (OCCUR, 2 * clips), 0)
                own_ref[pair] = jnp.max(
                    jnp.where(index == local_id, scores[:OCCUR], -jnp.inf), axis=0, keepdims=True
                )

    for pair in range(blocks // 2):
        near_ref[pair] = jnp.max(best_ref[pair], axis=0, keepdims=True)


def near_kernel(
    rows_ref, flip_ref, panel_ref, turned_hbm, near_ref, own_ref, spread_hbm, extra_ref, turned_ref, best_ref, line_ref, done,
    spread_done,
):
    sends = [
        pltpu.make_async_copy(rows_ref.at[0], spread_hbm.at[peer], spread_done.at[peer])
        for peer in range(spread_hbm.shape[0])
    ]
    for send in sends:
        send.start()
    panel_rows = panel_ref.shape[0]
    left = panel_ref[panel_rows - LEFT : panel_rows, :]
    extra = jnp.concatenate([left] * (8 // LEFT), axis=0)
    extra_ref[...] = extra
    copy = pltpu.make_async_copy(turned_ref, turned_hbm, done)
    score_rows(
        rows_ref, flip_ref, panel_ref, turned_ref, near_ref, own_ref, best_ref, line_ref,
        copy.start, lambda step: None, extra
    )
    for send in sends:
        send.wait()
    copy.wait()


def far_kernel(
    rows_ref, flip_ref, stored_ref, extra_ref, turned_hbm, near_ref, own_ref, turned_ref, best_ref, line_ref, done,
    panel_ref, arrival,
):
    copies = []
    for step in range(arrival.shape[0]):
        rows = slice(step * PANEL_ROWS, min(panel_ref.shape[0], (step + 1) * PANEL_ROWS))
        copies.append(pltpu.make_async_copy(stored_ref.at[rows], panel_ref.at[rows], arrival.at[step]))
        copies[-1].start()
    copy = pltpu.make_async_copy(turned_ref, turned_hbm, done)
    score_rows(
        rows_ref, flip_ref, panel_ref, turned_ref, near_ref, own_ref, best_ref, line_ref,
        copy.start, lambda step: copies[step].wait(), extra_ref[...],
    )
    copy.wait()


def scored(kernel, name, rows, flip, panel, limit, spread=None, extra=None):
    blocks, height, clips = rows.shape
    dims, channels = flip.shape
    pairs, width = blocks // 2, 2 * clips
    panel_rows = panel.shape[0]
    here = pl.BlockSpec(memory_space=pltpu.VMEM)
    stored = pl.BlockSpec(memory_space=pltpu.HBM)
    shapes = [
        pltpu.HBM((pairs, dims, width), BF),
        jax.ShapeDtypeStruct((pairs, 1, width), F32),
        jax.ShapeDtypeStruct((pairs, 1, width), F32),
    ]
    scratch = [
        pltpu.VMEM((pairs, dims, width), BF),
        pltpu.VMEM((pairs, 8, width), F32),
        pltpu.VMEM((dims, width), F32),
        pltpu.SemaphoreType.DMA(()),
    ]
    if spread is None:
        even = panel_rows // 8 * 8
        scratch += [
            pltpu.VMEM((even, dims), BF), pltpu.SemaphoreType.DMA((pl.cdiv(even, PANEL_ROWS),))
        ]
    else:
        assert panel_rows % 8 == LEFT
        scratch.append(pltpu.SemaphoreType.DMA((spread,)))
        shapes.append(pltpu.HBM((spread, height, clips), BF))
        shapes.append(jax.ShapeDtypeStruct((8, dims), BF))
    return pl.pallas_call(
        kernel,
        out_shape=shapes,
        in_specs=[here, here] + ([stored, here] if spread is None else [here]),
        out_specs=[stored, here, here] + ([] if spread is None else [stored, here]),
        scratch_shapes=scratch,
        compiler_params=pltpu.CompilerParams(vmem_limit_bytes=limit << 20),
        cost_estimate=pl.CostEstimate(
            flops=2 * blocks * clips * panel_rows * dims, bytes_accessed=2 * panel_rows * dims, transcendentals=0
        ),
        name=name,
    )(rows, flip, panel, *([extra] if spread is None else []))


GROUP = 4


def peer_kernel(
    near_rows_ref, near_turned_ref, near_best_ref, near_own_ref, far_rows_ref, far_turned_hbm, far_best_ref, far_own_ref,
    cols_ref, head_ref, out_ref, far_turned_ref, best_ref, arrival,
):
    far_copy = pltpu.make_async_copy(far_turned_hbm, far_turned_ref, arrival)
    far_copy.start()
    n_dp, height, clips = cols_ref.shape
    n_cent = out_ref.shape[0]
    channels = head_ref.shape[0]
    eye = identity(clips)
    best_ref[...] = jnp.full_like(best_ref, -1.0)
    mine_dp, mine_cent = lax.axis_index("dp"), lax.axis_index("cent")

    def visit(group, first):
        flipped = jnp.concatenate([turn(eye, cols_ref[group * GROUP + at]) for at in range(GROUP)], axis=0)
        projected = jnp.dot(flipped[:, :channels].astype(BF), head_ref[...], preferred_element_type=F32)
        vectors = unit(projected, 1)
        ids = flipped[:, channels : channels + 1] * 256.0 + flipped[:, channels + 1 : channels + 2]
        wide = jnp.broadcast_to(ids, (GROUP * clips, 2 * clips))
        for block in range(n_cent // 2):
            cols = slice(block * 2 * clips, (block + 1) * 2 * clips)
            if first and block == 1:
                far_copy.wait()
            if block == 0:
                turned, row_ids = near_turned_ref[0], label_of(near_rows_ref, 0, channels)
            else:
                turned, row_ids = far_turned_ref[block - 1], label_of(far_rows_ref, block - 1, channels)
            scores = jnp.dot(vectors, turned, preferred_element_type=F32)
            same = wide == row_ids
            if block == 0:
                line = lax.broadcasted_iota(jnp.int32, same.shape, 0)
                lane = lax.broadcasted_iota(jnp.int32, same.shape, 1)
                itself = jnp.where(lane < clips, lane + (mine_dp - group * GROUP) * clips, -1)
                same = same & (line != itself)
            found = jnp.where(same, scores, -1.0)
            best_ref[:, cols] = jnp.maximum(
                best_ref[:, cols], jnp.max(found.reshape(GROUP * clips // 8, 8, 2 * clips), axis=0)
            )

    visit(0, True)

    @pl.loop(1, n_dp // GROUP)
    def _(group):
        visit(group, False)

    best = jnp.max(best_ref[...], axis=0, keepdims=True)
    for block in range(n_cent // 2):
        for side in range(2):
            chip = (mine_cent // 2 + block) % (n_cent // 2)
            cent = 2 * chip + (mine_cent + side) % 2
            at = slice((2 * block + side) * clips, (2 * block + side + 1) * clips)
            part = slice(side * clips, (side + 1) * clips)
            if block == 0:
                nearest, own_best = near_best_ref[0, :, part], near_own_ref[0, :, part]
            else:
                nearest, own_best = far_best_ref[block - 1, :, part], far_own_ref[block - 1, :, part]
            out_ref[cent, 0:1, :] = nearest
            out_ref[cent, 1:2, :] = own_best
            out_ref[cent, 2:3, :] = best[:, at]
            out_ref[cent, 3:4, :] = best[:, at]


def peers_of(near_rows, near_found, far_rows, far_found, cols, head_weight):
    n_dp, height, clips = cols.shape
    n_cent = near_rows.shape[0] + far_rows.shape[0]
    dims = head_weight.shape[1]
    here = pl.BlockSpec(memory_space=pltpu.VMEM)
    stored = pl.BlockSpec(memory_space=pltpu.HBM)
    far_found = [pltpu.with_memory_space_constraint(far_found[0], pltpu.HBM), *far_found[1:]]
    return pl.pallas_call(
        peer_kernel,
        out_shape=jax.ShapeDtypeStruct((n_cent, 4, clips), F32),
        in_specs=[here] * 5 + [stored] + [here] * 4,
        out_specs=here,
        scratch_shapes=[
            pltpu.VMEM(far_found[0].shape, BF),
            pltpu.VMEM((8, n_cent * clips), F32),
            pltpu.SemaphoreType.DMA(()),
        ],
        compiler_params=pltpu.CompilerParams(vmem_limit_bytes=16 << 20),
        cost_estimate=pl.CostEstimate(
            flops=2 * n_dp * n_cent * clips * clips * dims, bytes_accessed=4 << 20, transcendentals=0
        ),
        name="peers",
    )(near_rows, *near_found, far_rows, *far_found, cols, head_weight)


def local(
    clip_data,
    frame_counts,
    send_list,
    cluster_ids,
    expand_weight,
    depth_kernel,
    reduce_weight,
    head_weight,
    centroids,
):
    n_dp = lax.axis_size("dp")
    n_cent = lax.axis_size("cent")
    pooled, panel, head, flip = embed(
        clip_data, frame_counts, send_list, expand_weight, depth_kernel, reduce_weight, head_weight, centroids, n_dp
    )
    arrived = lax.all_to_all(pooled, "dp", split_axis=0, concat_axis=0, tiled=True)
    payload, rows = own(arrived, cluster_ids, head_weight.shape[0])
    partner = lax.ppermute(payload, "cent", [(at, at ^ 1) for at in range(n_cent)])
    near_rows = jnp.stack([payload, partner])
    far_rows = jnp.concatenate(
        [
            lax.ppermute(near_rows, "cent", [((at + 2 * chip) % n_cent, at) for at in range(n_cent)])
            for chip in range(1, n_cent // 2)
        ]
    )
    *near_found, spread, extra = scored(near_kernel, "near", near_rows, flip, panel, 16, n_dp)
    cols = lax.all_to_all(spread, "dp", split_axis=0, concat_axis=0, tiled=True)
    vectors = vectors_of(rows, head)
    far_found = scored(
        far_kernel, "far", far_rows, flip, pltpu.with_memory_space_constraint(centroids, pltpu.HBM), 32, extra=extra
    )
    partial = peers_of(near_rows, near_found, far_rows, far_found, cols, head)
    parts = lax.all_to_all(partial, "cent", split_axis=0, concat_axis=0, tiled=True)
    final = jnp.max(parts, axis=0)
    return (vectors, final[0], final[1], final[2])


def solution(mesh):
    placed = (
        P(("dp", "cent"), None, None, None),
        P(("dp", "cent"), None),
        P(("dp", "cent"), None),
        P(("dp", "cent"), None),
        P(),
        P(),
        P(),
        P(),
        P("cent", None),
    )
    return jax.shard_map(
        local,
        mesh=mesh,
        in_specs=placed,
        out_specs=(
            P(("dp", "cent"), None),
            P(("dp", "cent")),
            P(("dp", "cent")),
            P(("dp", "cent")),
        ),
        check_vma=False,
    )
```

```python
import functools

import jax
import jax.numpy as jnp
from jax import lax
from jax.experimental import pallas as pl
from jax.experimental.pallas import tpu as pltpu
from jax.sharding import PartitionSpec as P

SIDE = 4
SPOTS = SIDE * SIDE
BF = jnp.bfloat16
F32 = jnp.float32


def neighbours(at, extent):
    return [(at + shift - 1, shift) for shift in range(3) if 0 <= at + shift - 1 < extent]


STEPS = 9


def identity(size):
    line = lax.broadcasted_iota(jnp.int32, (size, size), 0)
    lane = lax.broadcasted_iota(jnp.int32, (size, size), 1)
    return (line == lane).astype(F32).astype(BF)


def turn(eye, matrix):
    return lax.dot_general(eye, matrix, (((1,), (1,)), ((), ())), preferred_element_type=F32)


def embed_kernel(
    stored_ref, counts_hbm, send_hbm, wide_hbm, taps_ref, reduce_hbm, head_hbm, panel_hbm,
    out_ref, panel_ref, head_ref, flip_ref, *scratch,
):
    x_refs, act_refs = scratch[0:6], scratch[10:13]
    hidden_refs = scratch[6:10] + scratch[6:8]
    pool_ref, packed_pool_ref = scratch[13:15]
    weight_refs = scratch[15:17]
    expand_ref, depth_ref, clip_ref, arrival = scratch[17:21]
    count_ref, send_ref, wide_ref, reduce_ref, ready = scratch[21:26]
    channels, clips = clip_ref.shape[2], clip_ref.shape[3]
    early = [
        pltpu.make_async_copy(source, target, ready.at[at])
        for at, (source, target) in enumerate(
            [(counts_hbm, count_ref), (send_hbm, send_ref), (wide_hbm, wide_ref), (reduce_hbm, reduce_ref)]
        )
    ]
    late = [
        pltpu.make_async_copy(source, target, ready.at[4 + at])
        for at, (source, target) in enumerate([(head_hbm, head_ref), (panel_hbm, panel_ref)])
    ]
    early[0].start()
    early[2].start()
    copies = [
        pltpu.make_async_copy(stored_ref.at[frame], clip_ref.at[frame], arrival.at[frame])
        for frame in range(clip_ref.shape[0])
    ]
    copies[0].start()
    copies[1].start()
    expanded = wide_ref.shape[2]
    eye = identity(expanded)
    early[0].wait()
    early[2].wait()
    for layer in range(2):
        expand_ref[layer] = turn(eye, wide_ref[layer]).astype(BF)
        depth_ref[layer, :, : taps_ref.shape[0]] = turn(eye, taps_ref[:, layer, :])

    counts = count_ref[...].astype(F32)
    line = lax.broadcasted_iota(jnp.int32, (clips, clips), 0)
    lane = lax.broadcasted_iota(jnp.int32, (clips, clips), 1)
    count_lane = jnp.broadcast_to(counts, (clips, clips))
    count_line = jnp.transpose(count_lane)
    ahead = (count_lane > count_line) | ((count_lane == count_line) & (lane < line))
    rank = jnp.dot(
        ahead.astype(F32).astype(BF), jnp.ones((clips, clips), BF), preferred_element_type=F32
    ).astype(jnp.int32)
    n1, n2, n3 = [jnp.sum((counts > frame).astype(jnp.int32)) for frame in (1, 2, 3)]
    blocks = expanded // 16 // STEPS
    one_hot = lambda mask: mask.astype(F32).astype(BF)
    order = one_hot(rank == lane)
    none = jnp.zeros((clips, clips), BF)
    place = [
        jnp.concatenate(
            [
                jnp.concatenate([order, none], axis=1),
                jnp.concatenate([none, one_hot((rank == lane) & (count_line > 1))], axis=1),
            ],
            axis=0,
        ),
        jnp.concatenate(
            [
                one_hot((rank == lane) & (count_line > 2)),
                one_hot((rank + n2 == lane) & (count_line > 3)),
            ],
            axis=0,
        ),
    ]
    row_lane = lax.broadcasted_iota(jnp.int32, (1, clips), 1)
    kept = [None, (row_lane < n1).astype(F32), (row_lane < n2 + n3).astype(F32)]
    tile_lane = lax.broadcasted_iota(jnp.int32, (16, clips), 1)
    in_second, in_third = tile_lane < n2, tile_lane < n3

    def expand(layer, tile, pair, both):
        hidden = jnp.maximum(jnp.dot(expand_ref[layer], both, preferred_element_type=F32), 0.0)
        hidden_refs[3 * layer + tile][2 * pair] = hidden[:, :clips]
        hidden_refs[3 * layer + tile][2 * pair + 1] = hidden[:, clips:]

    def gather(first, pair):
        spots = jnp.concatenate(
            [
                jnp.concatenate([clip_ref[first, 2 * pair + side], clip_ref[first + 1, 2 * pair + side]], axis=1)
                for side in range(2)
            ],
            axis=0,
        )
        x = jnp.dot(spots, place[first // 2], preferred_element_type=F32).astype(BF)
        for side in range(2):
            rows = slice(side * channels, (side + 1) * channels)
            for at in range(x.shape[1] // clips):
                x_refs[first + at][2 * pair + side] = x[rows, at * clips : (at + 1) * clips]

    def expand_stored(layer, tile, pair):
        x_ref = x_refs[3 * layer + tile]
        expand(layer, tile, pair, jnp.concatenate([x_ref[2 * pair], x_ref[2 * pair + 1]], axis=1))

    def spread_taps(layer, step, first, last):
        rows = [pl.ds(pl.multiple_of((step * blocks + at) * 16, 16), 16) for at in range(blocks)]
        taps = [depth_ref[layer, row, :] for row in rows]
        for tap in range(first, last):
            for at in range(blocks):
                weight_refs[layer][step * blocks + at, tap] = jnp.broadcast_to(
                    taps[at][:, tap : tap + 1], (16, clips)
                )

    def reduce(layer, tile, pair):
        both = jnp.concatenate([act_refs[tile][2 * pair], act_refs[tile][2 * pair + 1]], axis=1)
        branch = jnp.dot(reduce_ref[layer], both, preferred_element_type=F32)
        result = []
        for side in range(2):
            part = branch[:, side * clips : (side + 1) * clips]
            if kept[tile] is not None:
                part = part * kept[tile]
            x = x_refs[3 * layer + tile][2 * pair + side].astype(F32) + part
            result.append(x.astype(BF))
        return result

    def reduce_store(tile, pair):
        x = reduce(0, tile, pair)
        x_refs[3 + tile][2 * pair] = x[0]
        x_refs[3 + tile][2 * pair + 1] = x[1]

    def reduce_pool(tile, pair, live):
        x = reduce(1, tile, pair)
        into = packed_pool_ref if tile == 2 else pool_ref
        into[...] += (x[0].astype(F32) + x[1].astype(F32)) * live

    def depthwise(layer, tile, block):
        rows = pl.ds(pl.multiple_of(block * 16, 16), 16)
        read = lambda source, spot: hidden_refs[3 * layer + source][spot, rows, :]
        if tile == 0:
            sources = [(1, lambda s: read(0, s)), (2, lambda s: read(1, s))]
        elif tile == 1:
            sources = [
                (0, lambda s: read(0, s)),
                (1, lambda s: read(1, s)),
                (2, lambda s: jnp.where(in_second, read(2, s), 0.0)),
            ]
        else:
            sources = [
                (0, lambda s: jnp.where(in_second, read(1, s), pltpu.roll(read(2, s), n2, 1))),
                (1, lambda s: read(2, s)),
                (2, lambda s: jnp.where(in_third, pltpu.roll(read(2, s), clips - n2, 1), 0.0)),
            ]
        mixed = [None] * SPOTS
        for shift_t, source in sources:
            weight = [weight_refs[layer][block, 9 * shift_t + tap].astype(BF) for tap in range(9)]
            hidden = [source(spot).astype(BF) for spot in range(SPOTS)]
            for y in range(SIDE):
                for from_y, shift_y in neighbours(y, SIDE):
                    for z in range(SIDE):
                        for from_z, shift_z in neighbours(z, SIDE):
                            term = hidden[from_y * SIDE + from_z] * weight[3 * shift_y + shift_z]
                            spot = y * SIDE + z
                            mixed[spot] = term if mixed[spot] is None else mixed[spot] + term
        for spot in range(SPOTS):
            half = mixed[spot] * BF(0.5)
            act_refs[tile][spot, rows, :] = half + half * jnp.tanh(half)

    def stage(layer, tile, other):
        @pl.loop(0, STEPS)
        def _(step):
            pair = jnp.minimum(step, SPOTS // 2 - 1)
            before = jnp.maximum(step - 1, 0)
            other(pair, before, (step < SPOTS // 2).astype(F32))
            if layer == 0:
                if tile == 0:
                    spread_taps(0, step, 0, 9)
                spread_taps(1, step, 9 * tile, 9 * tile + 9)
            for at in range(blocks):
                depthwise(layer, tile, step * blocks + at)

    def filler(first, second):
        def other(pair, before, live):
            second(before)
            first(pair)

        return other

    pool_ref[...] = jnp.zeros_like(pool_ref)
    packed_pool_ref[...] = jnp.zeros_like(packed_pool_ref)
    copies[0].wait()
    copies[1].wait()
    for copy in (copies[2], copies[3], early[1], early[3]):
        copy.start()

    @pl.loop(0, STEPS)
    def _(step):
        pair = jnp.minimum(step, SPOTS // 2 - 1)
        before = jnp.maximum(step - 1, 0)
        for tile in range(2):
            expand_stored(0, tile, before)
        gather(0, pair)
        spread_taps(0, step, 9, 27)

    copies[2].wait()
    copies[3].wait()
    early[1].wait()
    early[3].wait()
    for copy in late:
        copy.start()
    stage(0, 0, filler(lambda pair: gather(2, pair), lambda pair: expand_stored(0, 2, pair)))
    stage(0, 1, filler(lambda pair: reduce_store(0, pair), lambda pair: expand_stored(1, 0, pair)))
    stage(0, 2, filler(lambda pair: reduce_store(1, pair), lambda pair: expand_stored(1, 1, pair)))
    stage(1, 0, filler(lambda pair: reduce_store(2, pair), lambda pair: expand_stored(1, 2, pair)))
    stage(1, 1, lambda pair, before, live: reduce_pool(0, pair, live))
    stage(1, 2, lambda pair, before, live: reduce_pool(1, pair, live))

    @pl.loop(0, SPOTS // 2)
    def _(pair):
        reduce_pool(2, pair, 1.0)

    late[0].wait()
    small = identity(256)
    for part in range(flip_ref.shape[0] // 256):
        part = slice(part * 256, (part + 1) * 256)
        flip_ref[part, :] = turn(small, head_ref[:, part]).astype(BF)
    packed = packed_pool_ref[...]
    total = (
        pool_ref[...]
        + jnp.where(row_lane < n2, packed, 0.0)
        + jnp.where(row_lane < n3, pltpu.roll(packed, clips - n2, 1), 0.0)
    )
    lengths = jnp.dot(
        jnp.broadcast_to(counts, (16, clips)).astype(BF), order, preferred_element_type=F32
    )[0:1]
    pooled = (total / (lengths * SPOTS)).astype(BF)
    n_dp, per_peer = out_ref.shape[0], out_ref.shape[1]
    slot = (line % per_peer) * n_dp + line // per_peer
    pick = one_hot(jnp.broadcast_to(send_ref[...], (clips, clips)) == slot)
    pick = lax.dot_general(pick, order, (((1,), (0,)), ((), ())), preferred_element_type=F32).astype(BF)
    rows = lax.dot_general(pick, pooled, (((1,), (1,)), ((), ())), preferred_element_type=F32)
    out_ref[:, :, :channels] = rows.astype(BF).reshape(n_dp, per_peer, channels)
    out_ref[:, :, channels:] = jnp.zeros((n_dp, per_peer, out_ref.shape[2] - channels), BF)
    late[1].wait()


def embed(
    clip_data, frame_counts, send_list, expand_weight, depth_kernel, reduce_weight, head_weight, centroids, n_dp
):
    clips, frames, spots, channels = clip_data.shape
    expanded = expand_weight.shape[2]
    dims = head_weight.shape[1]
    stored = pl.BlockSpec(memory_space=pltpu.HBM)
    local_ref = pl.BlockSpec(memory_space=pltpu.VMEM)
    return pl.pallas_call(
        embed_kernel,
        out_shape=(
            jax.ShapeDtypeStruct((n_dp, clips // n_dp, 256), BF),
            pltpu.VMEM(centroids.shape, BF),
            pltpu.VMEM(head_weight.shape, BF),
            pltpu.VMEM((dims, channels), BF),
        ),
        in_specs=[stored] * 4 + [local_ref] + [stored] * 3,
        out_specs=(local_ref,) * 4,
        scratch_shapes=[pltpu.VMEM((spots, channels, clips), BF)] * 6
        + [pltpu.VMEM((spots, expanded, clips), F32)] * 4
        + [pltpu.VMEM((spots, expanded, clips), BF)] * 3
        + [pltpu.VMEM((channels, clips), F32)] * 2
        + [pltpu.VMEM((expanded // 16, 27, 16, clips), F32)] * 2
        + [pltpu.VMEM((2, expanded, channels), BF), pltpu.VMEM((2, expanded, clips), F32)]
        + [pltpu.VMEM((frames, spots, channels, clips), BF), pltpu.SemaphoreType.DMA((frames,))]
        + [pltpu.VMEM((1, clips), jnp.int32)] * 2
        + [
            pltpu.VMEM((2, channels, expanded), BF),
            pltpu.VMEM((2, channels, expanded), BF),
            pltpu.SemaphoreType.DMA((6,)),
        ],
        compiler_params=pltpu.CompilerParams(vmem_limit_bytes=48 << 20),
        name="embed",
    )(
        jnp.transpose(clip_data, (1, 2, 3, 0)),
        frame_counts,
        send_list,
        expand_weight,
        jnp.transpose(depth_kernel, (1, 0, 2)),
        jnp.swapaxes(reduce_weight, 1, 2),
        head_weight,
        centroids,
    )


def unit(projected, axis):
    square = jnp.sum(projected * projected, axis=axis, keepdims=True)
    return (projected * lax.rsqrt(square + 1e-06)).astype(BF)


LABEL_ROWS = 16


def own_kernel(arrived_ref, ids_ref, payload_ref, rows_ref):
    n_dp, per_peer, width = arrived_ref.shape
    clips = n_dp * per_peer
    channels = rows_ref.shape[1]
    arrived = arrived_ref[...].reshape(clips, width)[:, :channels]
    row = lax.broadcasted_iota(jnp.int32, (clips, clips), 0)
    lane = lax.broadcasted_iota(jnp.int32, (clips, clips), 1)
    pick = (lane == (row % n_dp) * per_peer + row // n_dp).astype(F32).astype(BF)
    rows = jnp.dot(pick, arrived, preferred_element_type=F32)
    rows_ref[...] = rows.astype(BF)
    ids = ids_ref[...]
    which = lax.broadcasted_iota(jnp.int32, (LABEL_ROWS, clips), 0)
    high, low = ids // 256, ids % 256
    label = jnp.where(which == 0, high, jnp.where(which == 1, low, 0))
    payload = jnp.concatenate([jnp.transpose(rows), label.astype(F32)], axis=0).astype(BF)
    payload_ref[...] = payload


def own(arrived, cluster_ids, channels):
    n_dp, per_peer, width = arrived.shape
    clips = n_dp * per_peer
    height = channels + LABEL_ROWS
    return pl.pallas_call(
        own_kernel,
        out_shape=(
            jax.ShapeDtypeStruct((height, clips), BF),
            jax.ShapeDtypeStruct((clips, channels), BF),
        ),
        in_specs=[pl.BlockSpec(memory_space=pltpu.VMEM)] * 2,
        out_specs=(pl.BlockSpec(memory_space=pltpu.VMEM),) * 2,
        compiler_params=pltpu.CompilerParams(vmem_limit_bytes=8 << 20),
        name="own",
    )(arrived, cluster_ids)


def vectors_kernel(rows_ref, head_ref, vectors_ref):
    projected = jnp.dot(rows_ref[...], head_ref[...], preferred_element_type=F32)
    vectors_ref[...] = unit(projected, 1)


def vectors_of(rows, head_weight):
    clips, channels = rows.shape
    dims = head_weight.shape[1]
    return pl.pallas_call(
        vectors_kernel,
        out_shape=jax.ShapeDtypeStruct((clips, dims), BF),
        in_specs=[pl.BlockSpec(memory_space=pltpu.VMEM)] * 2,
        out_specs=pl.BlockSpec(memory_space=pltpu.VMEM),
        compiler_params=pltpu.CompilerParams(vmem_limit_bytes=8 << 20),
        cost_estimate=pl.CostEstimate(
            flops=2 * clips * dims * channels, bytes_accessed=2 * dims * (clips + channels), transcendentals=0
        ),
        name="vectors",
    )(rows, head_weight)


PANEL_ROWS = 784
OCCUR = 64
LEFT = 2


def label_of(rows_ref, block, channels):
    label = jnp.concatenate(
        [rows_ref[2 * block, channels:, :], rows_ref[2 * block + 1, channels:, :]], axis=1
    ).astype(F32)
    return label[0:1] * 256.0 + label[1:2]


def score_rows(
    rows_ref, flip_ref, panel_ref, turned_ref, near_ref, own_ref, best_ref, line_ref, send_turned, arrive, extra
):
    blocks, height, clips = rows_ref.shape
    channels = flip_ref.shape[1]
    panel_rows = panel_ref.shape[0] // 8 * 8

    @pl.loop(0, blocks // 2)
    def _(pair):
        both = jnp.concatenate([rows_ref[2 * pair], rows_ref[2 * pair + 1]], axis=1)
        parts = [slice(at, at + 256) for at in range(0, flip_ref.shape[0], 256)]
        square = jnp.zeros((8, 2 * clips), F32)
        for part in parts:
            projected = jnp.dot(flip_ref[part, :], both[:channels], preferred_element_type=F32)
            line_ref[part, :] = projected
            square += jnp.sum((projected * projected).reshape(32, 8, 2 * clips), axis=0)
        scale = lax.rsqrt(jnp.sum(square, axis=0, keepdims=True) + 1e-06)
        for part in parts:
            turned_ref[pair, part, :] = (line_ref[part, :] * scale).astype(BF)
        best_ref[pair] = jnp.dot(extra, turned_ref[pair], preferred_element_type=F32)

    send_turned()
    base = lax.axis_index("cent") * (panel_rows + LEFT)
    for step in range(pl.cdiv(panel_rows, PANEL_ROWS)):
        arrive(step)
        rows = slice(step * PANEL_ROWS, min(panel_rows, (step + 1) * PANEL_ROWS))

        @pl.loop(0, blocks // 2)
        def _(pair):
            scores = jnp.dot(panel_ref[rows, :], turned_ref[pair], preferred_element_type=F32)
            best_ref[pair] = jnp.maximum(
                best_ref[pair], jnp.max(scores.reshape((rows.stop - rows.start) // 8, 8, 2 * clips), axis=0)
            )
            if step == 0:
                local_id = label_of(rows_ref, pair, channels).astype(jnp.int32) - base
                index = lax.broadcasted_iota(jnp.int32, (OCCUR, 2 * clips), 0)
                own_ref[pair] = jnp.max(
                    jnp.where(index == local_id, scores[:OCCUR], -jnp.inf), axis=0, keepdims=True
                )

    for pair in range(blocks // 2):
        near_ref[pair] = jnp.max(best_ref[pair], axis=0, keepdims=True)


def near_kernel(
    rows_ref, flip_ref, panel_ref, turned_hbm, near_ref, own_ref, spread_hbm, extra_ref, turned_ref, best_ref, line_ref, done,
    spread_done,
):
    sends = [
        pltpu.make_async_copy(rows_ref.at[0], spread_hbm.at[peer], spread_done.at[peer])
        for peer in range(spread_hbm.shape[0])
    ]
    for send in sends:
        send.start()
    panel_rows = panel_ref.shape[0]
    left = panel_ref[panel_rows - LEFT : panel_rows, :]
    extra = jnp.concatenate([left] * (8 // LEFT), axis=0)
    extra_ref[...] = extra
    copy = pltpu.make_async_copy(turned_ref, turned_hbm, done)
    score_rows(
        rows_ref, flip_ref, panel_ref, turned_ref, near_ref, own_ref, best_ref, line_ref,
        copy.start, lambda step: None, extra
    )
    for send in sends:
        send.wait()
    copy.wait()


def far_kernel(
    rows_ref, flip_ref, stored_ref, extra_ref, turned_hbm, near_ref, own_ref, turned_ref, best_ref, line_ref, done,
    panel_ref, arrival,
):
    copies = []
    for step in range(arrival.shape[0]):
        rows = slice(step * PANEL_ROWS, min(panel_ref.shape[0], (step + 1) * PANEL_ROWS))
        copies.append(pltpu.make_async_copy(stored_ref.at[rows], panel_ref.at[rows], arrival.at[step]))
        copies[-1].start()
    copy = pltpu.make_async_copy(turned_ref, turned_hbm, done)
    score_rows(
        rows_ref, flip_ref, panel_ref, turned_ref, near_ref, own_ref, best_ref, line_ref,
        copy.start, lambda step: copies[step].wait(), extra_ref[...],
    )
    copy.wait()


def scored(kernel, name, rows, flip, panel, limit, spread=None, extra=None):
    blocks, height, clips = rows.shape
    dims, channels = flip.shape
    pairs, width = blocks // 2, 2 * clips
    panel_rows = panel.shape[0]
    here = pl.BlockSpec(memory_space=pltpu.VMEM)
    stored = pl.BlockSpec(memory_space=pltpu.HBM)
    shapes = [
        pltpu.HBM((pairs, dims, width), BF),
        jax.ShapeDtypeStruct((pairs, 1, width), F32),
        jax.ShapeDtypeStruct((pairs, 1, width), F32),
    ]
    scratch = [
        pltpu.VMEM((pairs, dims, width), BF),
        pltpu.VMEM((pairs, 8, width), F32),
        pltpu.VMEM((dims, width), F32),
        pltpu.SemaphoreType.DMA(()),
    ]
    if spread is None:
        even = panel_rows // 8 * 8
        scratch += [
            pltpu.VMEM((even, dims), BF), pltpu.SemaphoreType.DMA((pl.cdiv(even, PANEL_ROWS),))
        ]
    else:
        assert panel_rows % 8 == LEFT
        scratch.append(pltpu.SemaphoreType.DMA((spread,)))
        shapes.append(pltpu.HBM((spread, height, clips), BF))
        shapes.append(jax.ShapeDtypeStruct((8, dims), BF))
    return pl.pallas_call(
        kernel,
        out_shape=shapes,
        in_specs=[here, here] + ([stored, here] if spread is None else [here]),
        out_specs=[stored, here, here] + ([] if spread is None else [stored, here]),
        scratch_shapes=scratch,
        compiler_params=pltpu.CompilerParams(vmem_limit_bytes=limit << 20),
        cost_estimate=pl.CostEstimate(
            flops=2 * blocks * clips * panel_rows * dims, bytes_accessed=2 * panel_rows * dims, transcendentals=0
        ),
        name=name,
    )(rows, flip, panel, *([extra] if spread is None else []))


GROUP = 4


def peer_kernel(
    near_rows_ref, near_turned_ref, near_best_ref, near_own_ref, far_rows_ref, far_turned_hbm, far_best_ref, far_own_ref,
    cols_ref, head_ref, out_ref, far_turned_ref, best_ref, arrival,
):
    far_copy = pltpu.make_async_copy(far_turned_hbm, far_turned_ref, arrival)
    far_copy.start()
    n_dp, height, clips = cols_ref.shape
    n_cent = out_ref.shape[0]
    channels = head_ref.shape[0]
    eye = identity(clips)
    best_ref[...] = jnp.full_like(best_ref, -1.0)
    mine_dp, mine_cent = lax.axis_index("dp"), lax.axis_index("cent")

    def visit(group, first):
        flipped = jnp.concatenate([turn(eye, cols_ref[group * GROUP + at]) for at in range(GROUP)], axis=0)
        projected = jnp.dot(flipped[:, :channels].astype(BF), head_ref[...], preferred_element_type=F32)
        vectors = unit(projected, 1)
        ids = flipped[:, channels : channels + 1] * 256.0 + flipped[:, channels + 1 : channels + 2]
        wide = jnp.broadcast_to(ids, (GROUP * clips, 2 * clips))
        for block in range(n_cent // 2):
            cols = slice(block * 2 * clips, (block + 1) * 2 * clips)
            if first and block == 1:
                far_copy.wait()
            if block == 0:
                turned, row_ids = near_turned_ref[0], label_of(near_rows_ref, 0, channels)
            else:
                turned, row_ids = far_turned_ref[block - 1], label_of(far_rows_ref, block - 1, channels)
            scores = jnp.dot(vectors, turned, preferred_element_type=F32)
            same = wide == row_ids
            if block == 0:
                line = lax.broadcasted_iota(jnp.int32, same.shape, 0)
                lane = lax.broadcasted_iota(jnp.int32, same.shape, 1)
                itself = jnp.where(lane < clips, lane + (mine_dp - group * GROUP) * clips, -1)
                same = same & (line != itself)
            found = jnp.where(same, scores, -1.0)
            best_ref[:, cols] = jnp.maximum(
                best_ref[:, cols], jnp.max(found.reshape(GROUP * clips // 8, 8, 2 * clips), axis=0)
            )

    visit(0, True)

    @pl.loop(1, n_dp // GROUP)
    def _(group):
        visit(group, False)

    best = jnp.max(best_ref[...], axis=0, keepdims=True)
    for block in range(n_cent // 2):
        for side in range(2):
            chip = (mine_cent // 2 + block) % (n_cent // 2)
            cent = 2 * chip + (mine_cent + side) % 2
            at = slice((2 * block + side) * clips, (2 * block + side + 1) * clips)
            part = slice(side * clips, (side + 1) * clips)
            if block == 0:
                nearest, own_best = near_best_ref[0, :, part], near_own_ref[0, :, part]
            else:
                nearest, own_best = far_best_ref[block - 1, :, part], far_own_ref[block - 1, :, part]
            out_ref[cent, 0:1, :] = nearest
            out_ref[cent, 1:2, :] = own_best
            out_ref[cent, 2:3, :] = best[:, at]
            out_ref[cent, 3:4, :] = best[:, at]


def peers_of(near_rows, near_found, far_rows, far_found, cols, head_weight):
    n_dp, height, clips = cols.shape
    n_cent = near_rows.shape[0] + far_rows.shape[0]
    dims = head_weight.shape[1]
    here = pl.BlockSpec(memory_space=pltpu.VMEM)
    stored = pl.BlockSpec(memory_space=pltpu.HBM)
    far_found = [pltpu.with_memory_space_constraint(far_found[0], pltpu.HBM), *far_found[1:]]
    return pl.pallas_call(
        peer_kernel,
        out_shape=jax.ShapeDtypeStruct((n_cent, 4, clips), F32),
        in_specs=[here] * 5 + [stored] + [here] * 4,
        out_specs=here,
        scratch_shapes=[
            pltpu.VMEM(far_found[0].shape, BF),
            pltpu.VMEM((8, n_cent * clips), F32),
            pltpu.SemaphoreType.DMA(()),
        ],
        compiler_params=pltpu.CompilerParams(vmem_limit_bytes=16 << 20),
        cost_estimate=pl.CostEstimate(
            flops=2 * n_dp * n_cent * clips * clips * dims, bytes_accessed=4 << 20, transcendentals=0
        ),
        name="peers",
    )(near_rows, *near_found, far_rows, *far_found, cols, head_weight)


def local(
    clip_data,
    frame_counts,
    send_list,
    cluster_ids,
    expand_weight,
    depth_kernel,
    reduce_weight,
    head_weight,
    centroids,
):
    n_dp = lax.axis_size("dp")
    n_cent = lax.axis_size("cent")
    pooled, panel, head, flip = embed(
        clip_data, frame_counts, send_list, expand_weight, depth_kernel, reduce_weight, head_weight, centroids, n_dp
    )
    arrived = lax.all_to_all(pooled, "dp", split_axis=0, concat_axis=0, tiled=True)
    payload, rows = own(arrived, cluster_ids, head_weight.shape[0])
    partner = lax.ppermute(payload, "cent", [(at, at ^ 1) for at in range(n_cent)])
    near_rows = jnp.stack([payload, partner])
    far_rows = jnp.concatenate(
        [
            lax.ppermute(near_rows, "cent", [((at + 2 * chip) % n_cent, at) for at in range(n_cent)])
            for chip in range(1, n_cent // 2)
        ]
    )
    *near_found, spread, extra = scored(near_kernel, "near", near_rows, flip, panel, 16, n_dp)
    cols = lax.all_to_all(spread, "dp", split_axis=0, concat_axis=0, tiled=True)
    vectors = vectors_of(rows, head)
    far_found = scored(
        far_kernel, "far", far_rows, flip, pltpu.with_memory_space_constraint(centroids, pltpu.HBM), 32, extra=extra
    )
    partial = peers_of(near_rows, near_found, far_rows, far_found, cols, head)
    parts = lax.all_to_all(partial, "cent", split_axis=0, concat_axis=0, tiled=True)
    final = jnp.max(parts, axis=0)
    return (vectors, final[0], final[1], final[2])


def solution(mesh):
    placed = (
        P(("dp", "cent"), None, None, None),
        P(("dp", "cent"), None),
        P(("dp", "cent"), None),
        P(("dp", "cent"), None),
        P(),
        P(),
        P(),
        P(),
        P("cent", None),
    )
    return jax.shard_map(
        local,
        mesh=mesh,
        in_specs=placed,
        out_specs=(
            P(("dp", "cent"), None),
            P(("dp", "cent")),
            P(("dp", "cent")),
            P(("dp", "cent")),
        ),
        check_vma=False,
    )
```
